32 devices in a mesh: seq: 4 (over y, core), fsdp: 8 (over z, x).
Axes of the slice: x: 2, y: 2, z: 4, core: 2. Of those that a mesh axis runs over, the one named last changes fastest.
Arguments:
- layer_input: bfloat16 [24, 1024, 768], P('fsdp', 'seq'), may hold values from -6 to 6
- doc_starts: int32 [24, 7], P('fsdp'), may hold values from 1 to 1023, as said below
- mem_rows: int32 [24, 20], P('fsdp'), may hold values from 0 to 1023, as said below
- w_query: bfloat16 [768, 768], P('fsdp'), may hold values from -0.21875 to 0.21875
- b_query: bfloat16 [768], P('fsdp'), may hold values from -2 to 2
- w_key: bfloat16 [768, 768], P('fsdp'), may hold values from -0.21875 to 0.21875
- w_value: bfloat16 [768, 768], P('fsdp'), may hold values from -0.21875 to 0.21875
- b_value: bfloat16 [768], P('fsdp'), may hold values from -0.29882812 to 0.29882812
- w_out: bfloat16 [768, 768], P('fsdp'), may hold values from -2.5 to 2.5
- b_out: bfloat16 [768], P('fsdp'), may hold values from -2 to 2
- attn_gain: bfloat16 [768], P('fsdp'), may hold values from 0.5 to 1.5
- attn_shift: bfloat16 [768], P('fsdp'), may hold values from -2 to 2
- w_up: bfloat16 [768, 3072], P('fsdp'), may hold values from -0.21875 to 0.21875
- b_up: bfloat16 [3072], P('fsdp'), may hold values from -2 to 2
- w_down: bfloat16 [3072, 768], P('fsdp'), may hold values from -0.109375 to 0.109375
- b_down: bfloat16 [768], P('fsdp'), may hold values from -2 to 2
- ffn_gain: bfloat16 [768], P('fsdp'), may hold values from 0.5 to 1.5
- ffn_shift: bfloat16 [768], P('fsdp'), may hold values from -2 to 2
- grad_out: bfloat16 [24, 1024, 768], P('fsdp', 'seq'), may hold values from -6 to 6
Outputs:
- layer_out: bfloat16 [24, 1024, 768], P('fsdp', 'seq')
- grad_input: float32 [24, 1024, 768], P('fsdp', 'seq')
- grad_w_query: float32 [768, 768], P('fsdp')
- grad_b_query: float32 [768], P('fsdp')
- grad_w_key: float32 [768, 768], P('fsdp')
- grad_w_value: float32 [768, 768], P('fsdp')
- grad_b_value: float32 [768], P('fsdp')
- grad_w_out: float32 [768, 768], P('fsdp')
- grad_b_out: float32 [768], P('fsdp')
- grad_attn_gain: float32 [768], P('fsdp')
- grad_attn_shift: float32 [768], P('fsdp')
- grad_w_up: float32 [768, 3072], P('fsdp')
- grad_b_up: float32 [3072], P('fsdp')
- grad_w_down: float32 [3072, 768], P('fsdp')
- grad_b_down: float32 [768], P('fsdp')
- grad_ffn_gain: float32 [768], P('fsdp')
- grad_ffn_shift: float32 [768], P('fsdp')
The draws below stay inside these ranges and needn't reach their ends.
Inputs may be any that keep to these rules, and one draw needn't show every extreme that they name: `doc_starts`: in each segment the 7 starts are distinct and rising, the first is 1 and the last is 1023; a document runs from 0 or a start to the position before the next start. `mem_rows`: in each segment the 20 memory positions are distinct and rising, the first is 0 and the last is 1023.
All inputs are finite; a program needn't handle non-finite values.
Results may differ from the reference program's by a relative error of at most 0.017.
Values may be sent and summed in bfloat16 or wider, within the bound.
No kernel may reach another device: no remote copies, remote signals or barrier semaphores. Data moves between devices by JAX's collectives and lax.ppermute only.
A program may use at most 128 MiB of HBM per device.

```python
import math
import jax
import jax.numpy as jnp
from jax import lax

D = 768
H = 12
HD = 64
FF = 3072
SEG_LEN = 1024
MEM = 20
NDOC = 7
SEGS = 24


def distinct_positions(base_key, count, low_end, span):
    scores = jax.random.randint(base_key, (SEGS, span), 0, 32768, dtype=jnp.int32) * span
    places = jnp.arange(span, dtype=jnp.int32)
    scores = scores + places[None, :]
    ends = (places == 0) | (places == span - 1)
    scores = jnp.where(ends[None, :], 32768 * span + places[None, :], scores)
    unused, picked = lax.top_k(scores, count)
    return (jnp.sort(picked, axis=-1) + low_end).astype(jnp.int32)


def draw_doc_starts(key, part):
    return distinct_positions(jax.random.fold_in(key, 11), NDOC, 1, SEG_LEN - 1)


def draw_mem_rows(key, part):
    return distinct_positions(jax.random.fold_in(key, 23), MEM, 0, SEG_LEN)


def levels(key, dims, shards, low, top_value):
    gain = 1.0
    for position, parts in shards:
        heights = jax.random.uniform(jax.random.fold_in(jax.random.fold_in(key, 6), position), (parts,), jnp.float32, low / len(shards), top_value / len(shards))
        gain = gain * jnp.repeat(jnp.exp(heights), dims[position] // parts).reshape((-1,) + (1,) * (len(dims) - 1 - position))
    return gain


def normal_values(own_key, shape, deviation, most, cuts=(), held_as=jnp.bfloat16):
    entries = deviation * jax.random.normal(own_key, shape, jnp.float32)
    if cuts:
        entries = entries * levels(own_key, shape, cuts, -0.22, 0.18)
    return jnp.clip(entries, -most, most).astype(held_as)


def setup_inputs(seed: int = 0) -> dict:
    streams_of = jax.random.split(jax.random.key(seed), 20)
    return {
        "layer_input": normal_values(streams_of[0], (SEGS, SEG_LEN, D), 1.0, 6.0, ((0, 8), (1, 4))),
        "doc_starts": draw_doc_starts(jax.random.fold_in(streams_of[19], 71), 0),
        "mem_rows": draw_mem_rows(jax.random.fold_in(streams_of[19], 71), 0),
        "w_query": normal_values(streams_of[3], (D, D), D ** -0.5, 0.21875, ((0, 8),)),
        "b_query": normal_values(streams_of[4], (D,), 0.3, 2.0, ((0, 8),)),
        "w_key": normal_values(streams_of[5], (D, D), D ** -0.5, 0.21875, ((0, 8),)),
        "w_value": normal_values(streams_of[6], (D, D), D ** -0.5, 0.21875, ((0, 8),)),
        "b_value": normal_values(streams_of[7], (D,), 0.05, 0.29882812, ((0, 8),)),
        "w_out": normal_values(streams_of[8], (D, D), (max(D // 128, 1)) ** -0.5, 2.5, ((0, 8),)),
        "b_out": normal_values(streams_of[9], (D,), 0.3, 2.0, ((0, 8),)),
        "attn_gain": jnp.clip(1.0 + 0.1 * jax.random.normal(streams_of[10], (D,), jnp.float32), 0.5, 1.5).astype(jnp.bfloat16),
        "attn_shift": normal_values(streams_of[11], (D,), 0.3, 2.0, ((0, 8),)),
        "w_up": normal_values(streams_of[12], (D, FF), D ** -0.5, 0.21875, ((0, 8),)),
        "b_up": normal_values(streams_of[13], (FF,), 0.3, 2.0, ((0, 8),)),
        "w_down": normal_values(streams_of[14], (FF, D), FF ** -0.5, 0.109375, ((0, 8),)),
        "b_down": normal_values(streams_of[15], (D,), 0.3, 2.0, ((0, 8),)),
        "ffn_gain": jnp.clip(1.0 + 0.1 * jax.random.normal(streams_of[16], (D,), jnp.float32), 0.5, 1.5).astype(jnp.bfloat16),
        "ffn_shift": normal_values(streams_of[17], (D,), 0.3, 2.0, ((0, 8),)),
        "grad_out": normal_values(streams_of[18], (SEGS, SEG_LEN, D), 1.0, 6.0, ((0, 8), (1, 4))),
    }


@jax.custom_vjp
def low(v):
    return lax.optimization_barrier(v.astype(jnp.bfloat16)).astype(jnp.float32)

@jax.custom_vjp
def low_back(v):
    return v

def low_keep(v):
    return (low(v), None)

def low_pass(kept, grad):
    return (grad,)

def back_keep(v):
    return (v, None)

def back_low(kept, grad):
    return (low(grad),)
low.defvjp(low_keep, low_pass)
low_back.defvjp(back_keep, back_low)
LN_EPS = 1e-12
MASKED = -1e+30
HIGHEST = lax.Precision.HIGHEST

def matmul(left, right):
    return jnp.dot(left, right, precision=HIGHEST)

def layer_norm(values, gain_vec, shift_vec):
    centre = values - lax.optimization_barrier(jnp.mean(values, axis=-1, keepdims=True))
    inv_dev = lax.rsqrt(lax.optimization_barrier(jnp.mean(centre * centre, axis=-1, keepdims=True)) + LN_EPS)
    return centre * inv_dev * gain_vec + shift_vec

def segment_forward(params, seg_rows, starts, memory):
    w_query, b_query, w_key, w_value, b_value, w_out, b_out, attn_gain, attn_shift, w_up, b_up, w_down, b_down, ffn_gain, ffn_shift = params
    positions = jnp.arange(SEG_LEN, dtype=jnp.int32)
    doc_ids = lax.optimization_barrier(jnp.sum((starts[:, None] <= positions[None, :]).astype(jnp.int32), axis=0))
    is_memory = jnp.any(memory[:, None] == positions[None, :], axis=0)
    visible = (doc_ids[:, None] == doc_ids[None, :]) | is_memory[:, None] | is_memory[None, :]
    factor = 1.0 / math.sqrt(HD)
    queries = low_back(low(matmul(seg_rows, w_query) + b_query)).reshape(SEG_LEN, H, HD)
    key_rows = low_back(low(matmul(seg_rows, w_key))).reshape(SEG_LEN, H, HD)
    value_rows = low_back(low(matmul(seg_rows, w_value) + b_value)).reshape(SEG_LEN, H, HD)
    scores = low_back(jnp.einsum('qhd,khd->hqk', queries, key_rows, precision=HIGHEST) * factor)
    scores = jnp.where(visible[None], scores, MASKED)
    row_max = lax.optimization_barrier(jnp.max(scores, axis=-1, keepdims=True))
    shifted = jnp.exp(scores - row_max)
    attn_probs = shifted / lax.optimization_barrier(jnp.sum(shifted, axis=-1, keepdims=True))
    context = jnp.einsum('hqk,khd->qhd', low(attn_probs), value_rows, precision=HIGHEST)
    context = low_back(low(context.reshape(SEG_LEN, H * HD)))
    attn_out = low_back(matmul(context, w_out) + b_out)
    normed_one = layer_norm(seg_rows + attn_out, attn_gain, attn_shift)
    hidden = low_back(matmul(low(normed_one), w_up) + b_up)
    active = low(jax.nn.gelu(hidden, approximate=False))
    branch = low_back(matmul(active, w_down) + b_down)
    return layer_norm(normed_one + branch, ffn_gain, ffn_shift)

def reference(layer_input, doc_starts, mem_rows, w_query, b_query, w_key, w_value, b_value, w_out, b_out, attn_gain, attn_shift, w_up, b_up, w_down, b_down, ffn_gain, ffn_shift, grad_out):
    params = tuple((tensor.astype(jnp.float32) for tensor in (w_query, b_query, w_key, w_value, b_value, w_out, b_out, attn_gain, attn_shift, w_up, b_up, w_down, b_down, ffn_gain, ffn_shift)))

    def whole_layer(weights, inputs):

        def advance(carried, pieces):
            seg_rows, starts, memory = pieces
            return (carried, jax.checkpoint(segment_forward)(weights, seg_rows, starts, memory))
        unused, outputs = lax.scan(advance, jnp.zeros((), jnp.float32), (inputs, doc_starts, mem_rows))
        return outputs
    outputs, pullback = jax.vjp(whole_layer, params, layer_input.astype(jnp.float32))
    weight_grads, grad_input = pullback(grad_out.astype(jnp.float32))
    return (outputs.astype(jnp.bfloat16), grad_input, weight_grads[0], weight_grads[1], weight_grads[2], weight_grads[3], weight_grads[4], weight_grads[5], weight_grads[6], weight_grads[7], weight_grads[8], weight_grads[9], weight_grads[10], weight_grads[11], weight_grads[12], weight_grads[13], weight_grads[14])
```

```python
import math

import jax
import jax.numpy as jnp
from jax import lax
from jax.experimental import pallas as pl
from jax.experimental.pallas import tpu as pltpu
from jax.sharding import PartitionSpec as P


HD = 64
LN_EPS = 1e-12
MASKED = -1e30
BF = jnp.bfloat16
F32 = jnp.float32


CORE, CHIP = 1, 2


SEQ, FSDP = "seq", "fsdp"


def hop(values, axis, bit):
    size = lax.axis_size(axis)
    return lax.ppermute(values, axis, [(i, i ^ bit) for i in range(size)])


def bit_of(index, bit):
    return (index & bit) != 0


def joined(mine, other, upper, axis):
    low = jnp.where(upper, other, mine)
    high = jnp.where(upper, mine, other)
    return jnp.concatenate([low, high], axis=axis)


def fsdp_digits():
    bits = lax.axis_size(FSDP).bit_length() - 1
    digits, at = [], 0
    while at < bits:
        take = 1 if at == 0 else min(2, bits - at)
        digits.append((at, 1 << take))
        at += take
    return digits


def gather_pieces(block):
    pieces = {0: block}
    for shift, size in reversed(fsdp_digits()):
        for held in list(pieces):
            for step in range(1, size):
                entry = held | step << shift
                pieces[entry] = hop(pieces[held], FSDP, step << shift)
    return [pieces[j] for j in range(len(pieces))]


def entry_at(values, indices):
    for index in indices:
        values = lax.dynamic_index_in_dim(values, index, 0, keepdims=False)
    return values


def halve(held, steps, extra=None):
    arrived, kept = [], []

    def total(index):
        values = entry_at(held, [k for k in kept] + [index] if index is not None else kept).astype(F32)
        if extra is not None:
            rows = jnp.broadcast_to(extra, values.shape[:-2] + extra.shape)
            values = jnp.concatenate([values, rows], axis=-2)
        for at, group in arrived:
            path = kept[at:] + ([index] if index is not None else [])
            for got in group:
                values = values + entry_at(got, path).astype(F32)
        return values

    for axis, shift, size, place in steps:
        digit = (place >> shift) & (size - 1)
        group = [hop(total(digit ^ step).astype(BF), axis, step << shift) for step in range(1, size)]
        kept.append(digit)
        arrived.append((len(kept), group))
    return total(None)


def mm(left, right):
    return lax.dot_general(left, right, (((1,), (0,)), ((), ())), preferred_element_type=F32)


def mm_nt(left, right):
    return lax.dot_general(left, right, (((1,), (1,)), ((), ())), preferred_element_type=F32)


def mm_tn(left, right):
    return lax.dot_general(left, right, (((0,), (0,)), ((), ())), preferred_element_type=F32)


def hidden_pairs(query_code, bias_ref):
    length = bias_ref.shape[0]
    key_code = query_code.T
    step = 128
    for start in range(0, length, step):
        part = key_code[start : start + step, :]
        same = part[:, 0:1] == query_code[0:1, :]
        bias_ref[start : start + step, :] = jnp.where(
            same, 0.0, jnp.maximum(part[:, 1:2], query_code[1:2, :])
        )


def erf_parts(values):
    cdf = 0.5 * (1.0 + lax.erf(values * (1.0 / math.sqrt(2.0))))
    return cdf, jnp.exp(-0.5 * values * values) * (1.0 / math.sqrt(2.0 * math.pi))


def place_rows(pieces, order_ref, rows, target):
    for j, piece in enumerate(pieces):
        at = pl.multiple_of(order_ref[j] * rows, rows)
        target[pl.ds(at, rows), :] = piece[0:rows, :]


def attend_kernel(heads, shard, count, order_ref, x0, x1, x2, x3, *refs):
    pieces, refs = refs[:count], refs[count:]
    b_ref, qc_ref, qkv_o, xrel_o, w_o, near_o, core_o, chip_o, log_o, vec_o = refs[:10]
    bias_ref, q_ref, k_ref, vt_ref, ctx_ref = refs[10:]
    width = heads * HD
    rows = x0.shape[1]
    length = 4 * rows
    place_rows(pieces, order_ref, shard, w_o)
    added = b_ref[...]
    if count > 1:
        for j, piece in enumerate(pieces):
            vec_o[order_ref[j]] = piece[shard:, 0:128].astype(F32)
        here = order_ref[count]
        near, far = vec_o[2 * here], vec_o[2 * here + 1]
        added = jnp.concatenate(
            [near[0:1, 0:shard], far[0:1, 0:shard], jnp.zeros((1, width), F32), near[1:2, 0:shard], far[1:2, 0:shard]],
            axis=1,
        )
    for j, piece in enumerate((x0, x1, x2, x3)):
        block = piece[0]
        xrel_o[j * rows : (j + 1) * rows, :] = block
        made = (mm(block, w_o[...]) + added).astype(BF)
        qkv_o[j * rows : (j + 1) * rows, :] = made
        for h in range(heads):
            at = h * HD
            q_ref[h, j * rows : (j + 1) * rows, :] = made[:, at : at + HD] * BF(1.0 / math.sqrt(HD))
            k_ref[h, j * rows : (j + 1) * rows, :] = made[:, width + at : width + at + HD]
            vt_ref[h, :, j * rows : (j + 1) * rows] = made[:, 2 * width + at : 2 * width + at + HD].T
    hidden_pairs(qc_ref[0], bias_ref)

    def block_of(step, carry):
        at = pl.ds(pl.multiple_of(step * 256, 256), 256)
        for h in range(heads):
            scores = mm_nt(k_ref[h], q_ref[h, at, :]) + bias_ref[:, at]
            top = jnp.max(scores, axis=0, keepdims=True)
            shifted = jnp.exp(scores - top)
            total = jnp.sum(shifted, axis=0, keepdims=True)
            made = mm(vt_ref[h], shifted.astype(BF)) / total
            ctx_ref[h * HD : (h + 1) * HD, at] = made
            log_o[h : h + 1, at] = top + jnp.log(total)
        return carry

    lax.fori_loop(0, length // 256, block_of, 0)
    near_o[...] = ctx_ref[:, 0:rows].T.astype(BF)
    core_o[...] = ctx_ref[:, rows : 2 * rows].T.astype(BF)
    chip_o[...] = ctx_ref[:, 2 * rows : 4 * rows].T.astype(BF)


def attend(seg, order, pieces, weights, shard, bias, query_code):
    (first, _), width = pieces[0], bias.shape[1] // 3
    rows, depth = first.shape[1:]
    length, heads = 4 * rows, width // HD
    shape = jax.ShapeDtypeStruct
    vmem = pl.BlockSpec(memory_space=pltpu.VMEM)

    def rows_of(at):
        return pl.BlockSpec((1, rows, depth), lambda g, at=at: (at, 0, 0))

    count = len(weights)
    whole = lambda a: pl.BlockSpec(a.shape, lambda g, n=len(a.shape): (0,) * n)
    outs = (
        shape((length, 3 * width), BF),
        shape((length, depth), BF),
        shape((depth, 3 * width), BF),
        shape((rows, width), BF),
        shape((rows, width), BF),
        shape((2 * rows, width), BF),
        shape((8, length), F32),
        shape((count, max(weights[0].shape[0] - shard, 8), 128), F32),
    )
    return pl.pallas_call(
        lambda *refs: attend_kernel(heads, shard, count, *refs),
        grid=(1,),
        out_shape=outs,
        in_specs=[pl.BlockSpec(memory_space=pltpu.SMEM)]
        + [rows_of(at) for _, at in pieces]
        + [whole(w) for w in weights]
        + [whole(bias), pl.BlockSpec((1,) + query_code.shape[1:], lambda g: (seg, 0, 0))],
        out_specs=[whole(o) for o in outs],
        scratch_shapes=[
            pltpu.VMEM((length, length), F32),
            pltpu.VMEM((heads, length, HD), BF),
            pltpu.VMEM((heads, length, HD), BF),
            pltpu.VMEM((heads, HD, length), BF),
            pltpu.VMEM((width, length), F32),
        ],
        cost_estimate=pl.CostEstimate(
            flops=2 * length * depth * 3 * width + 16 * length * length * width,
            bytes_accessed=12 << 20,
            transcendentals=heads * length * length,
        ),
        name="attend",
    )(order, *[p for p, _ in pieces], *weights, bias, query_code)


def pack_kernel(place_ref, wq, wk, wv, wo, wu, wd, *refs):
    vectors, (own_o, up_o, rest_o) = refs[:-3], refs[-3:]
    here, core, chip = place_ref[0], place_ref[1], place_ref[2]
    shard, depth = wq.shape
    width, half, rows = depth // 4, depth // 2, shard // 2
    for i, ref in enumerate((wq, wk, wv)):
        picked = ref[:, 0:width]
        for j in range(1, 4):
            picked = jnp.where(here == j, ref[:, j * width : (j + 1) * width], picked)
        own_o[0:shard, i * width : (i + 1) * width] = picked
    below = [ref[0:1, at : at + shard] for ref in vectors for at in range(0, ref.shape[1], shard)]
    below.append(jnp.zeros((own_o.shape[0] - shard - len(below), shard), BF))
    own_o[shard:, :] = jnp.zeros((own_o.shape[0] - shard, 3 * width), BF)
    own_o[shard:, 0:shard] = jnp.concatenate([b.astype(F32) for b in below], axis=0).astype(BF)
    ff_half = wu.shape[1] // 2
    up_o[...] = wu[:, pl.ds(pl.multiple_of(core * ff_half, ff_half), ff_half)]
    columns = pl.ds(pl.multiple_of(core * half, half), half)
    at = pl.multiple_of(chip * rows, rows)
    rest_o[:, 0:half] = wo[pl.ds(at, rows), columns]
    for i in range(wd.shape[0] // shard):
        rest_o[:, (i + 1) * half : (i + 2) * half] = wd[pl.ds(i * shard + at, rows), columns]


def pack(place, weights, vectors):
    shard, depth = weights[0].shape
    ff, ratio = weights[4].shape[1], weights[5].shape[0] // shard
    shape = jax.ShapeDtypeStruct
    vmem = pl.BlockSpec(memory_space=pltpu.VMEM)
    return pl.pallas_call(
        pack_kernel,
        out_shape=(
            shape((shard + 16, 3 * depth // 4), BF),
            shape((shard, ff // 2), BF),
            shape((shard // 2, (1 + ratio) * depth // 2), BF),
        ),
        in_specs=[pl.BlockSpec(memory_space=pltpu.SMEM)] + [vmem] * (6 + len(vectors)),
        out_specs=[vmem] * 3,
        cost_estimate=pl.CostEstimate(flops=1 << 16, bytes_accessed=4 << 20, transcendentals=0),
        name="pack",
    )(place, *weights, *[v[None, :] for v in vectors])


def norm_stats(values):
    centre = values - jnp.mean(values, axis=-1, keepdims=True)
    inv_dev = lax.rsqrt(jnp.mean(centre * centre, axis=-1, keepdims=True) + LN_EPS)
    return centre * inv_dev, inv_dev


def norm_back(grads, unit, inv_dev, gain):
    scaled = grads * gain
    return inv_dev * (
        scaled
        - jnp.mean(scaled, axis=-1, keepdims=True)
        - unit * jnp.mean(scaled * unit, axis=-1, keepdims=True)
    )


def swapped(parts, upper_core, upper_chip):
    a, b, c, d = parts
    a, b, c, d = (jnp.where(upper_core, y, x) for x, y in ((a, b), (b, a), (c, d), (d, c)))
    return [jnp.where(upper_chip, y, x) for x, y in ((a, c), (b, d), (c, a), (d, b))]


def middle_kernel(segs, shard_rows, direct, order_ref, *refs):
    weights_in, refs = (refs[:12], refs[12:]) if direct else (refs[:3], refs[3:])
    context_in, refs = refs[: 4 * segs], refs[4 * segs :]
    x_ref, go_ref, vec_ref, up_ref = refs[:4]
    (
        out_o, ctx_o, low_o, act_o, gb_o, gh_o, ga_o, gsum_o, g0_o, g1_o, g2_o, g3_o, vec_o,
    ) = refs[4:17]
    wo, wu, wd, slope_ref, half_ref, vec_s, up_s, sums_o, up_sums_o, sems = refs[17:]
    seg = pl.program_id(0)
    depth, ff = wu.shape
    rows, half, ff_half = x_ref.shape[0], depth // 2, ff // 2
    _, core, chip = (order_ref[order_ref.shape[0] - 3 + i] for i in range(3))
    upper_core, upper_chip = core != 0, chip != 0

    def copies():
        if not direct:
            return [[(a, b)] for a, b in zip(weights_in, (wo, wu, wd))]
        found = [[], [], []]
        near, shard = weights_in[0].shape[:2]
        part, ratio = shard // 2, ff // depth
        for side in range(2):
            column = pl.multiple_of((core ^ side) * half, half)
            for low in range(2):
                for j in range(near):
                    block = order_ref[2 * j + low]
                    at = pl.multiple_of(block * shard, shard)
                    found[1].append(
                        (weights_in[2 * side + low].at[j],
                         wu.at[pl.ds(at, shard), pl.ds(side * ff_half, ff_half)])
                    )
                    for other in range(2):
                        piece = weights_in[4 + 4 * side + 2 * other + low]
                        inner = (chip ^ other) * part
                        found[0].append(
                            (piece.at[j, :, 0:half],
                             wo.at[pl.ds(pl.multiple_of(at + inner, part), part), pl.ds(column, half)])
                        )
                        for i in range(ratio):
                            row = (block * ratio + i) * shard
                            turned = jnp.where(row < ff_half, row + core * ff_half, row - core * ff_half)
                            turned = pl.multiple_of(turned + inner, part)
                            found[2].append(
                                (piece.at[j, :, (i + 1) * half : (i + 2) * half],
                                 wd.at[pl.ds(turned, part), pl.ds(column, half)])
                            )
        return found

    groups, used = [], 0
    for found in copies():
        groups.append([pltpu.make_async_copy(a, b, sems.at[used + i]) for i, (a, b) in enumerate(found)])
        used += len(found)

    @pl.when(seg == 0)
    def _():
        for group in groups:
            for one in group:
                one.start()
        if direct:
            count, shard = vec_ref.shape[0], weights_in[0].shape[1]
            for i in range(6):
                vec_s[i : i + 1, :] = jnp.concatenate(
                    [vec_ref[j, i + 2 : i + 3, 0:shard] for j in range(count)], axis=1
                )
            halves = [
                jnp.concatenate(
                    [
                        vec_ref[j, 8 + r : 9 + r, 0:shard]
                        for j in range(side * count // 2, (side + 1) * count // 2)
                        for r in range(ff // depth)
                    ],
                    axis=1,
                )
                for side in range(2)
            ]
            up_s[:, 0:ff_half] = jnp.where(upper_core, halves[1], halves[0])
            up_s[:, ff_half:] = jnp.where(upper_core, halves[0], halves[1])
        else:
            vec_s[...] = vec_ref[...]
            up_s[...] = up_ref[...]
        sums_o[...] = jnp.zeros_like(sums_o)
        up_sums_o[...] = jnp.zeros_like(up_sums_o)

    def ready(which):
        @pl.when(seg == 0)
        def _():
            for one in groups[which]:
                one.wait()

    def vector(i):
        return vec_s[i : i + 1, :]

    ready(0)
    parts = []
    for j in range(4):
        picked = context_in[j][...]
        for i in range(1, segs):
            picked = jnp.where(seg == i, context_in[4 * i + j][...], picked)
        parts.append(picked)
    context = jnp.concatenate(swapped(parts, upper_core, upper_chip), axis=1)
    ctx_o[...] = context.T
    summed = x_ref[...].astype(F32) + mm(context, wo[...]) + vector(0)
    unit_one, inv_one = norm_stats(summed)
    normed_one = unit_one * vector(1) + vector(2)
    low = normed_one.astype(BF)
    low_o[...] = low.T
    ready(1)
    ready(2)
    step = depth if ff_half % depth == 0 else ff_half
    branch = jnp.zeros((rows, depth), F32)
    for start in range(0, ff, step):
        part = slice(start, start + step)
        hidden = mm(low, wu[:, part]) + up_s[:, part]
        cdf, density = erf_parts(hidden)
        active = (hidden * cdf).astype(BF)
        slope_ref[:, part] = cdf + hidden * density
        side = 0 if start < ff_half else 1
        target = pl.multiple_of((core ^ side) * ff_half, ff_half) + (start - side * ff_half)
        act_o[pl.ds(pl.multiple_of(target, 128), step), :] = active.T
        branch = branch + mm(active, wd[part, :])
    unit_two, inv_two = norm_stats(normed_one + (branch + vector(3)))
    out_o[...] = (unit_two * vector(4) + vector(5)).astype(BF)

    def add_sum(i, values):
        sums_o[i : i + 1, :] += jnp.sum(values, axis=0, keepdims=True)

    def halves(values, out):
        half_ref[...] = values
        out[:, 0:half] = half_ref[:, pl.ds(pl.multiple_of(core * half, half), half)].astype(BF)
        out[:, half:] = half_ref[:, pl.ds(pl.multiple_of((1 - core) * half, half), half)].astype(BF)

    grads = go_ref[...].astype(F32)
    add_sum(4, grads * unit_two)
    add_sum(5, grads)
    grad_two = norm_back(grads, unit_two, inv_two, vector(4))
    grad_branch = grad_two.astype(BF)
    add_sum(3, grad_branch.astype(F32))
    halves(grad_branch.astype(F32), gb_o)
    grad_normed = grad_two
    for start in range(0, ff, step):
        part = slice(start, start + step)
        grad_hidden = (mm_nt(grad_branch, wd[part, :]) * slope_ref[:, part]).astype(BF)
        side, first = start // ff_half, start % ff_half
        for at in range(0, step, half):
            target = 2 * (first + at) + side * half
            gh_o[:, target : target + half] = grad_hidden[:, at : at + half]
        up_sums_o[:, part] += jnp.sum(grad_hidden.astype(F32), axis=0, keepdims=True)
        grad_normed = grad_normed + mm_nt(grad_hidden, wu[:, part])
    add_sum(1, grad_normed * unit_one)
    add_sum(2, grad_normed)
    grad_one = norm_back(grad_normed, unit_one, inv_one, vector(1))
    gsum_o[...] = grad_one
    grad_attn = grad_one.astype(BF)
    add_sum(0, grad_attn.astype(F32))
    halves(grad_attn.astype(F32), ga_o)
    grad_context = mm_nt(grad_attn, wo[...]).astype(BF)
    width = depth // 4
    turned = swapped([grad_context[:, j * width : (j + 1) * width] for j in range(4)], upper_core, upper_chip)
    g0_o[...] = turned[0]
    g1_o[...] = turned[1]
    g2_o[...] = turned[2]
    g3_o[...] = turned[3]

    @pl.when(seg == segs - 1)
    def _():
        low_half, high_half = up_sums_o[:, 0:ff_half], up_sums_o[:, ff_half:]
        ordered = jnp.concatenate(
            [jnp.where(upper_core, high_half, low_half), jnp.where(upper_core, low_half, high_half)], axis=1
        )
        vec_o[...] = jnp.zeros_like(vec_o)
        ratio, per = ff // depth, half // shard_rows
        for f in range(depth // shard_rows):
            own = slice(f * shard_rows, (f + 1) * shard_rows)
            parts = [sums_o[i : i + 1, own] for i in range(6)] + [
                ordered[:, (f * ratio + r) * shard_rows : (f * ratio + r + 1) * shard_rows] for r in range(ratio)
            ]
            for row in range(0, len(parts), per):
                line = jnp.concatenate(parts[row : row + per], axis=1)
                vec_o[2 * f, row // per : row // per + 1, 0 : line.shape[1]] = line


def middle(order, weights, shard, direct, contexts, rows_in, grad_out, vectors, up_bias):
    tokens, depth = rows_in.shape
    ff, segs = up_bias.shape[1], len(contexts)
    rows, width, half = tokens // segs, depth // 4, depth // 2
    shape = jax.ShapeDtypeStruct
    fixed = lambda a: pl.BlockSpec(a.shape, lambda g, n=len(a.shape): (0,) * n)
    moving = lambda columns: pl.BlockSpec((rows, columns), lambda g: (g, 0))
    turned = lambda units: pl.BlockSpec((units, rows), lambda g: (0, g))
    outs = [
        (shape((tokens, depth), BF), moving(depth)),
        (shape((depth, tokens), BF), turned(depth)),
        (shape((depth, tokens), BF), turned(depth)),
        (shape((ff, tokens), BF), turned(ff)),
    ]
    for columns, kind in [(depth, BF), (ff, BF), (depth, BF), (depth, F32), (width, BF), (width, BF),
                          (width, BF), (width, BF)]:
        outs.append((shape((tokens, columns), kind), moving(columns)))
    last = shape((2 * depth // shard, 8, half), F32)
    outs.append((last, fixed(last)))
    piece = pl.BlockSpec((rows, width), lambda g: (0, 0))
    flat = [one for four in contexts for one in four]
    if direct:
        copies = 2 * (2 * weights[0].shape[0]) * (1 + 2 * (1 + ff // depth))
    else:
        copies = 3
    return pl.pallas_call(
        lambda *refs: middle_kernel(segs, shard, direct, *refs),
        grid=(segs,),
        out_shape=tuple(o for o, _ in outs),
        in_specs=[pl.BlockSpec(memory_space=pltpu.SMEM)]
        + [pl.BlockSpec(memory_space=pl.ANY)] * len(weights)
        + [piece] * len(flat)
        + [moving(depth), moving(depth), fixed(vectors), fixed(up_bias)],
        out_specs=[b for _, b in outs],
        scratch_shapes=[
            pltpu.VMEM((depth, depth), BF),
            pltpu.VMEM((depth, ff), BF),
            pltpu.VMEM((ff, depth), BF),
            pltpu.VMEM((rows, ff), F32),
            pltpu.VMEM((rows, depth), F32),
            pltpu.VMEM((8, depth), F32),
            pltpu.VMEM((1, ff), F32),
            pltpu.VMEM((8, depth), F32),
            pltpu.VMEM((1, ff), F32),
            pltpu.SemaphoreType.DMA((copies,)),
        ],
        cost_estimate=pl.CostEstimate(
            flops=4 * tokens * depth * (depth + 2 * ff), bytes_accessed=40 << 20,
            transcendentals=2 * tokens * ff,
        ),
        name="middle",
    )(order, *weights, *flat, rows_in, grad_out, vectors, up_bias)


def first_grads(context_t, low_t, ga, gh):
    depth, tokens = low_t.shape
    half, ratio = depth // 2, gh.shape[1] // depth
    shape = jax.ShapeDtypeStruct

    def kernel(ctx_ref, low_ref, ga_ref, gh_ref, keep_o, send_o):
        step = pl.program_id(0)

        def put(left, right):
            made = mm(left, right)
            keep_o[0] = made[:, 0:half].astype(BF)
            send_o[0] = made[:, half:].astype(BF)

        @pl.when(step < ratio)
        def _():
            put(low_ref[...], gh_ref[...])

        @pl.when(step == ratio)
        def _():
            put(ctx_ref[...], ga_ref[...])

    whole = lambda a: pl.BlockSpec(a.shape, lambda g: (0, 0))
    out = pl.BlockSpec((1, depth, half), lambda g: (g, 0, 0))
    return pl.pallas_call(
        kernel,
        grid=(ratio + 1,),
        out_shape=(shape((ratio + 1, depth, half), BF),) * 2,
        in_specs=[
            whole(context_t), whole(low_t), whole(ga),
            pl.BlockSpec((tokens, depth), lambda g: (0, jnp.minimum(g, ratio - 1))),
        ],
        out_specs=(out, out),
        cost_estimate=pl.CostEstimate(
            flops=2 * tokens * depth * depth * (ratio + 1), bytes_accessed=16 << 20, transcendentals=0
        ),
        name="first_grads",
    )(context_t, low_t, ga, gh)


def second_grads(active_t, gb):
    ff, tokens = active_t.shape
    depth = gb.shape[1]
    half = depth // 2
    shape = jax.ShapeDtypeStruct

    def kernel(act_ref, gb_ref, keep_o, send_o):
        made = mm(act_ref[...], gb_ref[...])
        keep_o[...] = made[:, 0:half].astype(BF)
        send_o[...] = made[:, half:].astype(BF)

    out = pl.BlockSpec((depth, half), lambda g: (g, 0))
    return pl.pallas_call(
        kernel,
        grid=(ff // depth,),
        out_shape=(shape((ff, half), BF),) * 2,
        in_specs=[pl.BlockSpec((depth, tokens), lambda g: (g, 0)), pl.BlockSpec(gb.shape, lambda g: (0, 0))],
        out_specs=(out, out),
        cost_estimate=pl.CostEstimate(flops=2 * tokens * depth * ff, bytes_accessed=14 << 20, transcendentals=0),
        name="second_grads",
    )(active_t, gb)


def attend_back_kernel(
    heads, qkv_ref, g0, g1, g2, g3, log_ref, w_ref, qc_ref,
    grad_o, keep_near_o, keep_chip_o, send_o, sums_o,
    bias_ref, q_ref, k_ref, kt_ref, v_ref, g_ref, gqt_ref, gk_ref, gv_ref,
):
    width = heads * HD
    length = qkv_ref.shape[0]
    rows = length // 4
    factor = BF(1.0 / math.sqrt(HD))
    made = qkv_ref[...]
    for h in range(heads):
        at = h * HD
        q_ref[h] = made[:, at : at + HD] * factor
        key_rows = made[:, width + at : width + at + HD]
        k_ref[h] = key_rows
        kt_ref[h] = (key_rows * factor).T
        v_ref[h] = made[:, 2 * width + at : 2 * width + at + HD]
        for j, piece in enumerate((g0, g1, g2, g3)):
            g_ref[h, j * rows : (j + 1) * rows, :] = piece[...].reshape(rows, width)[:, at : at + HD]
    gk_ref[...] = jnp.zeros_like(gk_ref)
    gv_ref[...] = jnp.zeros_like(gv_ref)
    hidden_pairs(qc_ref[0], bias_ref)

    def block_of(step, carry):
        at = pl.ds(pl.multiple_of(step * 256, 256), 256)
        for h in range(heads):
            q_rows, g_rows = q_ref[h, at, :], g_ref[h, at, :]
            probs = jnp.exp(mm_nt(k_ref[h], q_rows) + (bias_ref[:, at] - log_ref[h : h + 1, at]))
            grad_probs = mm_nt(v_ref[h], g_rows)
            gv_ref[h] += mm(probs.astype(BF), g_rows)
            weighted = probs * grad_probs
            row_dot = jnp.sum(weighted, axis=0, keepdims=True)
            grad_scores = (weighted - probs * row_dot).astype(BF)
            gk_ref[h] += mm(grad_scores, q_rows)
            gqt_ref[h * HD : (h + 1) * HD, at] = mm(kt_ref[h], grad_scores)
        return carry

    lax.fori_loop(0, length // 256, block_of, 0)
    column_sums = jnp.zeros((1, 3 * width), F32)
    targets = (keep_near_o, send_o.at[0:rows], keep_chip_o, send_o.at[rows : 2 * rows])
    for j, out in enumerate(targets):
        part = slice(j * rows, (j + 1) * rows)
        grads = jnp.concatenate(
            [gqt_ref[:, part].T]
            + [gk_ref[h, part, :] for h in range(heads)]
            + [gv_ref[h, part, :] for h in range(heads)],
            axis=1,
        ).astype(BF)
        grad_o[part, :] = grads
        column_sums += jnp.sum(grads.astype(F32), axis=0, keepdims=True)
        out[...] = mm_nt(grads, w_ref[...]).astype(out.dtype)
    sums_o[...] = jnp.broadcast_to(column_sums, sums_o.shape)


def attend_back(seg, rows, qkv, grads_in, log_total, weight, query_code):
    length, width = qkv.shape[0], qkv.shape[1] // 3
    depth, heads = weight.shape[0], width // HD
    shape = jax.ShapeDtypeStruct
    fixed = lambda a: pl.BlockSpec(a.shape, lambda g, n=len(a.shape): (0,) * n)

    def piece(grads):
        if len(grads.shape) == 2:
            return pl.BlockSpec((rows, width), lambda g: (seg, 0))
        return pl.BlockSpec((1, rows, width), lambda g: (0, seg, 0))

    outs = (
        shape((length, 3 * width), BF),
        shape((rows, depth), F32),
        shape((rows, depth), F32),
        shape((2 * rows, depth), BF),
        shape((8, 3 * width), F32),
    )
    return pl.pallas_call(
        lambda *refs: attend_back_kernel(heads, *refs),
        grid=(1,),
        out_shape=outs,
        in_specs=[fixed(qkv)] + [piece(a) for a in grads_in] + [fixed(a) for a in (log_total, weight)]
        + [pl.BlockSpec((1,) + query_code.shape[1:], lambda g: (seg, 0, 0))],
        out_specs=[fixed(o) for o in outs],
        scratch_shapes=[
            pltpu.VMEM((length, length), F32),
            pltpu.VMEM((heads, length, HD), BF),
            pltpu.VMEM((heads, length, HD), BF),
            pltpu.VMEM((heads, HD, length), BF),
            pltpu.VMEM((heads, length, HD), BF),
            pltpu.VMEM((heads, length, HD), BF),
            pltpu.VMEM((width, length), F32),
            pltpu.VMEM((heads, length, HD), F32),
            pltpu.VMEM((heads, length, HD), F32),
        ],
        cost_estimate=pl.CostEstimate(
            flops=2 * length * depth * 3 * width + 40 * length * length * width,
            bytes_accessed=12 << 20,
            transcendentals=heads * length * length,
        ),
        name="attend_back",
    )(qkv, *grads_in, log_total, weight, query_code)


def finish(seg, held, keep, near, far):
    rows, depth = keep.shape
    steps = 2
    part = rows // steps
    block = pl.BlockSpec((part, depth), lambda g: (seg * steps + g, 0))
    whole = pl.BlockSpec((part, depth), lambda g: (g, 0))

    def kernel(held_ref, keep_ref, near_ref, far_ref, out_ref):
        out_ref[...] = held_ref[...] + keep_ref[...] + near_ref[...].astype(F32) + far_ref[...].astype(F32)

    return pl.pallas_call(
        kernel,
        grid=(steps,),
        out_shape=jax.ShapeDtypeStruct(held.shape, F32),
        in_specs=[block, whole, whole, whole],
        out_specs=block,
        input_output_aliases={0: 0},
        cost_estimate=pl.CostEstimate(flops=1 << 20, bytes_accessed=4 << 20, transcendentals=0),
        name="finish",
    )(held, keep, near, far)


def own_columns(values, group, width):
    return lax.dynamic_slice_in_dim(values, group * width, width, axis=1)


def per_device(
    layer_input, doc_starts, mem_rows, w_query, b_query, w_key, w_value, b_value, w_out, b_out,
    attn_gain, attn_shift, w_up, b_up, w_down, b_down, ffn_gain, ffn_shift, grad_out,
):
    segs, rows, depth = layer_input.shape
    groups = lax.axis_size(SEQ)
    width, half = depth // groups, depth // 2
    ff = w_up.shape[1]
    length = rows * groups
    here, place = lax.axis_index(SEQ), lax.axis_index(FSDP)
    upper_core, upper_chip = bit_of(here, CORE), bit_of(here, CHIP)
    core, chip = upper_core.astype(jnp.int32), upper_chip.astype(jnp.int32)
    shard = w_query.shape[0]
    devices = lax.axis_size(FSDP)
    direct = shard % 32 == 0

    over_core = hop(layer_input, SEQ, CORE)
    first, later = (hop(part, SEQ, CHIP) for part in (layer_input[:1], layer_input[1:]))
    first_both, later_both = (hop(part, SEQ, CORE) for part in (first, later))

    def rows_of(i):
        chip_rows, both, at = (first, first_both, 0) if i == 0 else (later, later_both, i - 1)
        return ((layer_input, i), (over_core, i), (chip_rows, at), (both, at))

    vectors = (b_query, b_value, b_out, attn_gain, attn_shift, b_down, ffn_gain, ffn_shift, b_up)
    spot = jnp.stack([here, core, chip]).astype(jnp.int32)
    if direct:
        own, up_part, rest_part = pack(spot, (w_query, w_key, w_value, w_out, w_up, w_down), vectors)
        qkv_pieces = gather_pieces(own)
        order = jnp.arange(devices, dtype=jnp.int32) ^ place

        def two_parts(block):
            pieces = {0: block}
            for shift, n in reversed(fsdp_digits()[1:]):
                for held in list(pieces):
                    for step in range(1, n):
                        pieces[held | step << shift] = hop(pieces[held], FSDP, step << shift)
            near = jnp.stack([pieces[j] for j in sorted(pieces)])
            return near, hop(near, FSDP, 1)

        rest = two_parts(rest_part)
        rest_far = [hop(part, SEQ, CHIP) for part in rest]
        up = two_parts(up_part)
        middle_weights = (
            *up, *[hop(part, SEQ, CORE) for part in up],
            *rest, *rest_far,
            *[hop(part, SEQ, CORE) for part in rest],
            *[hop(part, SEQ, CORE) for part in rest_far],
        )
        up_bias = jnp.zeros((1, ff), F32)
        qkv_bias = jnp.zeros((1, 3 * width), F32)
    else:
        own = jnp.concatenate([own_columns(w, here, width) for w in (w_query, w_key, w_value)], axis=1)
        qkv_pieces = [lax.all_gather(own, FSDP, axis=0, tiled=True)]
        found = lax.all_gather(jnp.concatenate(vectors), FSDP, axis=0).astype(F32)
        order = jnp.zeros((1,), jnp.int32)
        out_whole, up_whole, down_whole = (
            lax.all_gather(w, FSDP, axis=0, tiled=True) for w in (w_out, w_up, w_down)
        )
        up_halves, down_halves = up_whole.reshape(depth, 2, ff // 2), down_whole.reshape(2, ff // 2, depth)
        middle_weights = (
            out_whole,
            jnp.where(upper_core, up_halves[:, ::-1], up_halves).reshape(depth, ff),
            jnp.where(upper_core, down_halves[::-1], down_halves).reshape(ff, depth),
        )
        names = len(vectors) - 1
        q_bias, v_bias, o_bias, gain_one, shift_one, down_bias, gain_two, shift_two = (
            found[:, i * shard : (i + 1) * shard].reshape(-1) for i in range(names)
        )
        up_bias = found[:, names * shard :].reshape(2, ff // 2)
        up_bias = jnp.where(upper_core, up_bias[::-1], up_bias).reshape(1, ff)
        vector_rows = jnp.stack([o_bias, gain_one, shift_one, down_bias, gain_two, shift_two, o_bias, o_bias])
        qkv_bias = jnp.concatenate(
            [
                lax.dynamic_slice_in_dim(q_bias, here * width, width),
                jnp.zeros((width,), F32),
                lax.dynamic_slice_in_dim(v_bias, here * width, width),
            ]
        )[None, :]
    piece_rows = shard if direct else devices * shard
    order = jnp.concatenate([order, spot])

    spots = jnp.arange(length, dtype=jnp.int32)
    positions = ((spots // rows) ^ here) * rows + spots % rows
    doc_ids = jnp.sum((doc_starts[:, :, None] <= positions[None, None, :]).astype(F32), axis=1)
    is_memory = jnp.any(mem_rows[:, :, None] == positions[None, None, :], axis=1)
    penalty = jnp.where(is_memory, 0.0, MASKED)
    query_code = jnp.stack([doc_ids, penalty] + [jnp.zeros_like(doc_ids)] * 6, axis=1)

    done = []
    for i in range(segs):
        done.append(attend(i, order, rows_of(i), qkv_pieces, piece_rows, qkv_bias, query_code))

    contexts = []
    for i in range(segs):
        near, to_core, to_chip = done[i][3:6]
        from_core = hop(to_core, SEQ, CORE)
        from_chip = hop(to_chip, SEQ, CHIP)
        contexts.append((near, from_core, from_chip, hop(from_chip[rows:], SEQ, CORE)))

    (
        layer_out, context_t, low_t, active_t, gb, gh, ga, grad_sum_one, g0, g1, g2, g3, vector_sums,
    ) = middle(
        order, middle_weights, shard, direct, contexts, layer_input.reshape(segs * rows, depth),
        grad_out.reshape(segs * rows, depth), done[0][7] if direct else vector_rows, up_bias,
    )
    heads_grads = (g0, hop(g1, SEQ, CORE), hop(g2, SEQ, CHIP), hop(hop(g3, SEQ, CORE), SEQ, CHIP))

    digits = fsdp_digits()
    place_digits = [(FSDP, shift, n, place) for shift, n in digits]

    second_keep, second_send = second_grads(active_t, gb)
    second_got = hop(second_send, SEQ, CORE)
    first_keep, first_send = first_grads(context_t, low_t, ga, gh)
    first_got = hop(first_send, SEQ, CORE)
    vector_sums = vector_sums + hop(vector_sums, SEQ, CORE)

    sizes = tuple(n for _, n in reversed(digits))
    count = len(digits)
    below = list(range(count - 1, -1, -1))

    def x_then_chip(values):
        values = values.reshape((values.shape[0],) + sizes + (2, -1, half))
        turn = [below[0] + 1, count + 1] + [b + 1 for b in below[1:]] + [0, count + 2, count + 3]
        return values.transpose(turn)

    def chip_then_x(values):
        values = values.reshape(sizes + (2, -1, half))
        return values.transpose([count] + below + [count + 1, count + 2])

    digit = [(place >> shift) & (n - 1) for shift, n in digits]
    over_x, over_chip = (FSDP, digits[0][0], digit[0]), (SEQ, 1, chip)

    def added(*terms):
        return lambda path: sum(entry_at(t, path).astype(F32) for t in terms)

    def chain(base, steps):
        path, arrived = [], []

        def total(at):
            return base(at) + sum(entry_at(a, at[d:]).astype(F32) for d, a in arrived)

        for axis, shift, mine in steps:
            send = total(path + [1 - mine]).astype(BF)
            path = path + [mine]
            arrived.append((len(path), hop(send, axis, 1 << shift)))
        return lambda rest: total(path + rest)

    first_sum = added(x_then_chip(first_keep), x_then_chip(first_got))
    second_sum = added(chip_then_x(second_keep), chip_then_x(second_got))
    vector_sum = added(chip_then_x(vector_sums))
    second_total = chain(
        lambda path: jnp.concatenate([second_sum(path), vector_sum(path)], axis=-2), (over_chip, over_x)
    )
    first_total = chain(first_sum, (over_x, over_chip))

    backs = []
    for i in range(segs):
        backs.append(
            attend_back(i, rows, done[i][0], heads_grads, done[i][6], done[0][2], query_code)
        )

    if count == 2:
        def joint(at):
            return jnp.concatenate([part([at]).reshape(-1, half) for part in (first_total, second_total)], axis=0)

        shift, n = digits[1]
        arrived = [hop(joint(digit[1] ^ k).astype(BF), FSDP, k << shift) for k in range(1, n)]
        mine = joint(digit[1]) + sum(a.astype(F32) for a in arrived)
    else:
        rest = place_digits[1:]
        lead = tuple(n for _, _, n, _ in rest) + (-1, half)
        merged = jnp.concatenate([part([]).reshape(lead) for part in (first_total, second_total)], axis=-2)
        mine = halve(merged, rest)
    mine = mine.astype(BF)
    other = hop(mine, SEQ, CHIP)
    far = [hop(part, SEQ, CORE) for part in (mine, other)]
    part_rows, ratio = shard // 2, ff // depth

    def quarter(values):
        blocks = values[: (ratio + 1) * part_rows].reshape(ratio + 1, part_rows, half)
        return (
            blocks[ratio],
            jnp.concatenate([blocks[i] for i in range(ratio)], axis=1),
            values[(ratio + 1) * part_rows :],
        )

    corners = [quarter(values[:-8]) for values in (mine, other, *far)]
    vector_rows = jnp.where(upper_chip, other[-8:], mine[-8:]).astype(F32)
    per = half // shard

    def vector_of(i):
        return vector_rows[i // per, i % per * shard : (i % per + 1) * shard]


    def assembled(i):
        near = joined(corners[0][i], corners[1][i], upper_chip, 0)
        return joined(near, joined(corners[2][i], corners[3][i], upper_chip, 0), upper_core, 1).astype(F32)

    grad_w_out, grad_w_up, grad_w_down = (assembled(i) for i in range(3))

    grad_input = grad_sum_one
    for i in range(segs):
        _, keep_near, keep_chip, send, _ = backs[i]
        near = hop(send, SEQ, CORE)
        far = (keep_chip + near[rows:].astype(F32)).astype(BF)
        grad_input = finish(i, grad_input, keep_near, near, hop(far, SEQ, CHIP))

    grad_qkv = sum(mm_tn(done[i][1], backs[i][0]) for i in range(segs - 1))
    grad_qkv = grad_qkv + mm_tn(done[-1][1], backs[-1][0])
    grad_qkv = grad_qkv.reshape(tuple(n for _, n in reversed(digits)) + (shard, 3 * width))
    grad_qkv = grad_qkv.transpose(list(range(len(digits) - 1, -1, -1)) + [len(digits), len(digits) + 1])
    bias_rows = sum(backs[i][4] for i in range(segs))
    mine = halve(grad_qkv, place_digits, bias_rows).astype(BF)
    other = hop(mine, SEQ, CORE)
    far_mine = hop(mine, SEQ, CHIP)
    far_other = hop(other, SEQ, CHIP)
    parts = swapped([mine, other, far_mine, far_other], upper_core, upper_chip)

    def columns_of(i):
        return jnp.concatenate([p[:, i * width : (i + 1) * width] for p in parts], axis=1).astype(F32)

    def own_part(vector):
        count = vector.shape[0] * shard // depth
        return lax.dynamic_slice_in_dim(vector, place * count, count)

    grad_q, grad_k, grad_v = (columns_of(i) for i in range(3))
    return (
        layer_out.reshape(layer_input.shape),
        grad_input.reshape(layer_input.shape),
        grad_q[:shard],
        own_part(grad_q[shard]),
        grad_k[:shard],
        grad_v[:shard],
        own_part(grad_v[shard]),
        grad_w_out,
        vector_of(0),
        vector_of(1),
        vector_of(2),
        grad_w_up,
        jnp.concatenate([vector_of(6 + r) for r in range(ratio)]),
        grad_w_down,
        vector_of(3),
        vector_of(4),
        vector_of(5),
    )


def solution(mesh):
    rows, cols = P(FSDP, SEQ, None), P(FSDP, None)
    vec = P(FSDP)
    return jax.shard_map(
        per_device,
        mesh=mesh,
        in_specs=(
            rows, cols, cols, cols, vec, cols, cols, vec, cols, vec,
            vec, vec, cols, vec, cols, vec, vec, vec, rows,
        ),
        out_specs=(
            rows, rows, cols, vec, cols, cols, vec, cols, vec,
            vec, vec, cols, vec, cols, vec, vec, vec,
        ),
        check_vma=False,
    )
```

```python
import math

import jax
import jax.numpy as jnp
from jax import lax
from jax.experimental import pallas as pl
from jax.experimental.pallas import tpu as pltpu
from jax.sharding import PartitionSpec as P


HD = 64
LN_EPS = 1e-12
MASKED = -1e30
BF = jnp.bfloat16
F32 = jnp.float32


CORE, CHIP = 1, 2


SEQ, FSDP = "seq", "fsdp"


def hop(values, axis, bit):
    size = lax.axis_size(axis)
    return lax.ppermute(values, axis, [(i, i ^ bit) for i in range(size)])


def bit_of(index, bit):
    return (index & bit) != 0


def joined(mine, other, upper, axis):
    low = jnp.where(upper, other, mine)
    high = jnp.where(upper, mine, other)
    return jnp.concatenate([low, high], axis=axis)


def fsdp_digits():
    bits = lax.axis_size(FSDP).bit_length() - 1
    digits, at = [], 0
    while at < bits:
        take = 1 if at == 0 else min(2, bits - at)
        digits.append((at, 1 << take))
        at += take
    return digits


def gather_pieces(block):
    pieces = {0: block}
    for shift, size in reversed(fsdp_digits()):
        for held in list(pieces):
            for step in range(1, size):
                entry = held | step << shift
                pieces[entry] = hop(pieces[held], FSDP, step << shift)
    return [pieces[j] for j in range(len(pieces))]


def entry_at(values, indices):
    for index in indices:
        values = lax.dynamic_index_in_dim(values, index, values.ndim - 3, keepdims=False)
    return values


def halve(held, steps, extra=None):
    arrived, kept = [], []

    def total(index):
        values = entry_at(held, [k for k in kept] + [index] if index is not None else kept).astype(F32)
        if extra is not None:
            rows = jnp.broadcast_to(extra, values.shape[:-2] + extra.shape)
            values = jnp.concatenate([values, rows], axis=-2)
        for at, group in arrived:
            path = kept[at:] + ([index] if index is not None else [])
            for got in group:
                values = values + entry_at(got, path).astype(F32)
        return values

    for axis, shift, size, place in steps:
        digit = (place >> shift) & (size - 1)
        group = [hop(total(digit ^ step).astype(BF), axis, step << shift) for step in range(1, size)]
        kept.append(digit)
        arrived.append((len(kept), group))
    return total(None)


def mm(left, right):
    return lax.dot_general(left, right, (((1,), (0,)), ((), ())), preferred_element_type=F32)


def mm_nt(left, right):
    return lax.dot_general(left, right, (((1,), (1,)), ((), ())), preferred_element_type=F32)


def hidden_pairs(query_code, key_code, bias_ref, start, stop):
    step = 128
    for at in range(start, stop, step):
        part = key_code[at : at + step, :]
        same = part[:, 0:1] == query_code[0:1, :]
        bias_ref[at : at + step, :] = jnp.where(same, 0.0, jnp.maximum(part[:, 1:2], query_code[1:2, :]))


def erf_parts(values):
    cdf = 0.5 * (1.0 + lax.erf(values * (1.0 / math.sqrt(2.0))))
    return cdf, jnp.exp(-0.5 * values * values) * (1.0 / math.sqrt(2.0 * math.pi))


def place_rows(pieces, order_ref, rows, target):
    for j, piece in enumerate(pieces):
        at = pl.multiple_of(order_ref[j] * rows, rows)
        target[pl.ds(at, rows), :] = piece[0:rows, :]


def attend_kernel(heads, shard, count, order_ref, x0, x1, x2, x3, *refs):
    pieces, refs = refs[:count], refs[count:]
    b_ref, qc_ref, q_ref, k_ref, kt_ref, v_ref, xrel_o, w_o, near_o, core_o, chip_o, log_o, vec_o = refs[:13]
    bias_ref, vt_ref, ctx_ref, score_ref = refs[13:]
    width = heads * HD
    rows = x0.shape[1]
    length = 4 * rows
    place_rows(pieces, order_ref, shard, w_o)
    added = b_ref[...]
    if count > 1:
        for j, piece in enumerate(pieces):
            vec_o[order_ref[j]] = piece[shard:, 0:128].astype(F32)
        here = order_ref[count]
        near, far = vec_o[2 * here], vec_o[2 * here + 1]
        added = jnp.concatenate(
            [near[0:1, 0:shard], far[0:1, 0:shard], jnp.zeros((1, width), F32), near[1:2, 0:shard], far[1:2, 0:shard]],
            axis=1,
        )
    factor = BF(1.0 / math.sqrt(HD))
    query_code = qc_ref[0]
    key_code = query_code.T
    for j, piece in enumerate((x0, x1, x2, x3)):
        part = slice(j * rows, (j + 1) * rows)
        xrel_o[:, part] = piece[0].T
        made = (mm(piece[0], w_o[...]) + added).astype(BF)
        hidden_pairs(query_code, key_code, bias_ref, j * rows, (j + 1) * rows)
        turned = made.T
        for h in range(heads):
            at = h * HD
            q_ref[h, part, :] = made[:, at : at + HD] * factor
            k_ref[h, part, :] = made[:, width + at : width + at + HD]
            kt_ref[h, :, part] = turned[width + at : width + at + HD] * factor
            v_ref[h, part, :] = made[:, 2 * width + at : 2 * width + at + HD]
            vt_ref[h, :, part] = turned[2 * width + at : 2 * width + at + HD]
    block, chunk = 256, 256
    blocks = length // block

    def score(h, at, slot):
        top = None
        for start in range(0, length, chunk):
            keys = slice(start, start + chunk)
            scores = mm_nt(k_ref[h, keys, :], q_ref[h, at, :]) + bias_ref[keys, at]
            score_ref[slot, keys, :] = scores
            largest = jnp.max(scores.reshape(chunk // 8, 8, block), axis=0)
            top = largest if top is None else jnp.maximum(top, largest)
        return jnp.max(top, axis=0, keepdims=True)

    def one(h, top):
        for b in range(blocks):
            at = slice(b * block, (b + 1) * block)
            if b + 1 < blocks:
                following = score(h, slice((b + 1) * block, (b + 2) * block), (b + 1) % 2)
            else:
                following = score(jnp.minimum(h + 1, heads - 1), slice(0, block), 0)
            total, made = jnp.zeros((8, block), F32), jnp.zeros((HD, block), F32)
            for start in range(0, length, chunk):
                keys = slice(start, start + chunk)
                shifted = jnp.exp(score_ref[b % 2, keys, :] - top)
                total = total + jnp.sum(shifted.reshape(chunk // 8, 8, block), axis=0)
                made = made + mm(vt_ref[h, :, keys], shifted.astype(BF))
            total = jnp.sum(total, axis=0, keepdims=True)
            ctx_ref[pl.ds(pl.multiple_of(h * HD, HD), HD), at] = made / total
            log_o[pl.ds(h, 1), at] = top + jnp.log(total)
            top = following
        return top

    lax.fori_loop(0, heads, one, score(0, slice(0, block), 0))
    near_o[...] = ctx_ref[:, 0:rows].T.astype(BF)
    core_o[...] = ctx_ref[:, rows : 2 * rows].T.astype(BF)
    chip_o[...] = ctx_ref[:, 2 * rows : 4 * rows].T.astype(BF)


def attend(seg, order, pieces, weights, shard, bias, query_code):
    (first, _), width = pieces[0], bias.shape[1] // 3
    rows, depth = first.shape[1:]
    length, heads = 4 * rows, width // HD
    shape = jax.ShapeDtypeStruct
    vmem = pl.BlockSpec(memory_space=pltpu.VMEM)

    def rows_of(at):
        return pl.BlockSpec((1, rows, depth), lambda g, at=at: (at, 0, 0))

    count = len(weights)
    whole = lambda a: pl.BlockSpec(a.shape, lambda g, n=len(a.shape): (0,) * n)
    outs = (
        shape((heads, length, HD), BF),
        shape((heads, length, HD), BF),
        shape((heads, HD, length), BF),
        shape((heads, length, HD), BF),
        shape((depth, length), BF),
        shape((depth, 3 * width), BF),
        shape((rows, width), BF),
        shape((rows, width), BF),
        shape((2 * rows, width), BF),
        shape((8, length), F32),
        shape((count, max(weights[0].shape[0] - shard, 8), 128), F32),
    )
    return pl.pallas_call(
        lambda *refs: attend_kernel(heads, shard, count, *refs),
        grid=(1,),
        out_shape=outs,
        in_specs=[pl.BlockSpec(memory_space=pltpu.SMEM)]
        + [rows_of(at) for _, at in pieces]
        + [whole(w) for w in weights]
        + [whole(bias), pl.BlockSpec((1,) + query_code.shape[1:], lambda g: (seg, 0, 0))],
        out_specs=[whole(o) for o in outs],
        scratch_shapes=[
            pltpu.VMEM((length, length), F32),
            pltpu.VMEM((heads, HD, length), BF),
            pltpu.VMEM((width, length), F32),
            pltpu.VMEM((2, length, 256), F32),
        ],
        cost_estimate=pl.CostEstimate(
            flops=2 * length * depth * 3 * width + 16 * length * length * width,
            bytes_accessed=12 << 20,
            transcendentals=heads * length * length,
        ),
        name="attend",
    )(order, *[p for p, _ in pieces], *weights, bias, query_code)


def pack_kernel(place_ref, wq, wk, wv, wo, wu, wd, *refs):
    vectors, (own_o, up_o, rest_o) = refs[:-3], refs[-3:]
    here, core, chip = place_ref[0], place_ref[1], place_ref[2]
    shard, depth = wq.shape
    width, half, rows = depth // 4, depth // 2, shard // 2
    for i, ref in enumerate((wq, wk, wv)):
        picked = ref[:, 0:width]
        for j in range(1, 4):
            picked = jnp.where(here == j, ref[:, j * width : (j + 1) * width], picked)
        own_o[0:shard, i * width : (i + 1) * width] = picked
    below = [ref[0:1, at : at + shard] for ref in vectors for at in range(0, ref.shape[1], shard)]
    below.append(jnp.zeros((own_o.shape[0] - shard - len(below), shard), BF))
    own_o[shard:, :] = jnp.zeros((own_o.shape[0] - shard, 3 * width), BF)
    own_o[shard:, 0:shard] = jnp.concatenate([b.astype(F32) for b in below], axis=0).astype(BF)
    ff_half = wu.shape[1] // 2
    up_o[...] = wu[:, pl.ds(pl.multiple_of(core * ff_half, ff_half), ff_half)]
    columns = pl.ds(pl.multiple_of(core * half, half), half)
    at = pl.multiple_of(chip * rows, rows)
    rest_o[:, 0:half] = wo[pl.ds(at, rows), columns]
    for i in range(wd.shape[0] // shard):
        rest_o[:, (i + 1) * half : (i + 2) * half] = wd[pl.ds(i * shard + at, rows), columns]


def pack(place, weights, vectors):
    shard, depth = weights[0].shape
    ff, ratio = weights[4].shape[1], weights[5].shape[0] // shard
    shape = jax.ShapeDtypeStruct
    vmem = pl.BlockSpec(memory_space=pltpu.VMEM)
    return pl.pallas_call(
        pack_kernel,
        out_shape=(
            shape((shard + 16, 3 * depth // 4), BF),
            shape((shard, ff // 2), BF),
            shape((shard // 2, (1 + ratio) * depth // 2), BF),
        ),
        in_specs=[pl.BlockSpec(memory_space=pltpu.SMEM)] + [vmem] * (6 + len(vectors)),
        out_specs=[vmem] * 3,
        cost_estimate=pl.CostEstimate(flops=1 << 16, bytes_accessed=4 << 20, transcendentals=0),
        name="pack",
    )(place, *weights, *[v[None, :] for v in vectors])


def norm_stats(values):
    centre = values - jnp.mean(values, axis=-1, keepdims=True)
    inv_dev = lax.rsqrt(jnp.mean(centre * centre, axis=-1, keepdims=True) + LN_EPS)
    return centre * inv_dev, inv_dev


def norm_back(grads, unit, inv_dev, gain):
    scaled = grads * gain
    return inv_dev * (
        scaled
        - jnp.mean(scaled, axis=-1, keepdims=True)
        - unit * jnp.mean(scaled * unit, axis=-1, keepdims=True)
    )


def swapped(parts, upper_core, upper_chip):
    a, b, c, d = parts
    a, b, c, d = (jnp.where(upper_core, y, x) for x, y in ((a, b), (b, a), (c, d), (d, c)))
    return [jnp.where(upper_chip, y, x) for x, y in ((a, c), (b, d), (c, a), (d, b))]


def middle_kernel(segs, shard_rows, direct, order_ref, *refs):
    weights_in, refs = (refs[:16], refs[16:]) if direct else (refs[:3], refs[3:])
    context_in, refs = refs[: 4 * segs], refs[4 * segs :]
    x_ref, go_ref, vec_ref, up_ref = refs[:4]
    (
        out_o, ctx_o, low_o, act_o, gb_o, gh_o, ga_o, gsum_o, g0_o, g1_o, g2_o, g3_o, vec_o,
    ) = refs[4:17]
    wo, wu, wd, slope_ref, half_ref, vec_s, up_s, sums_o, up_sums_o, sems = refs[17:]
    seg = pl.program_id(0)
    depth, ff = wu.shape
    rows, half, ff_half = x_ref.shape[0], depth // 2, ff // 2
    _, core, chip = (order_ref[order_ref.shape[0] - 3 + i] for i in range(3))
    upper_core, upper_chip = core != 0, chip != 0

    def copies():
        if not direct:
            return [[(a, b)] for a, b in zip(weights_in, (wo, wu, wd))]
        found = [[], [], []]
        near, shard = weights_in[0].shape[:2]
        part, ratio = shard // 2, ff // depth
        for side in range(2):
            column = pl.multiple_of((core ^ side) * half, half)
            for low in range(2):
                for j in range(near):
                    block = order_ref[2 * j + low]
                    at = pl.multiple_of(block * shard, shard)
                    for i in range(2):
                        start = side * ff_half + i * ff_half // 2
                        found[1].append(
                            (weights_in[4 * side + 2 * i + low].at[j],
                             wu.at[pl.ds(at, shard), pl.ds(start, ff_half // 2)])
                        )
                    for other in range(2):
                        piece = weights_in[8 + 4 * side + 2 * other + low]
                        inner = (chip ^ other) * part
                        found[0].append(
                            (piece.at[j, :, 0:half],
                             wo.at[pl.ds(pl.multiple_of(at + inner, part), part), pl.ds(column, half)])
                        )
                        for i in range(ratio):
                            row = (block * ratio + i) * shard
                            turned = jnp.where(row < ff_half, row + core * ff_half, row - core * ff_half)
                            turned = pl.multiple_of(turned + inner, part)
                            found[2].append(
                                (piece.at[j, :, (i + 1) * half : (i + 2) * half],
                                 wd.at[pl.ds(turned, part), pl.ds(column, half)])
                            )
        return found

    groups, used = [], 0
    for found in copies():
        groups.append([pltpu.make_async_copy(a, b, sems.at[used + i]) for i, (a, b) in enumerate(found)])
        used += len(found)

    @pl.when(seg == 0)
    def _():
        for group in groups:
            for one in group:
                one.start()
        if direct:
            count, shard = vec_ref.shape[0], weights_in[0].shape[1]
            for i in range(6):
                vec_s[i : i + 1, :] = jnp.concatenate(
                    [vec_ref[j, i + 2 : i + 3, 0:shard] for j in range(count)], axis=1
                )
            halves = [
                jnp.concatenate(
                    [
                        vec_ref[j, 8 + r : 9 + r, 0:shard]
                        for j in range(side * count // 2, (side + 1) * count // 2)
                        for r in range(ff // depth)
                    ],
                    axis=1,
                )
                for side in range(2)
            ]
            up_s[:, 0:ff_half] = jnp.where(upper_core, halves[1], halves[0])
            up_s[:, ff_half:] = jnp.where(upper_core, halves[0], halves[1])
        else:
            vec_s[...] = vec_ref[...]
            up_s[...] = up_ref[...]
        sums_o[...] = jnp.zeros_like(sums_o)
        up_sums_o[...] = jnp.zeros_like(up_sums_o)

    def ready(which):
        @pl.when(seg == 0)
        def _():
            for one in groups[which]:
                one.wait()

    def vector(i):
        return vec_s[i : i + 1, :]

    ready(0)
    parts = []
    for j in range(4):
        picked = context_in[j][...]
        for i in range(1, segs):
            picked = jnp.where(seg == i, context_in[4 * i + j][...], picked)
        parts.append(picked)
    context = jnp.concatenate(swapped(parts, upper_core, upper_chip), axis=1)
    ctx_o[...] = context.T
    summed = x_ref[...].astype(F32) + mm(context, wo[...]) + vector(0)
    unit_one, inv_one = norm_stats(summed)
    normed_one = unit_one * vector(1) + vector(2)
    low = normed_one.astype(BF)
    low_o[...] = low.T
    ready(1)
    ready(2)
    step = depth if ff_half % depth == 0 else ff_half
    branch = jnp.zeros((rows, depth), F32)
    for start in range(0, ff, step):
        part = slice(start, start + step)
        hidden = mm(low, wu[:, part]) + up_s[:, part]
        cdf, density = erf_parts(hidden)
        active = (hidden * cdf).astype(BF)
        slope_ref[:, part] = cdf + hidden * density
        side = 0 if start < ff_half else 1
        target = pl.multiple_of((core ^ side) * ff_half, ff_half) + (start - side * ff_half)
        act_o[pl.ds(pl.multiple_of(target, 128), step), :] = active.T
        branch = branch + mm(active, wd[part, :])
    unit_two, inv_two = norm_stats(normed_one + (branch + vector(3)))
    out_o[...] = (unit_two * vector(4) + vector(5)).astype(BF)

    def add_sum(i, values):
        sums_o[i : i + 1, :] += jnp.sum(values, axis=0, keepdims=True)

    def halves(values, out):
        half_ref[...] = values
        out[:, 0:half] = half_ref[:, pl.ds(pl.multiple_of(core * half, half), half)].astype(BF)
        out[:, half:] = half_ref[:, pl.ds(pl.multiple_of((1 - core) * half, half), half)].astype(BF)

    grads = go_ref[...].astype(F32)
    add_sum(4, grads * unit_two)
    add_sum(5, grads)
    grad_two = norm_back(grads, unit_two, inv_two, vector(4))
    grad_branch = grad_two.astype(BF)
    add_sum(3, grad_branch.astype(F32))
    halves(grad_branch.astype(F32), gb_o)
    grad_normed = grad_two
    for start in range(0, ff, step):
        part = slice(start, start + step)
        grad_hidden = (mm_nt(grad_branch, wd[part, :]) * slope_ref[:, part]).astype(BF)
        side, first = start // ff_half, start % ff_half
        for at in range(0, step, half):
            target = 2 * (first + at) + side * half
            gh_o[:, target : target + half] = grad_hidden[:, at : at + half]
        up_sums_o[:, part] += jnp.sum(grad_hidden.astype(F32), axis=0, keepdims=True)
        grad_normed = grad_normed + mm_nt(grad_hidden, wu[:, part])
    add_sum(1, grad_normed * unit_one)
    add_sum(2, grad_normed)
    grad_one = norm_back(grad_normed, unit_one, inv_one, vector(1))
    gsum_o[...] = grad_one
    grad_attn = grad_one.astype(BF)
    add_sum(0, grad_attn.astype(F32))
    halves(grad_attn.astype(F32), ga_o)
    grad_context = mm_nt(grad_attn, wo[...]).astype(BF)
    width = depth // 4
    turned = swapped([grad_context[:, j * width : (j + 1) * width] for j in range(4)], upper_core, upper_chip)
    g0_o[...] = turned[0]
    g1_o[...] = turned[1]
    g2_o[...] = turned[2]
    g3_o[...] = turned[3]

    @pl.when(seg == segs - 1)
    def _():
        low_half, high_half = up_sums_o[:, 0:ff_half], up_sums_o[:, ff_half:]
        ordered = jnp.concatenate(
            [jnp.where(upper_core, high_half, low_half), jnp.where(upper_core, low_half, high_half)], axis=1
        )
        vec_o[...] = jnp.zeros_like(vec_o)
        ratio, per = ff // depth, half // shard_rows
        for f in range(depth // shard_rows):
            own = slice(f * shard_rows, (f + 1) * shard_rows)
            parts = [sums_o[i : i + 1, own] for i in range(6)] + [
                ordered[:, (f * ratio + r) * shard_rows : (f * ratio + r + 1) * shard_rows] for r in range(ratio)
            ]
            for row in range(0, len(parts), per):
                line = jnp.concatenate(parts[row : row + per], axis=1)
                vec_o[2 * f, row // per : row // per + 1, 0 : line.shape[1]] = line


def middle(order, weights, shard, direct, contexts, rows_in, grad_out, vectors, up_bias):
    tokens, depth = rows_in.shape
    ff, segs = up_bias.shape[1], len(contexts)
    rows, width, half = tokens // segs, depth // 4, depth // 2
    shape = jax.ShapeDtypeStruct
    fixed = lambda a: pl.BlockSpec(a.shape, lambda g, n=len(a.shape): (0,) * n)
    moving = lambda columns: pl.BlockSpec((rows, columns), lambda g: (g, 0))
    turned = lambda units: pl.BlockSpec((units, rows), lambda g: (0, g))
    outs = [
        (shape((tokens, depth), BF), moving(depth)),
        (shape((depth, tokens), BF), turned(depth)),
        (shape((depth, tokens), BF), turned(depth)),
        (shape((ff, tokens), BF), turned(ff)),
    ]
    for columns, kind in [(depth, BF), (ff, BF), (depth, BF), (depth, F32), (width, BF), (width, BF),
                          (width, BF), (width, BF)]:
        outs.append((shape((tokens, columns), kind), moving(columns)))
    last = shape((2 * depth // shard, 8, half), F32)
    outs.append((last, fixed(last)))
    piece = pl.BlockSpec((rows, width), lambda g: (0, 0))
    flat = [one for four in contexts for one in four]
    if direct:
        copies = 2 * (2 * weights[0].shape[0]) * (2 + 2 * (1 + ff // depth))
    else:
        copies = 3
    return pl.pallas_call(
        lambda *refs: middle_kernel(segs, shard, direct, *refs),
        grid=(segs,),
        out_shape=tuple(o for o, _ in outs),
        in_specs=[pl.BlockSpec(memory_space=pltpu.SMEM)]
        + [pl.BlockSpec(memory_space=pl.ANY)] * len(weights)
        + [piece] * len(flat)
        + [moving(depth), moving(depth), fixed(vectors), fixed(up_bias)],
        out_specs=[b for _, b in outs],
        scratch_shapes=[
            pltpu.VMEM((depth, depth), BF),
            pltpu.VMEM((depth, ff), BF),
            pltpu.VMEM((ff, depth), BF),
            pltpu.VMEM((rows, ff), F32),
            pltpu.VMEM((rows, depth), F32),
            pltpu.VMEM((8, depth), F32),
            pltpu.VMEM((1, ff), F32),
            pltpu.VMEM((8, depth), F32),
            pltpu.VMEM((1, ff), F32),
            pltpu.SemaphoreType.DMA((copies,)),
        ],
        cost_estimate=pl.CostEstimate(
            flops=4 * tokens * depth * (depth + 2 * ff), bytes_accessed=40 << 20,
            transcendentals=2 * tokens * ff,
        ),
        name="middle",
    )(order, *weights, *flat, rows_in, grad_out, vectors, up_bias)


def first_grads(context_t, low_t, ga, gh):
    depth, tokens = low_t.shape
    half, ratio = depth // 2, gh.shape[1] // depth
    shape = jax.ShapeDtypeStruct

    def kernel(ctx_ref, low_ref, ga_ref, gh_ref, keep_o, send_o):
        step = pl.program_id(0)

        def put(left, right):
            made = mm(left, right)
            keep_o[0] = made[:, 0:half].astype(BF)
            send_o[0] = made[:, half:].astype(BF)

        @pl.when(step < ratio)
        def _():
            put(low_ref[...], gh_ref[...])

        @pl.when(step == ratio)
        def _():
            put(ctx_ref[...], ga_ref[...])

    whole = lambda a: pl.BlockSpec(a.shape, lambda g: (0, 0))
    out = pl.BlockSpec((1, depth, half), lambda g: (g, 0, 0))
    return pl.pallas_call(
        kernel,
        grid=(ratio + 1,),
        out_shape=(shape((ratio + 1, depth, half), BF),) * 2,
        in_specs=[
            whole(context_t), whole(low_t), whole(ga),
            pl.BlockSpec((tokens, depth), lambda g: (0, jnp.minimum(g, ratio - 1))),
        ],
        out_specs=(out, out),
        cost_estimate=pl.CostEstimate(
            flops=2 * tokens * depth * depth * (ratio + 1), bytes_accessed=16 << 20, transcendentals=0
        ),
        name="first_grads",
    )(context_t, low_t, ga, gh)


def second_grads(active_t, gb):
    ff, tokens = active_t.shape
    depth = gb.shape[1]
    half = depth // 2
    shape = jax.ShapeDtypeStruct

    def kernel(act_ref, gb_ref, keep_o, send_o):
        made = mm(act_ref[...], gb_ref[...])
        keep_o[...] = made[:, 0:half].astype(BF)
        send_o[...] = made[:, half:].astype(BF)

    out = pl.BlockSpec((depth, half), lambda g: (g, 0))
    return pl.pallas_call(
        kernel,
        grid=(ff // depth,),
        out_shape=(shape((ff, half), BF),) * 2,
        in_specs=[pl.BlockSpec((depth, tokens), lambda g: (g, 0)), pl.BlockSpec(gb.shape, lambda g: (0, 0))],
        out_specs=(out, out),
        cost_estimate=pl.CostEstimate(flops=2 * tokens * depth * ff, bytes_accessed=14 << 20, transcendentals=0),
        name="second_grads",
    )(active_t, gb)


def attend_back_kernel(
    heads, q_ref, k_ref, kt_ref, v_ref, g0, g1, g2, g3, log_ref, w_ref, qc_ref,
    grad_o, keep_near_o, keep_chip_o, send_o, sums_o,
    bias_ref, g_ref, gqt_ref, gk_ref, gv_ref, score_ref, prob_ref,
):
    length = grad_o.shape[0]
    rows = length // 4
    for h in range(heads):
        at = h * HD
        for j, piece in enumerate((g0, g1, g2, g3)):
            g_ref[h, j * rows : (j + 1) * rows, :] = piece[:, at : at + HD]
    query_code = qc_ref[0]
    hidden_pairs(query_code, query_code.T, bias_ref, 0, length)
    block, chunk = 256, 256
    blocks = length // block

    def score(h, at, slot):
        log_total = log_ref[pl.ds(h, 1), at]
        for start in range(0, length, chunk):
            keys = slice(start, start + chunk)
            score_ref[slot, keys, :] = mm_nt(k_ref[h, keys, :], q_ref[h, at, :]) + (bias_ref[keys, at] - log_total)
            prob_ref[slot, keys, :] = mm_nt(v_ref[h, keys, :], g_ref[h, at, :])

    score(0, slice(0, block), 0)

    def one(h, carry):
        for b in range(blocks):
            at, slot = slice(b * block, (b + 1) * block), b % 2
            if b + 1 < blocks:
                score(h, slice((b + 1) * block, (b + 2) * block), 1 - slot)
            else:
                score(jnp.minimum(h + 1, heads - 1), slice(0, block), 1 - slot)

            def put(ref, keys, values):
                ref[h, keys, :] = values if b == 0 else ref[h, keys, :] + values

            row_dot = jnp.zeros((8, block), F32)
            for start in range(0, length, chunk):
                keys = slice(start, start + chunk)
                probs = jnp.exp(score_ref[slot, keys, :])
                weighted = probs * prob_ref[slot, keys, :]
                row_dot = row_dot + jnp.sum(weighted.reshape(chunk // 8, 8, block), axis=0)
                score_ref[slot, keys, :] = probs
                prob_ref[slot, keys, :] = weighted
                put(gv_ref, keys, mm(probs.astype(BF), g_ref[h, at, :]))
            row_dot = jnp.sum(row_dot, axis=0, keepdims=True)
            grad_q = jnp.zeros((HD, block), F32)
            for start in range(0, length, chunk):
                keys = slice(start, start + chunk)
                grad_scores = (prob_ref[slot, keys, :] - score_ref[slot, keys, :] * row_dot).astype(BF)
                put(gk_ref, keys, mm(grad_scores, q_ref[h, at, :]))
                grad_q = grad_q + mm(kt_ref[h, :, keys], grad_scores)
            gqt_ref[pl.ds(pl.multiple_of(h * HD, HD), HD), at] = grad_q
        return carry

    lax.fori_loop(0, heads, one, 0)
    grads = jnp.concatenate(
        [gqt_ref[...].T] + [gk_ref[h] for h in range(heads)] + [gv_ref[h] for h in range(heads)], axis=1
    ).astype(BF)
    grad_o[...] = grads
    sums_o[...] = jnp.broadcast_to(jnp.sum(grads.astype(F32), axis=0, keepdims=True), sums_o.shape)
    back = mm_nt(grad_o[...], w_ref[...])
    keep_near_o[...] = back[0:rows]
    send_o[0:rows] = back[rows : 2 * rows].astype(BF)
    keep_chip_o[...] = back[2 * rows : 3 * rows]
    send_o[rows : 2 * rows] = back[3 * rows : 4 * rows].astype(BF)


def attend_back(seg, rows, parts, grads_in, log_total, weight, query_code):
    heads, length = parts[0].shape[:2]
    depth, width = weight.shape[0], heads * HD
    shape = jax.ShapeDtypeStruct
    fixed = lambda a: pl.BlockSpec(a.shape, lambda g, n=len(a.shape): (0,) * n)

    def piece(grads):
        if len(grads.shape) == 2:
            return pl.BlockSpec((rows, width), lambda g: (seg, 0))
        return pl.BlockSpec((1, rows, width), lambda g: (0, seg, 0))

    outs = (
        shape((length, 3 * width), BF),
        shape((rows, depth), F32),
        shape((rows, depth), F32),
        shape((2 * rows, depth), BF),
        shape((8, 3 * width), F32),
    )
    return pl.pallas_call(
        lambda *refs: attend_back_kernel(heads, *refs),
        grid=(1,),
        out_shape=outs,
        in_specs=[fixed(a) for a in parts] + [piece(a) for a in grads_in] + [fixed(a) for a in (log_total, weight)]
        + [pl.BlockSpec((1,) + query_code.shape[1:], lambda g: (seg, 0, 0))],
        out_specs=[fixed(o) for o in outs],
        scratch_shapes=[
            pltpu.VMEM((length, length), F32),
            pltpu.VMEM((heads, length, HD), BF),
            pltpu.VMEM((width, length), F32),
            pltpu.VMEM((heads, length, HD), F32),
            pltpu.VMEM((heads, length, HD), F32),
            pltpu.VMEM((2, length, 256), F32),
            pltpu.VMEM((2, length, 256), F32),
        ],
        cost_estimate=pl.CostEstimate(
            flops=2 * length * depth * 3 * width + 40 * length * length * width,
            bytes_accessed=12 << 20,
            transcendentals=heads * length * length,
        ),
        name="attend_back",
    )(*parts, *grads_in, log_total, weight, query_code)


def finish(seg, held, keep, near, far):
    rows, depth = keep.shape
    steps = 2
    part = rows // steps
    block = pl.BlockSpec((part, depth), lambda g: (seg * steps + g, 0))
    whole = pl.BlockSpec((part, depth), lambda g: (g, 0))

    def kernel(held_ref, keep_ref, near_ref, far_ref, out_ref):
        out_ref[...] = held_ref[...] + keep_ref[...] + near_ref[...].astype(F32) + far_ref[...].astype(F32)

    return pl.pallas_call(
        kernel,
        grid=(steps,),
        out_shape=jax.ShapeDtypeStruct(held.shape, F32),
        in_specs=[block, whole, whole, whole],
        out_specs=block,
        input_output_aliases={0: 0},
        cost_estimate=pl.CostEstimate(flops=1 << 20, bytes_accessed=4 << 20, transcendentals=0),
        name="finish",
    )(held, keep, near, far)


def fold(place, steps, terms, outs, turned=False):
    shape = jax.ShapeDtypeStruct
    columns = terms[0][0].shape[-1]

    def lead_of(term):
        return term[1][1:-2] if term[3] else term[1][:-2]

    count = math.prod(lead_of(terms[0]))
    total = max(row + block[-2] * (block[0] if stacked else 1) for _, block, _, stacked, row in terms)

    def spec(term):
        index = term[2]
        return pl.BlockSpec(term[1], lambda g, p: tuple(index(g, p)) + (0, 0))

    def kernel(place_ref, *refs):
        ins, out_refs = refs[: len(terms)], refs[len(terms) :]
        for number in range(count):
            pieces = {}

            def add(start, values):
                size = values.shape[0]
                inside = [k for k in pieces if start <= k[0] and sum(k) <= start + size]
                for k in inside:
                    pieces[k] = pieces[k] + values[k[0] - start : sum(k) - start]
                if not inside:
                    pieces[start, size] = values

            for ref, term in zip(ins, terms):
                rest, entry = number, []
                for n in reversed(lead_of(term)):
                    entry.insert(0, rest % n)
                    rest //= n
                if turned:
                    entry[0] = place_ref[0] ^ number
                _, block, _, stacked, row = term
                if stacked:
                    for i in range(block[0]):
                        add(row + i * block[-2], ref[(i, *entry)].astype(F32))
                else:
                    add(row, ref[tuple(entry)].astype(F32))
            out = out_refs[0].at[number] if len(outs) == 1 else out_refs[number]
            for (start, size), values in pieces.items():
                out[start : start + size, :] = values.astype(out.dtype)

    if len(outs) == 1:
        out_shape = [shape((steps * count, total, columns), outs[0])]
        out_specs = [pl.BlockSpec((count, total, columns), lambda g, p: (g, 0, 0))]
    else:
        out_shape = [shape((total, columns), kind) for kind in outs]
        out_specs = [pl.BlockSpec((total, columns), lambda g, p: (0, 0))] * len(outs)
    return pl.pallas_call(
        kernel,
        grid_spec=pltpu.PrefetchScalarGridSpec(
            num_scalar_prefetch=1, grid=(steps,), in_specs=[spec(t) for t in terms], out_specs=out_specs
        ),
        out_shape=out_shape,
        cost_estimate=pl.CostEstimate(flops=1 << 20, bytes_accessed=4 << 20, transcendentals=0),
        name="fold",
    )(place, *[t[0] for t in terms])


def own_columns(values, group, width):
    return lax.dynamic_slice_in_dim(values, group * width, width, axis=1)


def per_device(
    layer_input, doc_starts, mem_rows, w_query, b_query, w_key, w_value, b_value, w_out, b_out,
    attn_gain, attn_shift, w_up, b_up, w_down, b_down, ffn_gain, ffn_shift, grad_out,
):
    segs, rows, depth = layer_input.shape
    groups = lax.axis_size(SEQ)
    width, half = depth // groups, depth // 2
    ff = w_up.shape[1]
    length = rows * groups
    here, place = lax.axis_index(SEQ), lax.axis_index(FSDP)
    upper_core, upper_chip = bit_of(here, CORE), bit_of(here, CHIP)
    core, chip = upper_core.astype(jnp.int32), upper_chip.astype(jnp.int32)
    shard = w_query.shape[0]
    devices = lax.axis_size(FSDP)
    ratio = ff // depth
    direct = shard % 32 == 0

    over_core = hop(layer_input, SEQ, CORE)
    first, later = (hop(part, SEQ, CHIP) for part in (layer_input[:1], layer_input[1:]))
    first_both, later_both = (hop(part, SEQ, CORE) for part in (first, later))

    def rows_of(i):
        chip_rows, both, at = (first, first_both, 0) if i == 0 else (later, later_both, i - 1)
        return ((layer_input, i), (over_core, i), (chip_rows, at), (both, at))

    vectors = (b_query, b_value, b_out, attn_gain, attn_shift, b_down, ffn_gain, ffn_shift, b_up)
    spot = jnp.stack([here, core, chip]).astype(jnp.int32)
    if direct:
        own, up_part, rest_part = pack(spot, (w_query, w_key, w_value, w_out, w_up, w_down), vectors)
        qkv_pieces = gather_pieces(own)
        order = jnp.arange(devices, dtype=jnp.int32) ^ place

        def two_parts(block):
            pieces = {0: block}
            for shift, n in reversed(fsdp_digits()[1:]):
                for held in list(pieces):
                    for step in range(1, n):
                        pieces[held | step << shift] = hop(pieces[held], FSDP, step << shift)
            near = jnp.stack([pieces[j] for j in sorted(pieces)])
            return near, hop(near, FSDP, 1)

        rest = two_parts(rest_part)
        rest_far = [hop(part, SEQ, CHIP) for part in rest]
        quarter_ff = ff // 4
        up = two_parts(up_part[:, :quarter_ff]) + two_parts(up_part[:, quarter_ff:])
        middle_weights = (
            *up, *[hop(part, SEQ, CORE) for part in up],
            *rest, *rest_far,
            *[hop(part, SEQ, CORE) for part in rest],
            *[hop(part, SEQ, CORE) for part in rest_far],
        )
        up_bias = jnp.zeros((1, ff), F32)
        qkv_bias = jnp.zeros((1, 3 * width), F32)
    else:
        own = jnp.concatenate([own_columns(w, here, width) for w in (w_query, w_key, w_value)], axis=1)
        qkv_pieces = [lax.all_gather(own, FSDP, axis=0, tiled=True)]
        found = lax.all_gather(jnp.concatenate(vectors), FSDP, axis=0).astype(F32)
        order = jnp.zeros((1,), jnp.int32)
        out_whole, up_whole, down_whole = (
            lax.all_gather(w, FSDP, axis=0, tiled=True) for w in (w_out, w_up, w_down)
        )
        up_halves, down_halves = up_whole.reshape(depth, 2, ff // 2), down_whole.reshape(2, ff // 2, depth)
        middle_weights = (
            out_whole,
            jnp.where(upper_core, up_halves[:, ::-1], up_halves).reshape(depth, ff),
            jnp.where(upper_core, down_halves[::-1], down_halves).reshape(ff, depth),
        )
        names = len(vectors) - 1
        q_bias, v_bias, o_bias, gain_one, shift_one, down_bias, gain_two, shift_two = (
            found[:, i * shard : (i + 1) * shard].reshape(-1) for i in range(names)
        )
        up_bias = found[:, names * shard :].reshape(2, ff // 2)
        up_bias = jnp.where(upper_core, up_bias[::-1], up_bias).reshape(1, ff)
        vector_rows = jnp.stack([o_bias, gain_one, shift_one, down_bias, gain_two, shift_two, o_bias, o_bias])
        qkv_bias = jnp.concatenate(
            [
                lax.dynamic_slice_in_dim(q_bias, here * width, width),
                jnp.zeros((width,), F32),
                lax.dynamic_slice_in_dim(v_bias, here * width, width),
            ]
        )[None, :]
    piece_rows = shard if direct else devices * shard
    order = jnp.concatenate([order, spot])

    spots = jnp.arange(length, dtype=jnp.int32)
    positions = ((spots // rows) ^ here) * rows + spots % rows
    doc_ids = jnp.sum((doc_starts[:, :, None] <= positions[None, None, :]).astype(F32), axis=1)
    is_memory = jnp.any(mem_rows[:, :, None] == positions[None, None, :], axis=1)
    penalty = jnp.where(is_memory, 0.0, MASKED)
    query_code = jnp.stack([doc_ids, penalty] + [jnp.zeros_like(doc_ids)] * 6, axis=1)

    done = []
    for i in range(segs):
        done.append(attend(i, order, rows_of(i), qkv_pieces, piece_rows, qkv_bias, query_code))

    contexts = []
    for i in range(segs):
        near, to_core, to_chip = done[i][6:9]
        from_core = hop(to_core, SEQ, CORE)
        from_chip = hop(to_chip, SEQ, CHIP)
        contexts.append((near, from_core, from_chip, hop(from_chip[rows:], SEQ, CORE)))

    (
        layer_out, context_t, low_t, active_t, gb, gh, ga, grad_sum_one, g0, g1, g2, g3, vector_sums,
    ) = middle(
        order, middle_weights, shard, direct, contexts, layer_input.reshape(segs * rows, depth),
        grad_out.reshape(segs * rows, depth), done[0][10] if direct else vector_rows, up_bias,
    )
    heads_grads = (g0, hop(g1, SEQ, CORE), hop(g2, SEQ, CHIP), hop(hop(g3, SEQ, CORE), SEQ, CHIP))

    digits = fsdp_digits()
    place_digits = [(FSDP, shift, n, place) for shift, n in digits]

    second_keep, second_send = second_grads(active_t, gb)
    second_got = hop(second_send, SEQ, CORE)
    first_keep, first_send = first_grads(context_t, low_t, ga, gh)
    first_got = hop(first_send, SEQ, CORE)
    vector_sums = vector_sums + hop(vector_sums, SEQ, CORE)

    rest_count = devices // 2
    part_rows = shard // 2
    at_place = jnp.stack([place >> 1, place & 1, chip]).astype(jnp.int32)

    def by_block(values, size):
        return values.reshape(values.shape[:-2] + (rest_count, 2, 2, size, half))

    first = [by_block(v, part_rows) for v in (first_keep, first_got)]
    second = [by_block(v, part_rows * ratio) for v in (second_keep, second_got)]
    vector_blocks = by_block(vector_sums.reshape(-1, half), 8)
    below_first = (ratio + 1) * part_rows
    chunk = max(rest_count // 2, 1)

    def first_terms(size, block, index):
        return [
            (v, (ratio + 1, size) + block + (part_rows, half), lambda g, p: (0, g) + index(p), True, 0) for v in first
        ]

    def second_terms(size, block, index, row=0):
        at = lambda g, p: (g,) + index(p)
        terms = [(v, (size,) + block + (part_rows * ratio, half), at, False, row) for v in second]
        return terms + [(vector_blocks, (size,) + block + (8, half), at, False, row + part_rows * ratio)]

    def got_terms(got, many, index, row=0):
        if not many:
            return [(got, (rest_count,) + got.shape[1:], lambda g, p: (0,), False, row)]
        got = got.reshape((rest_count, 2) + got.shape[1:])
        return [(got, (rest_count, 1) + got.shape[2:], lambda g, p: (0, index(p)), False, row)]

    send_b = fold(at_place, rest_count // chunk, second_terms(chunk, (2, 1), lambda p: (0, 1 - p[2])), (BF,))[0]
    got_b0 = hop(send_b, SEQ, CHIP)
    send_a = fold(at_place, rest_count // chunk, first_terms(chunk, (1, 2), lambda p: (1 - p[1], 0)), (BF,))[0]
    got_a0 = hop(send_a, FSDP, 1)
    send_b = fold(
        at_place, 1,
        second_terms(rest_count, (1, 1), lambda p: (1 - p[1], p[2])) + got_terms(got_b0, True, lambda p: 1 - p[1]),
        (BF,),
    )[0]
    got_b1 = hop(send_b, FSDP, 1)
    send_a = fold(
        at_place, 1,
        first_terms(rest_count, (1, 1), lambda p: (p[1], 1 - p[2])) + got_terms(got_a0, True, lambda p: 1 - p[2]),
        (BF,),
    )[0]
    got_a1 = hop(send_a, SEQ, CHIP)

    backs = []
    for i in range(segs):
        backs.append(
            attend_back(i, rows, done[i][:4], heads_grads, done[i][9], done[0][5], query_code)
        )

    last_terms = (
        first_terms(rest_count, (1, 1), lambda p: (p[1], p[2]))
        + got_terms(got_a0, True, lambda p: p[2]) + got_terms(got_a1, False, None)
        + second_terms(rest_count, (1, 1), lambda p: (p[1], p[2]), below_first)
        + got_terms(got_b0, True, lambda p: p[1], below_first) + got_terms(got_b1, False, None, below_first)
    )
    if len(digits) == 2:
        shift, n = digits[1]
        kinds = (F32,) + (BF,) * (n - 1)
        mine, *sends = fold(at_place, 1, last_terms, kinds, turned=True)
        for k, send in enumerate(sends, 1):
            mine = mine + hop(send, FSDP, k << shift).astype(F32)
    else:
        merged = fold(at_place, 1, last_terms, (F32,))[0]
        lead = tuple(n for _, n in reversed(digits[1:]))
        mine = halve(merged.reshape(lead + merged.shape[1:]), place_digits[1:])
    mine = mine.astype(BF)
    other = hop(mine, SEQ, CHIP)
    far = [hop(part, SEQ, CORE) for part in (mine, other)]

    def quarter(values):
        blocks = values[: (ratio + 1) * part_rows].reshape(ratio + 1, part_rows, half)
        return (
            blocks[ratio],
            jnp.concatenate([blocks[i] for i in range(ratio)], axis=1),
            values[(ratio + 1) * part_rows :],
        )

    corners = [quarter(values[:-8]) for values in (mine, other, *far)]
    vector_rows = jnp.where(upper_chip, other[-8:], mine[-8:]).astype(F32)
    per = half // shard

    def vector_of(i):
        return vector_rows[i // per, i % per * shard : (i % per + 1) * shard]


    def assembled(i):
        near = joined(corners[0][i], corners[1][i], upper_chip, 0)
        return joined(near, joined(corners[2][i], corners[3][i], upper_chip, 0), upper_core, 1).astype(F32)

    grad_w_out, grad_w_up, grad_w_down = (assembled(i) for i in range(3))

    grad_input = grad_sum_one
    for i in range(segs):
        _, keep_near, keep_chip, send, _ = backs[i]
        near = hop(send, SEQ, CORE)
        far = (keep_chip + near[rows:].astype(F32)).astype(BF)
        grad_input = finish(i, grad_input, keep_near, near, hop(far, SEQ, CHIP))

    grad_qkv = sum(mm(done[i][4], backs[i][0]) for i in range(segs - 1))
    grad_qkv = grad_qkv + mm(done[-1][4], backs[-1][0])
    grad_qkv = grad_qkv.reshape(tuple(n for _, n in reversed(digits)) + (shard, 3 * width))
    bias_rows = sum(backs[i][4] for i in range(segs))
    mine = halve(grad_qkv, place_digits, bias_rows).astype(BF)
    other = hop(mine, SEQ, CORE)
    far_mine = hop(mine, SEQ, CHIP)
    far_other = hop(other, SEQ, CHIP)
    parts = swapped([mine, other, far_mine, far_other], upper_core, upper_chip)

    def columns_of(i):
        return jnp.concatenate([p[:, i * width : (i + 1) * width] for p in parts], axis=1).astype(F32)

    def own_part(vector):
        count = vector.shape[0] * shard // depth
        return lax.dynamic_slice_in_dim(vector, place * count, count)

    grad_q, grad_k, grad_v = (columns_of(i) for i in range(3))
    return (
        layer_out.reshape(layer_input.shape),
        grad_input.reshape(layer_input.shape),
        grad_q[:shard],
        own_part(grad_q[shard]),
        grad_k[:shard],
        grad_v[:shard],
        own_part(grad_v[shard]),
        grad_w_out,
        vector_of(0),
        vector_of(1),
        vector_of(2),
        grad_w_up,
        jnp.concatenate([vector_of(6 + r) for r in range(ratio)]),
        grad_w_down,
        vector_of(3),
        vector_of(4),
        vector_of(5),
    )


def solution(mesh):
    rows, cols = P(FSDP, SEQ, None), P(FSDP, None)
    vec = P(FSDP)
    return jax.shard_map(
        per_device,
        mesh=mesh,
        in_specs=(
            rows, cols, cols, cols, vec, cols, cols, vec, cols, vec,
            vec, vec, cols, vec, cols, vec, vec, vec, rows,
        ),
        out_specs=(
            rows, rows, cols, vec, cols, cols, vec, cols, vec,
            vec, vec, cols, vec, cols, vec, vec, vec,
        ),
        check_vma=False,
    )
```

```python
import math

import jax
import jax.numpy as jnp
from jax import lax
from jax.experimental import pallas as pl
from jax.experimental.pallas import tpu as pltpu
from jax.sharding import PartitionSpec as P


HD = 64
LN_EPS = 1e-12
MASKED = -1e30
BF = jnp.bfloat16
F32 = jnp.float32


CORE, CHIP = 1, 2


SEQ, FSDP = "seq", "fsdp"


def hop(values, axis, bit):
    size = lax.axis_size(axis)
    return lax.ppermute(values, axis, [(i, i ^ bit) for i in range(size)])


def bit_of(index, bit):
    return (index & bit) != 0


def joined(mine, other, upper, axis):
    low = jnp.where(upper, other, mine)
    high = jnp.where(upper, mine, other)
    return jnp.concatenate([low, high], axis=axis)


def fsdp_digits():
    bits = lax.axis_size(FSDP).bit_length() - 1
    digits, at = [], 0
    while at < bits:
        take = 1 if at == 0 else min(2, bits - at)
        digits.append((at, 1 << take))
        at += take
    return digits


def gather_pieces(block):
    pieces = {0: block}
    for shift, size in reversed(fsdp_digits()):
        for held in list(pieces):
            for step in range(1, size):
                entry = held | step << shift
                pieces[entry] = hop(pieces[held], FSDP, step << shift)
    return [pieces[j] for j in range(len(pieces))]


def entry_at(values, indices):
    for index in indices:
        values = lax.dynamic_index_in_dim(values, index, values.ndim - 3, keepdims=False)
    return values


def halve(held, steps, beside=()):
    arrived, kept = [(0, list(beside))], []

    def total(last):
        values = entry_at(held, kept + last).astype(F32)
        for at, group in arrived:
            for got in group:
                values = values + entry_at(got, kept[at:] + last).astype(F32)
        return values

    for axis, shift, size, place in steps:
        digit = (place >> shift) & (size - 1)
        group = [hop(total([digit ^ step]).astype(BF), axis, step << shift) for step in range(1, size)]
        kept.append(digit)
        arrived.append((len(kept), group))
    return total([])


def mm(left, right):
    return lax.dot_general(left, right, (((1,), (0,)), ((), ())), preferred_element_type=F32)


def mm_nt(left, right):
    return lax.dot_general(left, right, (((1,), (1,)), ((), ())), preferred_element_type=F32)


def hidden_pairs(query_code, key_code, bias_ref, start, stop):
    step = 128
    for at in range(start, stop, step):
        part = key_code[at : at + step, :]
        same = part[:, 0:1] == query_code[0:1, :]
        bias_ref[at : at + step, :] = jnp.where(same, 0.0, jnp.maximum(part[:, 1:2], query_code[1:2, :]))


def erf_parts(values):
    cdf = 0.5 * (1.0 + lax.erf(values * (1.0 / math.sqrt(2.0))))
    return cdf, jnp.exp(-0.5 * values * values) * (1.0 / math.sqrt(2.0 * math.pi))


def place_rows(pieces, order_ref, rows, target):
    for j, piece in enumerate(pieces):
        at = pl.multiple_of(order_ref[j] * rows, rows)
        target[pl.ds(at, rows), :] = piece[0:rows, :]


def attend_kernel(heads, shard, count, order_ref, x0, x1, x2, x3, *refs):
    pieces, refs = refs[:count], refs[count:]
    b_ref, qc_ref, q_ref, k_ref, kt_ref, v_ref, xrel_o, w_o, near_o, core_o, chip_o, log_o, vec_o = refs[:13]
    bias_ref, vt_ref, ctx_ref, score_ref = refs[13:]
    width = heads * HD
    rows = x0.shape[1]
    length = 4 * rows
    place_rows(pieces, order_ref, shard, w_o)
    added = b_ref[...]
    if count > 1:
        for j, piece in enumerate(pieces):
            vec_o[order_ref[j]] = piece[shard:, 0:128].astype(F32)
        here = order_ref[count]
        near, far = vec_o[2 * here], vec_o[2 * here + 1]
        added = jnp.concatenate(
            [near[0:1, 0:shard], far[0:1, 0:shard], jnp.zeros((1, width), F32), near[1:2, 0:shard], far[1:2, 0:shard]],
            axis=1,
        )
    factor = BF(1.0 / math.sqrt(HD))
    query_code = qc_ref[0]
    key_code = query_code.T
    for j, piece in enumerate((x0, x1, x2, x3)):
        part = slice(j * rows, (j + 1) * rows)
        xrel_o[:, part] = piece[0].T
        made = (mm(piece[0], w_o[...]) + added).astype(BF)
        hidden_pairs(query_code, key_code, bias_ref, j * rows, (j + 1) * rows)
        turned = made.T
        for h in range(heads):
            at = h * HD
            q_ref[h, part, :] = made[:, at : at + HD] * factor
            k_ref[h, part, :] = made[:, width + at : width + at + HD]
            kt_ref[h, :, part] = turned[width + at : width + at + HD] * factor
            v_ref[h, part, :] = made[:, 2 * width + at : 2 * width + at + HD]
            vt_ref[h, :, part] = turned[2 * width + at : 2 * width + at + HD]
    block, chunk = 256, 256
    blocks = length // block

    def score(h, at, slot):
        top = None
        for start in range(0, length, chunk):
            keys = slice(start, start + chunk)
            scores = mm_nt(k_ref[h, keys, :], q_ref[h, at, :]) + bias_ref[keys, at]
            score_ref[slot, keys, :] = scores
            largest = jnp.max(scores.reshape(chunk // 8, 8, block), axis=0)
            top = largest if top is None else jnp.maximum(top, largest)
        return jnp.max(top, axis=0, keepdims=True)

    def one(h, top):
        for b in range(blocks):
            at = slice(b * block, (b + 1) * block)
            if b + 1 < blocks:
                following = score(h, slice((b + 1) * block, (b + 2) * block), (b + 1) % 2)
            else:
                following = score(jnp.minimum(h + 1, heads - 1), slice(0, block), 0)
            total, made = jnp.zeros((8, block), F32), jnp.zeros((HD, block), F32)
            for start in range(0, length, chunk):
                keys = slice(start, start + chunk)
                shifted = jnp.exp(score_ref[b % 2, keys, :] - top)
                total = total + jnp.sum(shifted.reshape(chunk // 8, 8, block), axis=0)
                made = made + mm(vt_ref[h, :, keys], shifted.astype(BF))
            total = jnp.sum(total, axis=0, keepdims=True)
            ctx_ref[pl.ds(pl.multiple_of(h * HD, HD), HD), at] = made / total
            log_o[pl.ds(h, 1), at] = top + jnp.log(total)
            top = following
        return top

    lax.fori_loop(0, heads, one, score(0, slice(0, block), 0))
    near_o[...] = ctx_ref[:, 0:rows].T.astype(BF)
    core_o[...] = ctx_ref[:, rows : 2 * rows].T.astype(BF)
    chip_o[...] = ctx_ref[:, 2 * rows : 4 * rows].T.astype(BF)


def attend(seg, order, pieces, weights, shard, bias, query_code):
    (first, _), width = pieces[0], bias.shape[1] // 3
    rows, depth = first.shape[1:]
    length, heads = 4 * rows, width // HD
    shape = jax.ShapeDtypeStruct
    vmem = pl.BlockSpec(memory_space=pltpu.VMEM)

    def rows_of(at):
        return pl.BlockSpec((1, rows, depth), lambda g, at=at: (at, 0, 0))

    count = len(weights)
    whole = lambda a: pl.BlockSpec(a.shape, lambda g, n=len(a.shape): (0,) * n)
    outs = (
        shape((heads, length, HD), BF),
        shape((heads, length, HD), BF),
        shape((heads, HD, length), BF),
        shape((heads, length, HD), BF),
        shape((depth, length), BF),
        shape((depth, 3 * width), BF),
        shape((rows, width), BF),
        shape((rows, width), BF),
        shape((2 * rows, width), BF),
        shape((8, length), F32),
        shape((count, max(weights[0].shape[0] - shard, 8), 128), F32),
    )
    return pl.pallas_call(
        lambda *refs: attend_kernel(heads, shard, count, *refs),
        grid=(1,),
        out_shape=outs,
        in_specs=[pl.BlockSpec(memory_space=pltpu.SMEM)]
        + [rows_of(at) for _, at in pieces]
        + [whole(w) for w in weights]
        + [whole(bias), pl.BlockSpec((1,) + query_code.shape[1:], lambda g: (seg, 0, 0))],
        out_specs=[whole(o) for o in outs],
        scratch_shapes=[
            pltpu.VMEM((length, length), F32),
            pltpu.VMEM((heads, HD, length), BF),
            pltpu.VMEM((width, length), F32),
            pltpu.VMEM((2, length, 256), F32),
        ],
        cost_estimate=pl.CostEstimate(
            flops=2 * length * depth * 3 * width + 16 * length * length * width,
            bytes_accessed=12 << 20,
            transcendentals=heads * length * length,
        ),
        name="attend",
    )(order, *[p for p, _ in pieces], *weights, bias, query_code)


def pack_kernel(place_ref, wq, wk, wv, wo, wu, wd, *refs):
    vectors, (own_o, up_o, rest_o) = refs[:-3], refs[-3:]
    here, core, chip = place_ref[0], place_ref[1], place_ref[2]
    shard, depth = wq.shape
    width, half, rows = depth // 4, depth // 2, shard // 2
    for i, ref in enumerate((wq, wk, wv)):
        picked = ref[:, 0:width]
        for j in range(1, 4):
            picked = jnp.where(here == j, ref[:, j * width : (j + 1) * width], picked)
        own_o[0:shard, i * width : (i + 1) * width] = picked
    below = [ref[0:1, at : at + shard] for ref in vectors for at in range(0, ref.shape[1], shard)]
    below.append(jnp.zeros((own_o.shape[0] - shard - len(below), shard), BF))
    own_o[shard:, :] = jnp.zeros((own_o.shape[0] - shard, 3 * width), BF)
    own_o[shard:, 0:shard] = jnp.concatenate([b.astype(F32) for b in below], axis=0).astype(BF)
    ff_half = wu.shape[1] // 2
    up_o[...] = wu[:, pl.ds(pl.multiple_of(core * ff_half, ff_half), ff_half)]
    columns = pl.ds(pl.multiple_of(core * half, half), half)
    at = pl.multiple_of(chip * rows, rows)
    rest_o[:, 0:half] = wo[pl.ds(at, rows), columns]
    for i in range(wd.shape[0] // shard):
        rest_o[:, (i + 1) * half : (i + 2) * half] = wd[pl.ds(i * shard + at, rows), columns]


def pack(place, weights, vectors):
    shard, depth = weights[0].shape
    ff, ratio = weights[4].shape[1], weights[5].shape[0] // shard
    shape = jax.ShapeDtypeStruct
    vmem = pl.BlockSpec(memory_space=pltpu.VMEM)
    return pl.pallas_call(
        pack_kernel,
        out_shape=(
            shape((shard + 16, 3 * depth // 4), BF),
            shape((shard, ff // 2), BF),
            shape((shard // 2, (1 + ratio) * depth // 2), BF),
        ),
        in_specs=[pl.BlockSpec(memory_space=pltpu.SMEM)] + [vmem] * (6 + len(vectors)),
        out_specs=[vmem] * 3,
        cost_estimate=pl.CostEstimate(flops=1 << 16, bytes_accessed=4 << 20, transcendentals=0),
        name="pack",
    )(place, *weights, *[v[None, :] for v in vectors])


def norm_stats(values):
    centre = values - jnp.mean(values, axis=-1, keepdims=True)
    inv_dev = lax.rsqrt(jnp.mean(centre * centre, axis=-1, keepdims=True) + LN_EPS)
    return centre * inv_dev, inv_dev


def norm_back(grads, unit, inv_dev, gain):
    scaled = grads * gain
    return inv_dev * (
        scaled
        - jnp.mean(scaled, axis=-1, keepdims=True)
        - unit * jnp.mean(scaled * unit, axis=-1, keepdims=True)
    )


def swapped(parts, upper_core, upper_chip):
    a, b, c, d = parts
    a, b, c, d = (jnp.where(upper_core, y, x) for x, y in ((a, b), (b, a), (c, d), (d, c)))
    return [jnp.where(upper_chip, y, x) for x, y in ((a, c), (b, d), (c, a), (d, b))]


def middle_kernel(segs, shard_rows, direct, order_ref, *refs):
    weights_in, refs = (refs[:16], refs[16:]) if direct else (refs[:3], refs[3:])
    context_in, refs = refs[: 4 * segs], refs[4 * segs :]
    x_ref, go_ref, vec_ref, up_ref = refs[:4]
    (
        out_o, ctx_o, low_o, act_o, gb_o, gh_o, ga_o, gsum_o, g0_o, g1_o, g2_o, g3_o, vec_o,
    ) = refs[4:17]
    wo, wu, wd, slope_ref, half_ref, vec_s, up_s, sums_o, up_sums_o, sems = refs[17:]
    seg = pl.program_id(0)
    depth, ff = wu.shape
    rows, half, ff_half = x_ref.shape[0], depth // 2, ff // 2
    _, core, chip = (order_ref[order_ref.shape[0] - 3 + i] for i in range(3))
    upper_core, upper_chip = core != 0, chip != 0

    def copies():
        if not direct:
            return [[(a, b)] for a, b in zip(weights_in, (wo, wu, wd))]
        found = [[], [], []]
        near, shard = weights_in[0].shape[:2]
        part, ratio = shard // 2, ff // depth
        for side in range(2):
            column = pl.multiple_of((core ^ side) * half, half)
            for low in range(2):
                for j in range(near):
                    block = order_ref[2 * j + low]
                    at = pl.multiple_of(block * shard, shard)
                    for i in range(2):
                        start = side * ff_half + i * ff_half // 2
                        found[1].append(
                            (weights_in[4 * side + 2 * i + low].at[j],
                             wu.at[pl.ds(at, shard), pl.ds(start, ff_half // 2)])
                        )
                    for other in range(2):
                        piece = weights_in[8 + 4 * side + 2 * other + low]
                        inner = (chip ^ other) * part
                        found[0].append(
                            (piece.at[j, :, 0:half],
                             wo.at[pl.ds(pl.multiple_of(at + inner, part), part), pl.ds(column, half)])
                        )
                        for i in range(ratio):
                            row = (block * ratio + i) * shard
                            turned = jnp.where(row < ff_half, row + core * ff_half, row - core * ff_half)
                            turned = pl.multiple_of(turned + inner, part)
                            found[2].append(
                                (piece.at[j, :, (i + 1) * half : (i + 2) * half],
                                 wd.at[pl.ds(turned, part), pl.ds(column, half)])
                            )
        return found

    groups, used = [], 0
    for found in copies():
        groups.append([pltpu.make_async_copy(a, b, sems.at[used + i]) for i, (a, b) in enumerate(found)])
        used += len(found)

    @pl.when(seg == 0)
    def _():
        for group in groups:
            for one in group:
                one.start()
        if direct:
            count, shard = vec_ref.shape[0], weights_in[0].shape[1]
            for i in range(6):
                vec_s[i : i + 1, :] = jnp.concatenate(
                    [vec_ref[j, i + 2 : i + 3, 0:shard] for j in range(count)], axis=1
                )
            halves = [
                jnp.concatenate(
                    [
                        vec_ref[j, 8 + r : 9 + r, 0:shard]
                        for j in range(side * count // 2, (side + 1) * count // 2)
                        for r in range(ff // depth)
                    ],
                    axis=1,
                )
                for side in range(2)
            ]
            up_s[:, 0:ff_half] = jnp.where(upper_core, halves[1], halves[0])
            up_s[:, ff_half:] = jnp.where(upper_core, halves[0], halves[1])
        else:
            vec_s[...] = vec_ref[...]
            up_s[...] = up_ref[...]
        sums_o[...] = jnp.zeros_like(sums_o)
        up_sums_o[...] = jnp.zeros_like(up_sums_o)

    def ready(which):
        @pl.when(seg == 0)
        def _():
            for one in groups[which]:
                one.wait()

    def vector(i):
        return vec_s[i : i + 1, :]

    ready(0)
    parts = []
    for j in range(4):
        picked = context_in[j][...]
        for i in range(1, segs):
            picked = jnp.where(seg == i, context_in[4 * i + j][...], picked)
        parts.append(picked)
    context = jnp.concatenate(swapped(parts, upper_core, upper_chip), axis=1)
    ctx_o[...] = context.T
    summed = x_ref[...].astype(F32) + mm(context, wo[...]) + vector(0)
    unit_one, inv_one = norm_stats(summed)
    normed_one = unit_one * vector(1) + vector(2)
    low = normed_one.astype(BF)
    low_o[...] = low.T
    ready(1)
    ready(2)
    step = depth if ff_half % depth == 0 else ff_half
    branch = jnp.zeros((rows, depth), F32)
    for start in range(0, ff, step):
        part = slice(start, start + step)
        hidden = mm(low, wu[:, part]) + up_s[:, part]
        cdf, density = erf_parts(hidden)
        active = (hidden * cdf).astype(BF)
        slope_ref[:, part] = cdf + hidden * density
        side = 0 if start < ff_half else 1
        target = pl.multiple_of((core ^ side) * ff_half, ff_half) + (start - side * ff_half)
        act_o[pl.ds(pl.multiple_of(target, 128), step), :] = active.T
        branch = branch + mm(active, wd[part, :])
    unit_two, inv_two = norm_stats(normed_one + (branch + vector(3)))
    out_o[...] = (unit_two * vector(4) + vector(5)).astype(BF)

    def add_sum(i, values):
        sums_o[i : i + 1, :] += jnp.sum(values, axis=0, keepdims=True)

    def halves(values, out):
        half_ref[...] = values
        out[:, 0:half] = half_ref[:, pl.ds(pl.multiple_of(core * half, half), half)].astype(BF)
        out[:, half:] = half_ref[:, pl.ds(pl.multiple_of((1 - core) * half, half), half)].astype(BF)

    grads = go_ref[...].astype(F32)
    add_sum(4, grads * unit_two)
    add_sum(5, grads)
    grad_two = norm_back(grads, unit_two, inv_two, vector(4))
    grad_branch = grad_two.astype(BF)
    add_sum(3, grad_branch.astype(F32))
    halves(grad_branch.astype(F32), gb_o)
    grad_normed = grad_two
    for start in range(0, ff, step):
        part = slice(start, start + step)
        grad_hidden = (mm_nt(grad_branch, wd[part, :]) * slope_ref[:, part]).astype(BF)
        side, first = start // ff_half, start % ff_half
        for at in range(0, step, half):
            target = 2 * (first + at) + side * half
            gh_o[:, target : target + half] = grad_hidden[:, at : at + half]
        up_sums_o[:, part] += jnp.sum(grad_hidden.astype(F32), axis=0, keepdims=True)
        grad_normed = grad_normed + mm_nt(grad_hidden, wu[:, part])
    add_sum(1, grad_normed * unit_one)
    add_sum(2, grad_normed)
    grad_one = norm_back(grad_normed, unit_one, inv_one, vector(1))
    gsum_o[...] = grad_one
    grad_attn = grad_one.astype(BF)
    add_sum(0, grad_attn.astype(F32))
    halves(grad_attn.astype(F32), ga_o)
    grad_context = mm_nt(grad_attn, wo[...]).astype(BF)
    width = depth // 4
    turned = swapped([grad_context[:, j * width : (j + 1) * width] for j in range(4)], upper_core, upper_chip)
    g0_o[...] = turned[0]
    g1_o[...] = turned[1]
    g2_o[...] = turned[2]
    g3_o[...] = turned[3]

    @pl.when(seg == segs - 1)
    def _():
        low_half, high_half = up_sums_o[:, 0:ff_half], up_sums_o[:, ff_half:]
        ordered = jnp.concatenate(
            [jnp.where(upper_core, high_half, low_half), jnp.where(upper_core, low_half, high_half)], axis=1
        )
        vec_o[...] = jnp.zeros_like(vec_o)
        ratio, per = ff // depth, half // shard_rows
        for f in range(depth // shard_rows):
            own = slice(f * shard_rows, (f + 1) * shard_rows)
            parts = [sums_o[i : i + 1, own] for i in range(6)] + [
                ordered[:, (f * ratio + r) * shard_rows : (f * ratio + r + 1) * shard_rows] for r in range(ratio)
            ]
            for row in range(0, len(parts), per):
                line = jnp.concatenate(parts[row : row + per], axis=1)
                vec_o[2 * f, row // per : row // per + 1, 0 : line.shape[1]] = line


def middle(order, weights, shard, direct, contexts, rows_in, grad_out, vectors, up_bias):
    tokens, depth = rows_in.shape
    ff, segs = up_bias.shape[1], len(contexts)
    rows, width, half = tokens // segs, depth // 4, depth // 2
    shape = jax.ShapeDtypeStruct
    fixed = lambda a: pl.BlockSpec(a.shape, lambda g, n=len(a.shape): (0,) * n)
    moving = lambda columns: pl.BlockSpec((rows, columns), lambda g: (g, 0))
    turned = lambda units: pl.BlockSpec((units, rows), lambda g: (0, g))
    outs = [
        (shape((tokens, depth), BF), moving(depth)),
        (shape((depth, tokens), BF), turned(depth)),
        (shape((depth, tokens), BF), turned(depth)),
        (shape((ff, tokens), BF), turned(ff)),
    ]
    for columns, kind in [(depth, BF), (ff, BF), (depth, BF), (depth, F32), (width, BF), (width, BF),
                          (width, BF), (width, BF)]:
        outs.append((shape((tokens, columns), kind), moving(columns)))
    last = shape((2 * depth // shard, 8, half), F32)
    outs.append((last, fixed(last)))
    piece = pl.BlockSpec((rows, width), lambda g: (0, 0))
    flat = [one for four in contexts for one in four]
    if direct:
        copies = 2 * (2 * weights[0].shape[0]) * (2 + 2 * (1 + ff // depth))
    else:
        copies = 3
    return pl.pallas_call(
        lambda *refs: middle_kernel(segs, shard, direct, *refs),
        grid=(segs,),
        out_shape=tuple(o for o, _ in outs),
        in_specs=[pl.BlockSpec(memory_space=pltpu.SMEM)]
        + [pl.BlockSpec(memory_space=pl.ANY)] * len(weights)
        + [piece] * len(flat)
        + [moving(depth), moving(depth), fixed(vectors), fixed(up_bias)],
        out_specs=[b for _, b in outs],
        scratch_shapes=[
            pltpu.VMEM((depth, depth), BF),
            pltpu.VMEM((depth, ff), BF),
            pltpu.VMEM((ff, depth), BF),
            pltpu.VMEM((rows, ff), F32),
            pltpu.VMEM((rows, depth), F32),
            pltpu.VMEM((8, depth), F32),
            pltpu.VMEM((1, ff), F32),
            pltpu.VMEM((8, depth), F32),
            pltpu.VMEM((1, ff), F32),
            pltpu.SemaphoreType.DMA((copies,)),
        ],
        cost_estimate=pl.CostEstimate(
            flops=4 * tokens * depth * (depth + 2 * ff), bytes_accessed=40 << 20,
            transcendentals=2 * tokens * ff,
        ),
        name="middle",
    )(order, *weights, *flat, rows_in, grad_out, vectors, up_bias)


def first_grads(context_t, low_t, ga, gh):
    depth, tokens = low_t.shape
    half, ratio = depth // 2, gh.shape[1] // depth
    shape = jax.ShapeDtypeStruct

    def kernel(ctx_ref, low_ref, ga_ref, gh_ref, keep_o, send_o):
        step = pl.program_id(0)

        def put(left, right):
            made = mm(left, right)
            keep_o[0] = made[:, 0:half].astype(BF)
            send_o[0] = made[:, half:].astype(BF)

        @pl.when(step < ratio)
        def _():
            put(low_ref[...], gh_ref[...])

        @pl.when(step == ratio)
        def _():
            put(ctx_ref[...], ga_ref[...])

    whole = lambda a: pl.BlockSpec(a.shape, lambda g: (0, 0))
    out = pl.BlockSpec((1, depth, half), lambda g: (g, 0, 0))
    return pl.pallas_call(
        kernel,
        grid=(ratio + 1,),
        out_shape=(shape((ratio + 1, depth, half), BF),) * 2,
        in_specs=[
            whole(context_t), whole(low_t), whole(ga),
            pl.BlockSpec((tokens, depth), lambda g: (0, jnp.minimum(g, ratio - 1))),
        ],
        out_specs=(out, out),
        cost_estimate=pl.CostEstimate(
            flops=2 * tokens * depth * depth * (ratio + 1), bytes_accessed=16 << 20, transcendentals=0
        ),
        name="first_grads",
    )(context_t, low_t, ga, gh)


def second_grads(active_t, gb):
    ff, tokens = active_t.shape
    depth = gb.shape[1]
    half = depth // 2
    shape = jax.ShapeDtypeStruct

    def kernel(act_ref, gb_ref, keep_o, send_o):
        made = mm(act_ref[...], gb_ref[...])
        keep_o[...] = made[:, 0:half].astype(BF)
        send_o[...] = made[:, half:].astype(BF)

    out = pl.BlockSpec((depth, half), lambda g: (g, 0))
    return pl.pallas_call(
        kernel,
        grid=(ff // depth,),
        out_shape=(shape((ff, half), BF),) * 2,
        in_specs=[pl.BlockSpec((depth, tokens), lambda g: (g, 0)), pl.BlockSpec(gb.shape, lambda g: (0, 0))],
        out_specs=(out, out),
        cost_estimate=pl.CostEstimate(flops=2 * tokens * depth * ff, bytes_accessed=14 << 20, transcendentals=0),
        name="second_grads",
    )(active_t, gb)


def attend_back_kernel(
    heads, q_ref, k_ref, kt_ref, v_ref, g0, g1, g2, g3, log_ref, w_ref, qc_ref,
    grad_o, keep_near_o, keep_chip_o, send_o, sums_o,
    bias_ref, g_ref, gqt_ref, gk_ref, gv_ref, score_ref, prob_ref,
):
    length = grad_o.shape[0]
    rows = length // 4
    for h in range(heads):
        at = h * HD
        for j, piece in enumerate((g0, g1, g2, g3)):
            g_ref[h, j * rows : (j + 1) * rows, :] = piece[:, at : at + HD]
    query_code = qc_ref[0]
    hidden_pairs(query_code, query_code.T, bias_ref, 0, length)
    block, chunk = 256, 256
    blocks = length // block

    def score(h, at, slot):
        log_total = log_ref[pl.ds(h, 1), at]
        for start in range(0, length, chunk):
            keys = slice(start, start + chunk)
            score_ref[slot, keys, :] = mm_nt(k_ref[h, keys, :], q_ref[h, at, :]) + (bias_ref[keys, at] - log_total)
            prob_ref[slot, keys, :] = mm_nt(v_ref[h, keys, :], g_ref[h, at, :])

    score(0, slice(0, block), 0)

    def one(h, carry):
        for b in range(blocks):
            at, slot = slice(b * block, (b + 1) * block), b % 2
            if b + 1 < blocks:
                score(h, slice((b + 1) * block, (b + 2) * block), 1 - slot)
            else:
                score(jnp.minimum(h + 1, heads - 1), slice(0, block), 1 - slot)

            def put(ref, keys, values):
                ref[h, keys, :] = values if b == 0 else ref[h, keys, :] + values

            row_dot = jnp.zeros((8, block), F32)
            for start in range(0, length, chunk):
                keys = slice(start, start + chunk)
                probs = jnp.exp(score_ref[slot, keys, :])
                weighted = probs * prob_ref[slot, keys, :]
                row_dot = row_dot + jnp.sum(weighted.reshape(chunk // 8, 8, block), axis=0)
                score_ref[slot, keys, :] = probs
                prob_ref[slot, keys, :] = weighted
                put(gv_ref, keys, mm(probs.astype(BF), g_ref[h, at, :]))
            row_dot = jnp.sum(row_dot, axis=0, keepdims=True)
            grad_q = jnp.zeros((HD, block), F32)
            for start in range(0, length, chunk):
                keys = slice(start, start + chunk)
                grad_scores = (prob_ref[slot, keys, :] - score_ref[slot, keys, :] * row_dot).astype(BF)
                put(gk_ref, keys, mm(grad_scores, q_ref[h, at, :]))
                grad_q = grad_q + mm(kt_ref[h, :, keys], grad_scores)
            gqt_ref[pl.ds(pl.multiple_of(h * HD, HD), HD), at] = grad_q
        return carry

    lax.fori_loop(0, heads, one, 0)
    grads = jnp.concatenate(
        [gqt_ref[...].T] + [gk_ref[h] for h in range(heads)] + [gv_ref[h] for h in range(heads)], axis=1
    ).astype(BF)
    grad_o[...] = grads
    sums_o[...] = jnp.broadcast_to(jnp.sum(grads.astype(F32), axis=0, keepdims=True), sums_o.shape)
    back = mm_nt(grad_o[...], w_ref[...])
    keep_near_o[...] = back[0:rows]
    send_o[0:rows] = back[rows : 2 * rows].astype(BF)
    keep_chip_o[...] = back[2 * rows : 3 * rows]
    send_o[rows : 2 * rows] = back[3 * rows : 4 * rows].astype(BF)


def attend_back(seg, rows, parts, grads_in, log_total, weight, query_code):
    heads, length = parts[0].shape[:2]
    depth, width = weight.shape[0], heads * HD
    shape = jax.ShapeDtypeStruct
    fixed = lambda a: pl.BlockSpec(a.shape, lambda g, n=len(a.shape): (0,) * n)

    def piece(grads):
        if len(grads.shape) == 2:
            return pl.BlockSpec((rows, width), lambda g: (seg, 0))
        return pl.BlockSpec((1, rows, width), lambda g: (0, seg, 0))

    outs = (
        shape((length, 3 * width), BF),
        shape((rows, depth), F32),
        shape((rows, depth), F32),
        shape((2 * rows, depth), BF),
        shape((8, 3 * width), F32),
    )
    return pl.pallas_call(
        lambda *refs: attend_back_kernel(heads, *refs),
        grid=(1,),
        out_shape=outs,
        in_specs=[fixed(a) for a in parts] + [piece(a) for a in grads_in] + [fixed(a) for a in (log_total, weight)]
        + [pl.BlockSpec((1,) + query_code.shape[1:], lambda g: (seg, 0, 0))],
        out_specs=[fixed(o) for o in outs],
        scratch_shapes=[
            pltpu.VMEM((length, length), F32),
            pltpu.VMEM((heads, length, HD), BF),
            pltpu.VMEM((width, length), F32),
            pltpu.VMEM((heads, length, HD), F32),
            pltpu.VMEM((heads, length, HD), F32),
            pltpu.VMEM((2, length, 256), F32),
            pltpu.VMEM((2, length, 256), F32),
        ],
        cost_estimate=pl.CostEstimate(
            flops=2 * length * depth * 3 * width + 40 * length * length * width,
            bytes_accessed=12 << 20,
            transcendentals=heads * length * length,
        ),
        name="attend_back",
    )(*parts, *grads_in, log_total, weight, query_code)


def qkv_grads(place, rows_t, grads, sums, shard):
    depth, length = rows_t[0].shape
    columns, segs = grads[0].shape[1], len(grads)
    part = depth // 2
    blocks = part // shard
    shape = jax.ShapeDtypeStruct

    def kernel(place_ref, *refs):
        x_refs, g_refs, s_refs = refs[:segs], refs[segs : 2 * segs], refs[2 * segs : 3 * segs]
        keep_o, send_o, made_ref = refs[3 * segs :]
        made = sum(mm(x[...], g[...]) for x, g in zip(x_refs, g_refs))
        for f in range(blocks):
            made_ref[f] = made[f * shard : (f + 1) * shard]
        below = sum(s[...] for s in s_refs)
        for rest in range(blocks // 2):
            for out, entry in ((keep_o, place_ref[1]), (send_o, 1 - place_ref[1])):
                out[rest, 0:shard] = made_ref[2 * rest + entry].astype(out.dtype)
                out[rest, shard:] = below.astype(out.dtype)

    whole = lambda a: pl.BlockSpec(a.shape, lambda g: (0, 0))
    out = pl.BlockSpec((blocks // 2, shard + 8, columns), lambda g: (g, 0, 0))
    return pl.pallas_call(
        kernel,
        grid=(2,),
        out_shape=tuple(shape((blocks, shard + 8, columns), kind) for kind in (F32, BF)),
        in_specs=[pl.BlockSpec(memory_space=pltpu.SMEM)]
        + [pl.BlockSpec((part, length), lambda g: (g, 0))] * segs
        + [whole(a) for a in (*grads, *sums)],
        out_specs=(out, out),
        scratch_shapes=[pltpu.VMEM((blocks, shard, columns), F32)],
        cost_estimate=pl.CostEstimate(
            flops=2 * segs * length * depth * columns, bytes_accessed=12 << 20, transcendentals=0
        ),
        name="qkv_grads",
    )(place, *rows_t, *grads, *sums)


def finish(seg, held, keep, near, far):
    rows, depth = keep.shape
    steps = 2
    part = rows // steps
    block = pl.BlockSpec((part, depth), lambda g: (seg * steps + g, 0))
    whole = pl.BlockSpec((part, depth), lambda g: (g, 0))

    def kernel(held_ref, keep_ref, near_ref, far_ref, out_ref):
        out_ref[...] = held_ref[...] + keep_ref[...] + near_ref[...].astype(F32) + far_ref[...].astype(F32)

    return pl.pallas_call(
        kernel,
        grid=(steps,),
        out_shape=jax.ShapeDtypeStruct(held.shape, F32),
        in_specs=[block, whole, whole, whole],
        out_specs=block,
        input_output_aliases={0: 0},
        cost_estimate=pl.CostEstimate(flops=1 << 20, bytes_accessed=4 << 20, transcendentals=0),
        name="finish",
    )(held, keep, near, far)


def fold(place, steps, groups, turned=False):
    shape = jax.ShapeDtypeStruct

    def lead_of(term):
        return term[1][1:-2] if term[3] else term[1][:-2]

    def spec(term):
        index = term[2]
        return pl.BlockSpec(term[1], lambda g, p: tuple(index(g, p)) + (0, 0))

    def sums_of(place_ref, ins, terms, number):
        pieces = {}

        def add(start, values):
            size = values.shape[0]
            inside = [k for k in pieces if start <= k[0] and sum(k) <= start + size]
            for k in inside:
                pieces[k] = pieces[k] + values[k[0] - start : sum(k) - start]
            if not inside:
                pieces[start, size] = values

        for ref, term in zip(ins, terms):
            rest, entry = number, []
            for n in reversed(lead_of(term)):
                entry.insert(0, rest % n)
                rest //= n
            if turned:
                entry[0] = place_ref[0] ^ number
            _, block, _, stacked, row = term
            if stacked:
                for i in range(block[0]):
                    add(row + i * block[-2], ref[(i, *entry)].astype(F32))
            else:
                add(row, ref[tuple(entry)].astype(F32))
        return pieces

    counts = [math.prod(lead_of(terms[0])) for terms, _ in groups]
    in_terms = [t for terms, _ in groups for t in terms]
    out_shape, out_specs = [], []
    for (terms, outs), count in zip(groups, counts):
        total = max(row + block[-2] * (block[0] if stacked else 1) for _, block, _, stacked, row in terms)
        columns = terms[0][0].shape[-1]
        if len(outs) == 1:
            out_shape.append(shape((steps * count, total, columns), outs[0]))
            out_specs.append(pl.BlockSpec((count, total, columns), lambda g, p: (g, 0, 0)))
        else:
            out_shape += [shape((total, columns), kind) for kind in outs]
            out_specs += [pl.BlockSpec((total, columns), lambda g, p: (0, 0))] * len(outs)

    def kernel(place_ref, *refs):
        refs = list(refs)
        out_refs = refs[len(in_terms) :]
        for (terms, outs), count in zip(groups, counts):
            ins, refs = refs[: len(terms)], refs[len(terms) :]
            own, out_refs = out_refs[: len(outs)], out_refs[len(outs) :]
            for number in range(count):
                out = own[0].at[number] if len(outs) == 1 else own[number]
                for (start, size), values in sums_of(place_ref, ins, terms, number).items():
                    out[start : start + size, :] = values.astype(out.dtype)

    return pl.pallas_call(
        kernel,
        grid_spec=pltpu.PrefetchScalarGridSpec(
            num_scalar_prefetch=1, grid=(steps,), in_specs=[spec(t) for t in in_terms], out_specs=out_specs
        ),
        out_shape=out_shape,
        cost_estimate=pl.CostEstimate(flops=1 << 20, bytes_accessed=4 << 20, transcendentals=0),
        name="fold",
    )(place, *[t[0] for t in in_terms])


def own_columns(values, group, width):
    return lax.dynamic_slice_in_dim(values, group * width, width, axis=1)


def per_device(
    layer_input, doc_starts, mem_rows, w_query, b_query, w_key, w_value, b_value, w_out, b_out,
    attn_gain, attn_shift, w_up, b_up, w_down, b_down, ffn_gain, ffn_shift, grad_out,
):
    segs, rows, depth = layer_input.shape
    groups = lax.axis_size(SEQ)
    width, half = depth // groups, depth // 2
    ff = w_up.shape[1]
    length = rows * groups
    here, place = lax.axis_index(SEQ), lax.axis_index(FSDP)
    upper_core, upper_chip = bit_of(here, CORE), bit_of(here, CHIP)
    core, chip = upper_core.astype(jnp.int32), upper_chip.astype(jnp.int32)
    shard = w_query.shape[0]
    devices = lax.axis_size(FSDP)
    ratio = ff // depth
    direct = shard % 32 == 0

    over_core = hop(layer_input, SEQ, CORE)
    first, later = (hop(part, SEQ, CHIP) for part in (layer_input[:1], layer_input[1:]))
    first_both, later_both = (hop(part, SEQ, CORE) for part in (first, later))

    def rows_of(i):
        chip_rows, both, at = (first, first_both, 0) if i == 0 else (later, later_both, i - 1)
        return ((layer_input, i), (over_core, i), (chip_rows, at), (both, at))

    vectors = (b_query, b_value, b_out, attn_gain, attn_shift, b_down, ffn_gain, ffn_shift, b_up)
    spot = jnp.stack([here, core, chip]).astype(jnp.int32)
    if direct:
        own, up_part, rest_part = pack(spot, (w_query, w_key, w_value, w_out, w_up, w_down), vectors)
        qkv_pieces = gather_pieces(own)
        order = jnp.arange(devices, dtype=jnp.int32) ^ place

        def two_parts(block):
            pieces = {0: block}
            for shift, n in reversed(fsdp_digits()[1:]):
                for held in list(pieces):
                    for step in range(1, n):
                        pieces[held | step << shift] = hop(pieces[held], FSDP, step << shift)
            near = jnp.stack([pieces[j] for j in sorted(pieces)])
            return near, hop(near, FSDP, 1)

        rest = two_parts(rest_part)
        rest_far = [hop(part, SEQ, CHIP) for part in rest]
        quarter_ff = ff // 4
        up = two_parts(up_part[:, :quarter_ff]) + two_parts(up_part[:, quarter_ff:])
        middle_weights = (
            *up, *[hop(part, SEQ, CORE) for part in up],
            *rest, *rest_far,
            *[hop(part, SEQ, CORE) for part in rest],
            *[hop(part, SEQ, CORE) for part in rest_far],
        )
        up_bias = jnp.zeros((1, ff), F32)
        qkv_bias = jnp.zeros((1, 3 * width), F32)
    else:
        own = jnp.concatenate([own_columns(w, here, width) for w in (w_query, w_key, w_value)], axis=1)
        qkv_pieces = [lax.all_gather(own, FSDP, axis=0, tiled=True)]
        found = lax.all_gather(jnp.concatenate(vectors), FSDP, axis=0).astype(F32)
        order = jnp.zeros((1,), jnp.int32)
        out_whole, up_whole, down_whole = (
            lax.all_gather(w, FSDP, axis=0, tiled=True) for w in (w_out, w_up, w_down)
        )
        up_halves, down_halves = up_whole.reshape(depth, 2, ff // 2), down_whole.reshape(2, ff // 2, depth)
        middle_weights = (
            out_whole,
            jnp.where(upper_core, up_halves[:, ::-1], up_halves).reshape(depth, ff),
            jnp.where(upper_core, down_halves[::-1], down_halves).reshape(ff, depth),
        )
        names = len(vectors) - 1
        q_bias, v_bias, o_bias, gain_one, shift_one, down_bias, gain_two, shift_two = (
            found[:, i * shard : (i + 1) * shard].reshape(-1) for i in range(names)
        )
        up_bias = found[:, names * shard :].reshape(2, ff // 2)
        up_bias = jnp.where(upper_core, up_bias[::-1], up_bias).reshape(1, ff)
        vector_rows = jnp.stack([o_bias, gain_one, shift_one, down_bias, gain_two, shift_two, o_bias, o_bias])
        qkv_bias = jnp.concatenate(
            [
                lax.dynamic_slice_in_dim(q_bias, here * width, width),
                jnp.zeros((width,), F32),
                lax.dynamic_slice_in_dim(v_bias, here * width, width),
            ]
        )[None, :]
    piece_rows = shard if direct else devices * shard
    order = jnp.concatenate([order, spot])

    spots = jnp.arange(length, dtype=jnp.int32)
    positions = ((spots // rows) ^ here) * rows + spots % rows
    doc_ids = jnp.sum((doc_starts[:, :, None] <= positions[None, None, :]).astype(F32), axis=1)
    is_memory = jnp.any(mem_rows[:, :, None] == positions[None, None, :], axis=1)
    penalty = jnp.where(is_memory, 0.0, MASKED)
    query_code = jnp.stack([doc_ids, penalty] + [jnp.zeros_like(doc_ids)] * 6, axis=1)

    done = []
    for i in range(segs):
        done.append(attend(i, order, rows_of(i), qkv_pieces, piece_rows, qkv_bias, query_code))

    contexts = []
    for i in range(segs):
        near, to_core, to_chip = done[i][6:9]
        from_core = hop(to_core, SEQ, CORE)
        from_chip = hop(to_chip, SEQ, CHIP)
        contexts.append((near, from_core, from_chip, hop(from_chip[rows:], SEQ, CORE)))

    (
        layer_out, context_t, low_t, active_t, gb, gh, ga, grad_sum_one, g0, g1, g2, g3, vector_sums,
    ) = middle(
        order, middle_weights, shard, direct, contexts, layer_input.reshape(segs * rows, depth),
        grad_out.reshape(segs * rows, depth), done[0][10] if direct else vector_rows, up_bias,
    )
    heads_grads = (g0, hop(g1, SEQ, CORE), hop(g2, SEQ, CHIP), hop(hop(g3, SEQ, CORE), SEQ, CHIP))

    digits = fsdp_digits()
    place_digits = [(FSDP, shift, n, place) for shift, n in digits]

    second_keep, second_send = second_grads(active_t, gb)
    second_got = hop(second_send, SEQ, CORE)
    first_keep, first_send = first_grads(context_t, low_t, ga, gh)
    first_got = hop(first_send, SEQ, CORE)
    vector_sums = vector_sums + hop(vector_sums, SEQ, CORE)

    rest_count = devices // 2
    part_rows = shard // 2
    at_place = jnp.stack([place >> 1, place & 1, chip]).astype(jnp.int32)

    def by_block(values, size):
        return values.reshape(values.shape[:-2] + (rest_count, 2, 2, size, half))

    first = [by_block(v, part_rows) for v in (first_keep, first_got)]
    second = [by_block(v, part_rows * ratio) for v in (second_keep, second_got)]
    vector_blocks = by_block(vector_sums.reshape(-1, half), 8)
    below_first = (ratio + 1) * part_rows
    chunk = max(rest_count // 2, 1)

    def first_terms(size, block, index):
        return [
            (v, (ratio + 1, size) + block + (part_rows, half), lambda g, p: (0, g) + index(p), True, 0) for v in first
        ]

    def second_terms(size, block, index, row=0):
        at = lambda g, p: (g,) + index(p)
        terms = [(v, (size,) + block + (part_rows * ratio, half), at, False, row) for v in second]
        return terms + [(vector_blocks, (size,) + block + (8, half), at, False, row + part_rows * ratio)]

    def got_terms(got, many, index, row=0):
        if not many:
            return [(got, (rest_count,) + got.shape[1:], lambda g, p: (0,), False, row)]
        got = got.reshape((rest_count, 2) + got.shape[1:])
        return [(got, (rest_count, 1) + got.shape[2:], lambda g, p: (0, index(p)), False, row)]

    one, many = (BF,), rest_count // chunk
    send_b = fold(at_place, many, [(second_terms(chunk, (2, 1), lambda p: (0, 1 - p[2])), one)])[0]
    got_b0 = hop(send_b, SEQ, CHIP)
    send_a = fold(at_place, many, [(first_terms(chunk, (1, 2), lambda p: (1 - p[1], 0)), one)])[0]
    got_a0 = hop(send_a, FSDP, 1)
    send_b, send_a = fold(
        at_place,
        1,
        [
            (second_terms(rest_count, (1, 1), lambda p: (1 - p[1], p[2]))
             + got_terms(got_b0, True, lambda p: 1 - p[1]), one),
            (first_terms(rest_count, (1, 1), lambda p: (p[1], 1 - p[2]))
             + got_terms(got_a0, True, lambda p: 1 - p[2]), one),
        ],
    )
    got_b1 = hop(send_b, FSDP, 1)
    got_a1 = hop(send_a, SEQ, CHIP)

    backs = []
    for i in range(segs):
        backs.append(
            attend_back(i, rows, done[i][:4], heads_grads, done[i][9], done[0][5], query_code)
        )

    last_terms = (
        first_terms(rest_count, (1, 1), lambda p: (p[1], p[2]))
        + got_terms(got_a0, True, lambda p: p[2]) + got_terms(got_a1, False, None)
        + second_terms(rest_count, (1, 1), lambda p: (p[1], p[2]), below_first)
        + got_terms(got_b0, True, lambda p: p[1], below_first) + got_terms(got_b1, False, None, below_first)
    )
    if len(digits) == 2:
        shift, n = digits[1]
        kinds = (F32,) + (BF,) * (n - 1)
        mine, *sends = fold(at_place, 1, [(last_terms, kinds)], turned=True)
        for k, send in enumerate(sends, 1):
            mine = mine + hop(send, FSDP, k << shift).astype(F32)
    else:
        merged = fold(at_place, 1, [(last_terms, (F32,))])[0]
        lead = tuple(n for _, n in reversed(digits[1:]))
        mine = halve(merged.reshape(lead + merged.shape[1:]), place_digits[1:])
    mine = mine.astype(BF)
    other = hop(mine, SEQ, CHIP)
    far = [hop(part, SEQ, CORE) for part in (mine, other)]

    def quarter(values):
        blocks = values[: (ratio + 1) * part_rows].reshape(ratio + 1, part_rows, half)
        return (
            blocks[ratio],
            jnp.concatenate([blocks[i] for i in range(ratio)], axis=1),
            values[(ratio + 1) * part_rows :],
        )

    corners = [quarter(values[:-8]) for values in (mine, other, *far)]
    vector_rows = jnp.where(upper_chip, other[-8:], mine[-8:]).astype(F32)
    per = half // shard

    def vector_of(i):
        return vector_rows[i // per, i % per * shard : (i % per + 1) * shard]


    def assembled(i):
        near = joined(corners[0][i], corners[1][i], upper_chip, 0)
        return joined(near, joined(corners[2][i], corners[3][i], upper_chip, 0), upper_core, 1).astype(F32)

    grad_w_out, grad_w_up, grad_w_down = (assembled(i) for i in range(3))

    grad_input = grad_sum_one
    for i in range(segs):
        _, keep_near, keep_chip, send, _ = backs[i]
        near = hop(send, SEQ, CORE)
        far = (keep_chip + near[rows:].astype(F32)).astype(BF)
        grad_input = finish(i, grad_input, keep_near, near, hop(far, SEQ, CHIP))

    keep, send = qkv_grads(
        at_place, [d[4] for d in done], [b[0] for b in backs], [b[4] for b in backs], shard
    )
    lead = tuple(n for _, n in reversed(digits[1:])) + keep.shape[1:]
    mine = halve(keep.reshape(lead), place_digits[1:], [hop(send, FSDP, 1).reshape(lead)]).astype(BF)
    other = hop(mine, SEQ, CORE)
    far_mine = hop(mine, SEQ, CHIP)
    far_other = hop(other, SEQ, CHIP)
    parts = swapped([mine, other, far_mine, far_other], upper_core, upper_chip)

    def columns_of(i):
        return jnp.concatenate([p[:, i * width : (i + 1) * width] for p in parts], axis=1).astype(F32)

    def own_part(vector):
        count = vector.shape[0] * shard // depth
        return lax.dynamic_slice_in_dim(vector, place * count, count)

    grad_q, grad_k, grad_v = (columns_of(i) for i in range(3))
    return (
        layer_out.reshape(layer_input.shape),
        grad_input.reshape(layer_input.shape),
        grad_q[:shard],
        own_part(grad_q[shard]),
        grad_k[:shard],
        grad_v[:shard],
        own_part(grad_v[shard]),
        grad_w_out,
        vector_of(0),
        vector_of(1),
        vector_of(2),
        grad_w_up,
        jnp.concatenate([vector_of(6 + r) for r in range(ratio)]),
        grad_w_down,
        vector_of(3),
        vector_of(4),
        vector_of(5),
    )


def solution(mesh):
    rows, cols = P(FSDP, SEQ, None), P(FSDP, None)
    vec = P(FSDP)
    return jax.shard_map(
        per_device,
        mesh=mesh,
        in_specs=(
            rows, cols, cols, cols, vec, cols, cols, vec, cols, vec,
            vec, vec, cols, vec, cols, vec, vec, vec, rows,
        ),
        out_specs=(
            rows, rows, cols, vec, cols, cols, vec, cols, vec,
            vec, vec, cols, vec, cols, vec, vec, vec,
        ),
        check_vma=False,
    )
```

```python
import math

import jax
import jax.numpy as jnp
from jax import lax
from jax.experimental import pallas as pl
from jax.experimental.pallas import tpu as pltpu
from jax.sharding import PartitionSpec as P


HD = 64
LN_EPS = 1e-12
MASKED = -1e30
BF = jnp.bfloat16
F32 = jnp.float32


CORE, CHIP = 1, 2


SEQ, FSDP = "seq", "fsdp"


def hop(values, axis, bit):
    size = lax.axis_size(axis)
    return lax.ppermute(values, axis, [(i, i ^ bit) for i in range(size)])


def bit_of(index, bit):
    return (index & bit) != 0


def fsdp_digits():
    bits = lax.axis_size(FSDP).bit_length() - 1
    digits, at = [], 0
    while at < bits:
        take = 1 if at == 0 else min(2, bits - at)
        digits.append((at, 1 << take))
        at += take
    return digits


def gather_pieces(block):
    pieces = {0: block}
    for shift, size in reversed(fsdp_digits()):
        for held in list(pieces):
            for step in range(1, size):
                entry = held | step << shift
                pieces[entry] = hop(pieces[held], FSDP, step << shift)
    return [pieces[j] for j in range(len(pieces))]


def entry_at(values, indices):
    for index in indices:
        values = lax.dynamic_index_in_dim(values, index, values.ndim - 3, keepdims=False)
    return values


def halve(held, steps, beside=()):
    arrived, kept = [(0, list(beside))], []

    def total(last):
        values = entry_at(held, kept + last).astype(F32)
        for at, group in arrived:
            for got in group:
                values = values + entry_at(got, kept[at:] + last).astype(F32)
        return values

    for axis, shift, size, place in steps:
        digit = (place >> shift) & (size - 1)
        group = [hop(total([digit ^ step]).astype(BF), axis, step << shift) for step in range(1, size)]
        kept.append(digit)
        arrived.append((len(kept), group))
    return total([])


def mm(left, right):
    return lax.dot_general(left, right, (((1,), (0,)), ((), ())), preferred_element_type=F32)


def mm_nt(left, right):
    return lax.dot_general(left, right, (((1,), (1,)), ((), ())), preferred_element_type=F32)


def hidden_pairs(query_code, key_code, bias_ref, start, stop):
    step = 128
    for at in range(start, stop, step):
        part = key_code[at : at + step, :]
        same = part[:, 0:1] == query_code[0:1, :]
        bias_ref[at : at + step, :] = jnp.where(same, 0.0, jnp.maximum(part[:, 1:2], query_code[1:2, :]))


def erf_parts(values):
    cdf = 0.5 * (1.0 + lax.erf(values * (1.0 / math.sqrt(2.0))))
    return cdf, jnp.exp(-0.5 * values * values) * (1.0 / math.sqrt(2.0 * math.pi))


def place_rows(pieces, order_ref, rows, target):
    for j, piece in enumerate(pieces):
        at = pl.multiple_of(order_ref[j] * rows, rows)
        target[pl.ds(at, rows), :] = piece[0:rows, :]


def attend_kernel(heads, shard, count, order_ref, x0, x1, x2, x3, *refs):
    pieces, refs = refs[:count], refs[count:]
    b_ref, qc_ref, q_ref, k_ref, kt_ref, v_ref, xrel_o, w_o, near_o, core_o, chip_o, log_o, vec_o = refs[:13]
    bias_ref, vt_ref, ctx_ref, score_ref = refs[13:]
    width = heads * HD
    rows = x0.shape[1]
    length = 4 * rows
    place_rows(pieces, order_ref, shard, w_o)
    added = b_ref[...]
    if count > 1:
        for j, piece in enumerate(pieces):
            vec_o[order_ref[j]] = piece[shard:, 0:128].astype(F32)
        here = order_ref[count]
        near, far = vec_o[2 * here], vec_o[2 * here + 1]
        added = jnp.concatenate(
            [near[0:1, 0:shard], far[0:1, 0:shard], jnp.zeros((1, width), F32), near[1:2, 0:shard], far[1:2, 0:shard]],
            axis=1,
        )
    factor = BF(1.0 / math.sqrt(HD))
    query_code = qc_ref[0]
    key_code = query_code.T
    for j, piece in enumerate((x0, x1, x2, x3)):
        part = slice(j * rows, (j + 1) * rows)
        xrel_o[:, part] = piece[0].T
        made = (mm(piece[0], w_o[...]) + added).astype(BF)
        hidden_pairs(query_code, key_code, bias_ref, j * rows, (j + 1) * rows)
        turned = made.T
        for h in range(heads):
            at = h * HD
            q_ref[h, part, :] = made[:, at : at + HD] * factor
            k_ref[h, part, :] = made[:, width + at : width + at + HD]
            kt_ref[h, :, part] = turned[width + at : width + at + HD] * factor
            v_ref[h, part, :] = made[:, 2 * width + at : 2 * width + at + HD]
            vt_ref[h, :, part] = turned[2 * width + at : 2 * width + at + HD]
    block, chunk = 256, 256
    blocks = length // block

    def score(h, at, slot):
        top = None
        for start in range(0, length, chunk):
            keys = slice(start, start + chunk)
            scores = mm_nt(k_ref[h, keys, :], q_ref[h, at, :]) + bias_ref[keys, at]
            score_ref[slot, keys, :] = scores
            largest = jnp.max(scores.reshape(chunk // 8, 8, block), axis=0)
            top = largest if top is None else jnp.maximum(top, largest)
        return jnp.max(top, axis=0, keepdims=True)

    def one(h, top):
        for b in range(blocks):
            at = slice(b * block, (b + 1) * block)
            if b + 1 < blocks:
                following = score(h, slice((b + 1) * block, (b + 2) * block), (b + 1) % 2)
            else:
                following = score(jnp.minimum(h + 1, heads - 1), slice(0, block), 0)
            total, made = jnp.zeros((8, block), F32), jnp.zeros((HD, block), F32)
            for start in range(0, length, chunk):
                keys = slice(start, start + chunk)
                shifted = jnp.exp(score_ref[b % 2, keys, :] - top)
                total = total + jnp.sum(shifted.reshape(chunk // 8, 8, block), axis=0)
                made = made + mm(vt_ref[h, :, keys], shifted.astype(BF))
            total = jnp.sum(total, axis=0, keepdims=True)
            ctx_ref[pl.ds(pl.multiple_of(h * HD, HD), HD), at] = made / total
            log_o[pl.ds(h, 1), at] = top + jnp.log(total)
            top = following
        return top

    lax.fori_loop(0, heads, one, score(0, slice(0, block), 0))
    near_o[...] = ctx_ref[:, 0:rows].T.astype(BF)
    core_o[...] = ctx_ref[:, rows : 2 * rows].T.astype(BF)
    chip_o[...] = ctx_ref[:, 2 * rows : 4 * rows].T.astype(BF)


def attend(seg, order, pieces, weights, shard, bias, query_code):
    (first, _), width = pieces[0], bias.shape[1] // 3
    rows, depth = first.shape[1:]
    length, heads = 4 * rows, width // HD
    shape = jax.ShapeDtypeStruct
    vmem = pl.BlockSpec(memory_space=pltpu.VMEM)

    def rows_of(at):
        return pl.BlockSpec((1, rows, depth), lambda g, at=at: (at, 0, 0))

    count = len(weights)
    whole = lambda a: pl.BlockSpec(a.shape, lambda g, n=len(a.shape): (0,) * n)
    outs = (
        shape((heads, length, HD), BF),
        shape((heads, length, HD), BF),
        shape((heads, HD, length), BF),
        shape((heads, length, HD), BF),
        shape((depth, length), BF),
        shape((depth, 3 * width), BF),
        shape((rows, width), BF),
        shape((rows, width), BF),
        shape((2 * rows, width), BF),
        shape((8, length), F32),
        shape((count, max(weights[0].shape[0] - shard, 8), 128), F32),
    )
    return pl.pallas_call(
        lambda *refs: attend_kernel(heads, shard, count, *refs),
        grid=(1,),
        out_shape=outs,
        in_specs=[pl.BlockSpec(memory_space=pltpu.SMEM)]
        + [rows_of(at) for _, at in pieces]
        + [whole(w) for w in weights]
        + [whole(bias), pl.BlockSpec((1,) + query_code.shape[1:], lambda g: (seg, 0, 0))],
        out_specs=[whole(o) for o in outs],
        scratch_shapes=[
            pltpu.VMEM((length, length), F32),
            pltpu.VMEM((heads, HD, length), BF),
            pltpu.VMEM((width, length), F32),
            pltpu.VMEM((2, length, 256), F32),
        ],
        cost_estimate=pl.CostEstimate(
            flops=2 * length * depth * 3 * width + 16 * length * length * width,
            bytes_accessed=12 << 20,
            transcendentals=heads * length * length,
        ),
        name="attend",
    )(order, *[p for p, _ in pieces], *weights, bias, query_code)


def pack_kernel(place_ref, wq, wk, wv, wo, wu, wd, *refs):
    vectors, (own_o, up_o, rest_o) = refs[:-3], refs[-3:]
    here, core, chip = place_ref[0], place_ref[1], place_ref[2]
    shard, depth = wq.shape
    width, half, rows = depth // 4, depth // 2, shard // 2
    for i, ref in enumerate((wq, wk, wv)):
        picked = ref[:, 0:width]
        for j in range(1, 4):
            picked = jnp.where(here == j, ref[:, j * width : (j + 1) * width], picked)
        own_o[0:shard, i * width : (i + 1) * width] = picked
    below = [ref[0:1, at : at + shard] for ref in vectors for at in range(0, ref.shape[1], shard)]
    below.append(jnp.zeros((own_o.shape[0] - shard - len(below), shard), BF))
    own_o[shard:, :] = jnp.zeros((own_o.shape[0] - shard, 3 * width), BF)
    own_o[shard:, 0:shard] = jnp.concatenate([b.astype(F32) for b in below], axis=0).astype(BF)
    ff_half = wu.shape[1] // 2
    up_o[...] = wu[:, pl.ds(pl.multiple_of(core * ff_half, ff_half), ff_half)]
    columns = pl.ds(pl.multiple_of(core * half, half), half)
    at = pl.multiple_of(chip * rows, rows)
    rest_o[:, 0:half] = wo[pl.ds(at, rows), columns]
    for i in range(wd.shape[0] // shard):
        rest_o[:, (i + 1) * half : (i + 2) * half] = wd[pl.ds(i * shard + at, rows), columns]


def pack(place, weights, vectors):
    shard, depth = weights[0].shape
    ff, ratio = weights[4].shape[1], weights[5].shape[0] // shard
    shape = jax.ShapeDtypeStruct
    vmem = pl.BlockSpec(memory_space=pltpu.VMEM)
    return pl.pallas_call(
        pack_kernel,
        out_shape=(
            shape((shard + 16, 3 * depth // 4), BF),
            shape((shard, ff // 2), BF),
            shape((shard // 2, (1 + ratio) * depth // 2), BF),
        ),
        in_specs=[pl.BlockSpec(memory_space=pltpu.SMEM)] + [vmem] * (6 + len(vectors)),
        out_specs=[vmem] * 3,
        cost_estimate=pl.CostEstimate(flops=1 << 16, bytes_accessed=4 << 20, transcendentals=0),
        name="pack",
    )(place, *weights, *[v[None, :] for v in vectors])


def norm_stats(values):
    centre = values - jnp.mean(values, axis=-1, keepdims=True)
    inv_dev = lax.rsqrt(jnp.mean(centre * centre, axis=-1, keepdims=True) + LN_EPS)
    return centre * inv_dev, inv_dev


def norm_back(grads, unit, inv_dev, gain):
    scaled = grads * gain
    return inv_dev * (
        scaled
        - jnp.mean(scaled, axis=-1, keepdims=True)
        - unit * jnp.mean(scaled * unit, axis=-1, keepdims=True)
    )


def swapped(parts, upper_core, upper_chip):
    a, b, c, d = parts
    a, b, c, d = (jnp.where(upper_core, y, x) for x, y in ((a, b), (b, a), (c, d), (d, c)))
    return [jnp.where(upper_chip, y, x) for x, y in ((a, c), (b, d), (c, a), (d, b))]


def middle_kernel(segs, shard_rows, direct, order_ref, *refs):
    weights_in, refs = (refs[:16], refs[16:]) if direct else (refs[:3], refs[3:])
    context_in, refs = refs[: 4 * segs], refs[4 * segs :]
    x_ref, go_ref, vec_ref, up_ref = refs[:4]
    (
        out_o, ctx_o, low_o, act_o, gb_o, gh_o, ga_o, gsum_o, g0_o, g1_o, g2_o, g3_o, vec_o,
    ) = refs[4:17]
    wo, wu, wd, slope_ref, half_ref, vec_s, up_s, sums_o, up_sums_o, sems = refs[17:]
    seg = pl.program_id(0)
    depth, ff = wu.shape
    rows, half, ff_half = x_ref.shape[0], depth // 2, ff // 2
    _, core, chip = (order_ref[order_ref.shape[0] - 3 + i] for i in range(3))
    upper_core, upper_chip = core != 0, chip != 0

    def copies():
        if not direct:
            return [[(a, b)] for a, b in zip(weights_in, (wo, wu, wd))]
        found = [[], [], []]
        near, shard = weights_in[0].shape[:2]
        part, ratio = shard // 2, ff // depth
        for side in range(2):
            column = pl.multiple_of((core ^ side) * half, half)
            for low in range(2):
                for j in range(near):
                    block = order_ref[2 * j + low]
                    at = pl.multiple_of(block * shard, shard)
                    for i in range(2):
                        start = side * ff_half + i * ff_half // 2
                        found[1].append(
                            (weights_in[4 * side + 2 * i + low].at[j],
                             wu.at[pl.ds(at, shard), pl.ds(start, ff_half // 2)])
                        )
                    for other in range(2):
                        piece = weights_in[8 + 4 * side + 2 * other + low]
                        inner = (chip ^ other) * part
                        found[0].append(
                            (piece.at[j, :, 0:half],
                             wo.at[pl.ds(pl.multiple_of(at + inner, part), part), pl.ds(column, half)])
                        )
                        for i in range(ratio):
                            row = (block * ratio + i) * shard
                            turned = jnp.where(row < ff_half, row + core * ff_half, row - core * ff_half)
                            turned = pl.multiple_of(turned + inner, part)
                            found[2].append(
                                (piece.at[j, :, (i + 1) * half : (i + 2) * half],
                                 wd.at[pl.ds(turned, part), pl.ds(column, half)])
                            )
        return found

    groups, used = [], 0
    for found in copies():
        groups.append([pltpu.make_async_copy(a, b, sems.at[used + i]) for i, (a, b) in enumerate(found)])
        used += len(found)

    @pl.when(seg == 0)
    def _():
        for group in groups:
            for one in group:
                one.start()
        if direct:
            count, shard = vec_ref.shape[0], weights_in[0].shape[1]
            for i in range(6):
                vec_s[i : i + 1, :] = jnp.concatenate(
                    [vec_ref[j, i + 2 : i + 3, 0:shard] for j in range(count)], axis=1
                )
            halves = [
                jnp.concatenate(
                    [
                        vec_ref[j, 8 + r : 9 + r, 0:shard]
                        for j in range(side * count // 2, (side + 1) * count // 2)
                        for r in range(ff // depth)
                    ],
                    axis=1,
                )
                for side in range(2)
            ]
            up_s[:, 0:ff_half] = jnp.where(upper_core, halves[1], halves[0])
            up_s[:, ff_half:] = jnp.where(upper_core, halves[0], halves[1])
        else:
            vec_s[...] = vec_ref[...]
            up_s[...] = up_ref[...]
        sums_o[...] = jnp.zeros_like(sums_o)
        up_sums_o[...] = jnp.zeros_like(up_sums_o)

    def ready(which):
        @pl.when(seg == 0)
        def _():
            for one in groups[which]:
                one.wait()

    def vector(i):
        return vec_s[i : i + 1, :]

    ready(0)
    parts = []
    for j in range(4):
        picked = context_in[j][...]
        for i in range(1, segs):
            picked = jnp.where(seg == i, context_in[4 * i + j][...], picked)
        parts.append(picked)
    context = jnp.concatenate(swapped(parts, upper_core, upper_chip), axis=1)
    ctx_o[...] = context.T
    summed = x_ref[...].astype(F32) + mm(context, wo[...]) + vector(0)
    unit_one, inv_one = norm_stats(summed)
    normed_one = unit_one * vector(1) + vector(2)
    low = normed_one.astype(BF)
    low_o[...] = low.T
    ready(1)
    ready(2)
    step = depth if ff_half % depth == 0 else ff_half
    branch = jnp.zeros((rows, depth), F32)
    for start in range(0, ff, step):
        part = slice(start, start + step)
        hidden = mm(low, wu[:, part]) + up_s[:, part]
        cdf, density = erf_parts(hidden)
        active = (hidden * cdf).astype(BF)
        slope_ref[:, part] = cdf + hidden * density
        side = 0 if start < ff_half else 1
        target = pl.multiple_of((core ^ side) * ff_half, ff_half) + (start - side * ff_half)
        act_o[pl.ds(pl.multiple_of(target, 128), step), :] = active.T
        branch = branch + mm(active, wd[part, :])
    unit_two, inv_two = norm_stats(normed_one + (branch + vector(3)))
    out_o[...] = (unit_two * vector(4) + vector(5)).astype(BF)

    def add_sum(i, values):
        sums_o[i : i + 1, :] += jnp.sum(values, axis=0, keepdims=True)

    def halves(values, out):
        half_ref[...] = values
        out[:, 0:half] = half_ref[:, pl.ds(pl.multiple_of(core * half, half), half)].astype(BF)
        out[:, half:] = half_ref[:, pl.ds(pl.multiple_of((1 - core) * half, half), half)].astype(BF)

    grads = go_ref[...].astype(F32)
    add_sum(4, grads * unit_two)
    add_sum(5, grads)
    grad_two = norm_back(grads, unit_two, inv_two, vector(4))
    grad_branch = grad_two.astype(BF)
    add_sum(3, grad_branch.astype(F32))
    halves(grad_branch.astype(F32), gb_o)
    grad_normed = grad_two
    for start in range(0, ff, step):
        part = slice(start, start + step)
        grad_hidden = (mm_nt(grad_branch, wd[part, :]) * slope_ref[:, part]).astype(BF)
        side, first = start // ff_half, start % ff_half
        for at in range(0, step, half):
            target = 2 * (first + at) + side * half
            gh_o[:, target : target + half] = grad_hidden[:, at : at + half]
        up_sums_o[:, part] += jnp.sum(grad_hidden.astype(F32), axis=0, keepdims=True)
        grad_normed = grad_normed + mm_nt(grad_hidden, wu[:, part])
    add_sum(1, grad_normed * unit_one)
    add_sum(2, grad_normed)
    grad_one = norm_back(grad_normed, unit_one, inv_one, vector(1))
    gsum_o[...] = grad_one
    grad_attn = grad_one.astype(BF)
    add_sum(0, grad_attn.astype(F32))
    halves(grad_attn.astype(F32), ga_o)
    grad_context = mm_nt(grad_attn, wo[...]).astype(BF)
    width = depth // 4
    turned = swapped([grad_context[:, j * width : (j + 1) * width] for j in range(4)], upper_core, upper_chip)
    g0_o[...] = turned[0]
    g1_o[...] = turned[1]
    g2_o[...] = turned[2]
    g3_o[...] = turned[3]

    @pl.when(seg == segs - 1)
    def _():
        low_half, high_half = up_sums_o[:, 0:ff_half], up_sums_o[:, ff_half:]
        ordered = jnp.concatenate(
            [jnp.where(upper_core, high_half, low_half), jnp.where(upper_core, low_half, high_half)], axis=1
        )
        vec_o[...] = jnp.zeros_like(vec_o)
        ratio, per = ff // depth, half // shard_rows
        for f in range(depth // shard_rows):
            own = slice(f * shard_rows, (f + 1) * shard_rows)
            parts = [sums_o[i : i + 1, own] for i in range(6)] + [
                ordered[:, (f * ratio + r) * shard_rows : (f * ratio + r + 1) * shard_rows] for r in range(ratio)
            ]
            for row in range(0, len(parts), per):
                line = jnp.concatenate(parts[row : row + per], axis=1)
                vec_o[2 * f, row // per : row // per + 1, 0 : line.shape[1]] = line


def middle(order, weights, shard, direct, contexts, rows_in, grad_out, vectors, up_bias):
    tokens, depth = rows_in.shape
    ff, segs = up_bias.shape[1], len(contexts)
    rows, width, half = tokens // segs, depth // 4, depth // 2
    shape = jax.ShapeDtypeStruct
    fixed = lambda a: pl.BlockSpec(a.shape, lambda g, n=len(a.shape): (0,) * n)
    moving = lambda columns: pl.BlockSpec((rows, columns), lambda g: (g, 0))
    turned = lambda units: pl.BlockSpec((units, rows), lambda g: (0, g))
    outs = [
        (shape((tokens, depth), BF), moving(depth)),
        (shape((depth, tokens), BF), turned(depth)),
        (shape((depth, tokens), BF), turned(depth)),
        (shape((ff, tokens), BF), turned(ff)),
    ]
    for columns, kind in [(depth, BF), (ff, BF), (depth, BF), (depth, F32), (width, BF), (width, BF),
                          (width, BF), (width, BF)]:
        outs.append((shape((tokens, columns), kind), moving(columns)))
    last = shape((2 * depth // shard, 8, half), F32)
    outs.append((last, fixed(last)))
    piece = pl.BlockSpec((rows, width), lambda g: (0, 0))
    flat = [one for four in contexts for one in four]
    if direct:
        copies = 2 * (2 * weights[0].shape[0]) * (2 + 2 * (1 + ff // depth))
    else:
        copies = 3
    return pl.pallas_call(
        lambda *refs: middle_kernel(segs, shard, direct, *refs),
        grid=(segs,),
        out_shape=tuple(o for o, _ in outs),
        in_specs=[pl.BlockSpec(memory_space=pltpu.SMEM)]
        + [pl.BlockSpec(memory_space=pl.ANY)] * len(weights)
        + [piece] * len(flat)
        + [moving(depth), moving(depth), fixed(vectors), fixed(up_bias)],
        out_specs=[b for _, b in outs],
        scratch_shapes=[
            pltpu.VMEM((depth, depth), BF),
            pltpu.VMEM((depth, ff), BF),
            pltpu.VMEM((ff, depth), BF),
            pltpu.VMEM((rows, ff), F32),
            pltpu.VMEM((rows, depth), F32),
            pltpu.VMEM((8, depth), F32),
            pltpu.VMEM((1, ff), F32),
            pltpu.VMEM((8, depth), F32),
            pltpu.VMEM((1, ff), F32),
            pltpu.SemaphoreType.DMA((copies,)),
        ],
        cost_estimate=pl.CostEstimate(
            flops=4 * tokens * depth * (depth + 2 * ff), bytes_accessed=40 << 20,
            transcendentals=2 * tokens * ff,
        ),
        name="middle",
    )(order, *weights, *flat, rows_in, grad_out, vectors, up_bias)


def first_grads(context_t, low_t, ga, gh):
    depth, tokens = low_t.shape
    half, ratio = depth // 2, gh.shape[1] // depth
    shape = jax.ShapeDtypeStruct

    def kernel(ctx_ref, low_ref, ga_ref, gh_ref, keep_o, send_o):
        step = pl.program_id(0)

        def put(left, right):
            made = mm(left, right)
            keep_o[0] = made[:, 0:half].astype(BF)
            send_o[0] = made[:, half:].astype(BF)

        @pl.when(step < ratio)
        def _():
            put(low_ref[...], gh_ref[...])

        @pl.when(step == ratio)
        def _():
            put(ctx_ref[...], ga_ref[...])

    whole = lambda a: pl.BlockSpec(a.shape, lambda g: (0, 0))
    out = pl.BlockSpec((1, depth, half), lambda g: (g, 0, 0))
    return pl.pallas_call(
        kernel,
        grid=(ratio + 1,),
        out_shape=(shape((ratio + 1, depth, half), BF),) * 2,
        in_specs=[
            whole(context_t), whole(low_t), whole(ga),
            pl.BlockSpec((tokens, depth), lambda g: (0, jnp.minimum(g, ratio - 1))),
        ],
        out_specs=(out, out),
        cost_estimate=pl.CostEstimate(
            flops=2 * tokens * depth * depth * (ratio + 1), bytes_accessed=16 << 20, transcendentals=0
        ),
        name="first_grads",
    )(context_t, low_t, ga, gh)


def second_grads(active_t, gb):
    ff, tokens = active_t.shape
    depth = gb.shape[1]
    half = depth // 2
    shape = jax.ShapeDtypeStruct

    def kernel(act_ref, gb_ref, keep_o, send_o):
        made = mm(act_ref[...], gb_ref[...])
        keep_o[...] = made[:, 0:half].astype(BF)
        send_o[...] = made[:, half:].astype(BF)

    out = pl.BlockSpec((depth, half), lambda g: (g, 0))
    return pl.pallas_call(
        kernel,
        grid=(ff // depth,),
        out_shape=(shape((ff, half), BF),) * 2,
        in_specs=[pl.BlockSpec((depth, tokens), lambda g: (g, 0)), pl.BlockSpec(gb.shape, lambda g: (0, 0))],
        out_specs=(out, out),
        cost_estimate=pl.CostEstimate(flops=2 * tokens * depth * ff, bytes_accessed=14 << 20, transcendentals=0),
        name="second_grads",
    )(active_t, gb)


def attend_back_kernel(
    heads, q_ref, k_ref, kt_ref, v_ref, g0, g1, g2, g3, log_ref, w_ref, qc_ref,
    grad_o, keep_near_o, keep_chip_o, send_o, sums_o,
    bias_ref, g_ref, gqt_ref, gk_ref, gv_ref, score_ref, prob_ref,
):
    length = grad_o.shape[0]
    rows = length // 4
    for h in range(heads):
        at = h * HD
        for j, piece in enumerate((g0, g1, g2, g3)):
            g_ref[h, j * rows : (j + 1) * rows, :] = piece[:, at : at + HD]
    query_code = qc_ref[0]
    hidden_pairs(query_code, query_code.T, bias_ref, 0, length)
    block, chunk = 256, 256
    blocks = length // block

    def score(h, at, slot):
        log_total = log_ref[pl.ds(h, 1), at]
        for start in range(0, length, chunk):
            keys = slice(start, start + chunk)
            score_ref[slot, keys, :] = mm_nt(k_ref[h, keys, :], q_ref[h, at, :]) + (bias_ref[keys, at] - log_total)
            prob_ref[slot, keys, :] = mm_nt(v_ref[h, keys, :], g_ref[h, at, :])

    score(0, slice(0, block), 0)

    def one(h, carry):
        for b in range(blocks):
            at, slot = slice(b * block, (b + 1) * block), b % 2
            if b + 1 < blocks:
                score(h, slice((b + 1) * block, (b + 2) * block), 1 - slot)
            else:
                score(jnp.minimum(h + 1, heads - 1), slice(0, block), 1 - slot)

            def put(ref, keys, values):
                ref[h, keys, :] = values if b == 0 else ref[h, keys, :] + values

            row_dot = jnp.zeros((8, block), F32)
            for start in range(0, length, chunk):
                keys = slice(start, start + chunk)
                probs = jnp.exp(score_ref[slot, keys, :])
                weighted = probs * prob_ref[slot, keys, :]
                row_dot = row_dot + jnp.sum(weighted.reshape(chunk // 8, 8, block), axis=0)
                score_ref[slot, keys, :] = probs
                prob_ref[slot, keys, :] = weighted
                put(gv_ref, keys, mm(probs.astype(BF), g_ref[h, at, :]))
            row_dot = jnp.sum(row_dot, axis=0, keepdims=True)
            grad_q = jnp.zeros((HD, block), F32)
            for start in range(0, length, chunk):
                keys = slice(start, start + chunk)
                grad_scores = (prob_ref[slot, keys, :] - score_ref[slot, keys, :] * row_dot).astype(BF)
                put(gk_ref, keys, mm(grad_scores, q_ref[h, at, :]))
                grad_q = grad_q + mm(kt_ref[h, :, keys], grad_scores)
            gqt_ref[pl.ds(pl.multiple_of(h * HD, HD), HD), at] = grad_q
        return carry

    lax.fori_loop(0, heads, one, 0)
    grads = jnp.concatenate(
        [gqt_ref[...].T] + [gk_ref[h] for h in range(heads)] + [gv_ref[h] for h in range(heads)], axis=1
    ).astype(BF)
    grad_o[...] = grads
    sums_o[...] = jnp.broadcast_to(jnp.sum(grads.astype(F32), axis=0, keepdims=True), sums_o.shape)
    back = mm_nt(grad_o[...], w_ref[...])
    keep_near_o[...] = back[0:rows]
    send_o[0:rows] = back[rows : 2 * rows].astype(BF)
    keep_chip_o[...] = back[2 * rows : 3 * rows]
    send_o[rows : 2 * rows] = back[3 * rows : 4 * rows].astype(BF)


def attend_back(seg, rows, parts, grads_in, log_total, weight, query_code):
    heads, length = parts[0].shape[:2]
    depth, width = weight.shape[0], heads * HD
    shape = jax.ShapeDtypeStruct
    fixed = lambda a: pl.BlockSpec(a.shape, lambda g, n=len(a.shape): (0,) * n)

    def piece(grads):
        if len(grads.shape) == 2:
            return pl.BlockSpec((rows, width), lambda g: (seg, 0))
        return pl.BlockSpec((1, rows, width), lambda g: (0, seg, 0))

    outs = (
        shape((length, 3 * width), BF),
        shape((rows, depth), F32),
        shape((rows, depth), F32),
        shape((2 * rows, depth), BF),
        shape((8, 3 * width), F32),
    )
    return pl.pallas_call(
        lambda *refs: attend_back_kernel(heads, *refs),
        grid=(1,),
        out_shape=outs,
        in_specs=[fixed(a) for a in parts] + [piece(a) for a in grads_in] + [fixed(a) for a in (log_total, weight)]
        + [pl.BlockSpec((1,) + query_code.shape[1:], lambda g: (seg, 0, 0))],
        out_specs=[fixed(o) for o in outs],
        scratch_shapes=[
            pltpu.VMEM((length, length), F32),
            pltpu.VMEM((heads, length, HD), BF),
            pltpu.VMEM((width, length), F32),
            pltpu.VMEM((heads, length, HD), F32),
            pltpu.VMEM((heads, length, HD), F32),
            pltpu.VMEM((2, length, 256), F32),
            pltpu.VMEM((2, length, 256), F32),
        ],
        cost_estimate=pl.CostEstimate(
            flops=2 * length * depth * 3 * width + 40 * length * length * width,
            bytes_accessed=12 << 20,
            transcendentals=heads * length * length,
        ),
        name="attend_back",
    )(*parts, *grads_in, log_total, weight, query_code)


def qkv_grads(place, rows_t, grads, sums, shard):
    depth, length = rows_t[0].shape
    columns, segs = grads[0].shape[1], len(grads)
    part = depth // 2
    blocks = part // shard
    shape = jax.ShapeDtypeStruct

    def kernel(place_ref, *refs):
        x_refs, g_refs, s_refs = refs[:segs], refs[segs : 2 * segs], refs[2 * segs : 3 * segs]
        keep_o, send_o, made_ref = refs[3 * segs :]
        made = sum(mm(x[...], g[...]) for x, g in zip(x_refs, g_refs))
        for f in range(blocks):
            made_ref[f] = made[f * shard : (f + 1) * shard]
        below = sum(s[...] for s in s_refs)
        for rest in range(blocks // 2):
            for out, entry in ((keep_o, place_ref[1]), (send_o, 1 - place_ref[1])):
                out[rest, 0:shard] = made_ref[2 * rest + entry].astype(out.dtype)
                out[rest, shard:] = below.astype(out.dtype)

    whole = lambda a: pl.BlockSpec(a.shape, lambda g: (0, 0))
    out = pl.BlockSpec((blocks // 2, shard + 8, columns), lambda g: (g, 0, 0))
    return pl.pallas_call(
        kernel,
        grid=(2,),
        out_shape=tuple(shape((blocks, shard + 8, columns), kind) for kind in (F32, BF)),
        in_specs=[pl.BlockSpec(memory_space=pltpu.SMEM)]
        + [pl.BlockSpec((part, length), lambda g: (g, 0))] * segs
        + [whole(a) for a in (*grads, *sums)],
        out_specs=(out, out),
        scratch_shapes=[pltpu.VMEM((blocks, shard, columns), F32)],
        cost_estimate=pl.CostEstimate(
            flops=2 * segs * length * depth * columns, bytes_accessed=12 << 20, transcendentals=0
        ),
        name="qkv_grads",
    )(place, *rows_t, *grads, *sums)


def finish(seg, held, keep, near, far):
    rows, depth = keep.shape
    steps = 2
    part = rows // steps
    block = pl.BlockSpec((part, depth), lambda g: (seg * steps + g, 0))
    whole = pl.BlockSpec((part, depth), lambda g: (g, 0))

    def kernel(held_ref, keep_ref, near_ref, far_ref, out_ref):
        out_ref[...] = held_ref[...] + keep_ref[...] + near_ref[...].astype(F32) + far_ref[...].astype(F32)

    return pl.pallas_call(
        kernel,
        grid=(steps,),
        out_shape=jax.ShapeDtypeStruct(held.shape, F32),
        in_specs=[block, whole, whole, whole],
        out_specs=block,
        input_output_aliases={0: 0},
        cost_estimate=pl.CostEstimate(flops=1 << 20, bytes_accessed=4 << 20, transcendentals=0),
        name="finish",
    )(held, keep, near, far)


def fold(place, steps, groups, turned=False):
    shape = jax.ShapeDtypeStruct

    def lead_of(term):
        return term[1][1:-2] if term[3] else term[1][:-2]

    def spec(term):
        index = term[2]
        return pl.BlockSpec(term[1], lambda g, p: tuple(index(g, p)) + (0, 0))

    def sums_of(place_ref, ins, terms, number):
        pieces = {}

        def add(start, values):
            size = values.shape[0]
            inside = [k for k in pieces if start <= k[0] and sum(k) <= start + size]
            for k in inside:
                pieces[k] = pieces[k] + values[k[0] - start : sum(k) - start]
            if not inside:
                pieces[start, size] = values

        for ref, term in zip(ins, terms):
            rest, entry = number, []
            for n in reversed(lead_of(term)):
                entry.insert(0, rest % n)
                rest //= n
            if turned:
                entry[0] = place_ref[0] ^ number
            _, block, _, stacked, row = term
            if stacked:
                for i in range(block[0]):
                    add(row + i * block[-2], ref[(i, *entry)].astype(F32))
            else:
                add(row, ref[tuple(entry)].astype(F32))
        return pieces

    counts = [math.prod(lead_of(terms[0])) for terms, _ in groups]
    in_terms = [t for terms, _ in groups for t in terms]
    out_shape, out_specs = [], []
    for (terms, outs), count in zip(groups, counts):
        total = max(row + block[-2] * (block[0] if stacked else 1) for _, block, _, stacked, row in terms)
        columns = terms[0][0].shape[-1]
        if len(outs) == 1:
            out_shape.append(shape((steps * count, total, columns), outs[0]))
            out_specs.append(pl.BlockSpec((count, total, columns), lambda g, p: (g, 0, 0)))
        else:
            out_shape += [shape((total, columns), kind) for kind in outs]
            out_specs += [pl.BlockSpec((total, columns), lambda g, p: (0, 0))] * len(outs)

    def kernel(place_ref, *refs):
        refs = list(refs)
        out_refs = refs[len(in_terms) :]
        for (terms, outs), count in zip(groups, counts):
            ins, refs = refs[: len(terms)], refs[len(terms) :]
            own, out_refs = out_refs[: len(outs)], out_refs[len(outs) :]
            for number in range(count):
                out = own[0].at[number] if len(outs) == 1 else own[number]
                for (start, size), values in sums_of(place_ref, ins, terms, number).items():
                    out[start : start + size, :] = values.astype(out.dtype)

    return pl.pallas_call(
        kernel,
        grid_spec=pltpu.PrefetchScalarGridSpec(
            num_scalar_prefetch=1, grid=(steps,), in_specs=[spec(t) for t in in_terms], out_specs=out_specs
        ),
        out_shape=out_shape,
        cost_estimate=pl.CostEstimate(flops=1 << 20, bytes_accessed=4 << 20, transcendentals=0),
        name="fold",
    )(place, *[t[0] for t in in_terms])


def assemble(place, mine, other, far, far_other, shard, ratio):
    columns = mine.shape[1]
    depth, part = 2 * columns, shard // 2
    shape = jax.ShapeDtypeStruct

    def kernel(place_ref, mine_ref, other_ref, far_ref, far_other_ref, out_o, up_o, down_o, vec_o):
        chip, core = place_ref[0], place_ref[1]
        refs = (mine_ref, other_ref), (far_ref, far_other_ref)

        def picked(side, rows, at, size):
            near, away = ([ref[at : at + size, :] for ref in pair] for pair in refs)
            near, away = (jnp.where(chip == rows, a, b) for a, b in (near, away))
            return jnp.where(core == side, near, away).astype(F32)

        for side in range(2):
            for rows in range(2):
                at = slice(side * columns, (side + 1) * columns)
                own = slice(rows * part, (rows + 1) * part)
                for i in range(ratio):
                    start = side * ratio * columns + i * columns
                    up_o[own, start : start + columns] = picked(side, rows, i * part, part)
                out_o[own, at] = picked(side, rows, ratio * part, part)
                size = ratio * part
                down_o[rows * size : (rows + 1) * size, at] = picked(side, rows, (ratio + 1) * part, size)
        at = (2 * ratio + 1) * part
        vec_o[...] = jnp.where(chip == 0, mine_ref[at : at + 8, :], other_ref[at : at + 8, :]).astype(F32)

    vmem = pl.BlockSpec(memory_space=pltpu.VMEM)
    return pl.pallas_call(
        kernel,
        out_shape=(
            shape((shard, depth), F32),
            shape((shard, ratio * depth), F32),
            shape((ratio * shard, depth), F32),
            shape((8, columns), F32),
        ),
        in_specs=[pl.BlockSpec(memory_space=pltpu.SMEM)] + [vmem] * 4,
        out_specs=[vmem] * 4,
        cost_estimate=pl.CostEstimate(flops=1 << 20, bytes_accessed=4 << 20, transcendentals=0),
        name="assemble",
    )(place, mine, other, far, far_other)


def own_columns(values, group, width):
    return lax.dynamic_slice_in_dim(values, group * width, width, axis=1)


def per_device(
    layer_input, doc_starts, mem_rows, w_query, b_query, w_key, w_value, b_value, w_out, b_out,
    attn_gain, attn_shift, w_up, b_up, w_down, b_down, ffn_gain, ffn_shift, grad_out,
):
    segs, rows, depth = layer_input.shape
    groups = lax.axis_size(SEQ)
    width, half = depth // groups, depth // 2
    ff = w_up.shape[1]
    length = rows * groups
    here, place = lax.axis_index(SEQ), lax.axis_index(FSDP)
    upper_core, upper_chip = bit_of(here, CORE), bit_of(here, CHIP)
    core, chip = upper_core.astype(jnp.int32), upper_chip.astype(jnp.int32)
    shard = w_query.shape[0]
    devices = lax.axis_size(FSDP)
    ratio = ff // depth
    direct = shard % 32 == 0

    over_core = hop(layer_input, SEQ, CORE)
    first, later = (hop(part, SEQ, CHIP) for part in (layer_input[:1], layer_input[1:]))
    first_both, later_both = (hop(part, SEQ, CORE) for part in (first, later))

    def rows_of(i):
        chip_rows, both, at = (first, first_both, 0) if i == 0 else (later, later_both, i - 1)
        return ((layer_input, i), (over_core, i), (chip_rows, at), (both, at))

    vectors = (b_query, b_value, b_out, attn_gain, attn_shift, b_down, ffn_gain, ffn_shift, b_up)
    spot = jnp.stack([here, core, chip]).astype(jnp.int32)
    if direct:
        own, up_part, rest_part = pack(spot, (w_query, w_key, w_value, w_out, w_up, w_down), vectors)
        qkv_pieces = gather_pieces(own)
        order = jnp.arange(devices, dtype=jnp.int32) ^ place

        def two_parts(block):
            pieces = {0: block}
            for shift, n in reversed(fsdp_digits()[1:]):
                for held in list(pieces):
                    for step in range(1, n):
                        pieces[held | step << shift] = hop(pieces[held], FSDP, step << shift)
            near = jnp.stack([pieces[j] for j in sorted(pieces)])
            return near, hop(near, FSDP, 1)

        rest = two_parts(rest_part)
        rest_far = [hop(part, SEQ, CHIP) for part in rest]
        quarter_ff = ff // 4
        up = two_parts(up_part[:, :quarter_ff]) + two_parts(up_part[:, quarter_ff:])
        middle_weights = (
            *up, *[hop(part, SEQ, CORE) for part in up],
            *rest, *rest_far,
            *[hop(part, SEQ, CORE) for part in rest],
            *[hop(part, SEQ, CORE) for part in rest_far],
        )
        up_bias = jnp.zeros((1, ff), F32)
        qkv_bias = jnp.zeros((1, 3 * width), F32)
    else:
        own = jnp.concatenate([own_columns(w, here, width) for w in (w_query, w_key, w_value)], axis=1)
        qkv_pieces = [lax.all_gather(own, FSDP, axis=0, tiled=True)]
        found = lax.all_gather(jnp.concatenate(vectors), FSDP, axis=0).astype(F32)
        order = jnp.zeros((1,), jnp.int32)
        out_whole, up_whole, down_whole = (
            lax.all_gather(w, FSDP, axis=0, tiled=True) for w in (w_out, w_up, w_down)
        )
        up_halves, down_halves = up_whole.reshape(depth, 2, ff // 2), down_whole.reshape(2, ff // 2, depth)
        middle_weights = (
            out_whole,
            jnp.where(upper_core, up_halves[:, ::-1], up_halves).reshape(depth, ff),
            jnp.where(upper_core, down_halves[::-1], down_halves).reshape(ff, depth),
        )
        names = len(vectors) - 1
        q_bias, v_bias, o_bias, gain_one, shift_one, down_bias, gain_two, shift_two = (
            found[:, i * shard : (i + 1) * shard].reshape(-1) for i in range(names)
        )
        up_bias = found[:, names * shard :].reshape(2, ff // 2)
        up_bias = jnp.where(upper_core, up_bias[::-1], up_bias).reshape(1, ff)
        vector_rows = jnp.stack([o_bias, gain_one, shift_one, down_bias, gain_two, shift_two, o_bias, o_bias])
        qkv_bias = jnp.concatenate(
            [
                lax.dynamic_slice_in_dim(q_bias, here * width, width),
                jnp.zeros((width,), F32),
                lax.dynamic_slice_in_dim(v_bias, here * width, width),
            ]
        )[None, :]
    piece_rows = shard if direct else devices * shard
    order = jnp.concatenate([order, spot])

    spots = jnp.arange(length, dtype=jnp.int32)
    positions = ((spots // rows) ^ here) * rows + spots % rows
    doc_ids = jnp.sum((doc_starts[:, :, None] <= positions[None, None, :]).astype(F32), axis=1)
    is_memory = jnp.any(mem_rows[:, :, None] == positions[None, None, :], axis=1)
    penalty = jnp.where(is_memory, 0.0, MASKED)
    query_code = jnp.stack([doc_ids, penalty] + [jnp.zeros_like(doc_ids)] * 6, axis=1)

    done = []
    for i in range(segs):
        done.append(attend(i, order, rows_of(i), qkv_pieces, piece_rows, qkv_bias, query_code))

    contexts = []
    for i in range(segs):
        near, to_core, to_chip = done[i][6:9]
        from_core = hop(to_core, SEQ, CORE)
        from_chip = hop(to_chip, SEQ, CHIP)
        contexts.append((near, from_core, from_chip, hop(from_chip[rows:], SEQ, CORE)))

    (
        layer_out, context_t, low_t, active_t, gb, gh, ga, grad_sum_one, g0, g1, g2, g3, vector_sums,
    ) = middle(
        order, middle_weights, shard, direct, contexts, layer_input.reshape(segs * rows, depth),
        grad_out.reshape(segs * rows, depth), done[0][10] if direct else vector_rows, up_bias,
    )
    heads_grads = (g0, hop(g1, SEQ, CORE), hop(g2, SEQ, CHIP), hop(hop(g3, SEQ, CORE), SEQ, CHIP))

    digits = fsdp_digits()
    place_digits = [(FSDP, shift, n, place) for shift, n in digits]

    second_keep, second_send = second_grads(active_t, gb)
    second_got = hop(second_send, SEQ, CORE)
    first_keep, first_send = first_grads(context_t, low_t, ga, gh)
    first_got = hop(first_send, SEQ, CORE)
    vector_sums = vector_sums + hop(vector_sums, SEQ, CORE)

    rest_count = devices // 2
    part_rows = shard // 2
    at_place = jnp.stack([place >> 1, place & 1, chip]).astype(jnp.int32)

    def by_block(values, size):
        return values.reshape(values.shape[:-2] + (rest_count, 2, 2, size, half))

    first = [by_block(v, part_rows) for v in (first_keep, first_got)]
    second = [by_block(v, part_rows * ratio) for v in (second_keep, second_got)]
    vector_blocks = by_block(vector_sums.reshape(-1, half), 8)
    below_first = (ratio + 1) * part_rows
    chunk = max(rest_count // 2, 1)

    def first_terms(size, block, index):
        return [
            (v, (ratio + 1, size) + block + (part_rows, half), lambda g, p: (0, g) + index(p), True, 0) for v in first
        ]

    def second_terms(size, block, index, row=0):
        at = lambda g, p: (g,) + index(p)
        terms = [(v, (size,) + block + (part_rows * ratio, half), at, False, row) for v in second]
        return terms + [(vector_blocks, (size,) + block + (8, half), at, False, row + part_rows * ratio)]

    def got_terms(got, many, index, row=0):
        if not many:
            return [(got, (rest_count,) + got.shape[1:], lambda g, p: (0,), False, row)]
        got = got.reshape((rest_count, 2) + got.shape[1:])
        return [(got, (rest_count, 1) + got.shape[2:], lambda g, p: (0, index(p)), False, row)]

    one, many = (BF,), rest_count // chunk
    send_b = fold(at_place, many, [(second_terms(chunk, (2, 1), lambda p: (0, 1 - p[2])), one)])[0]
    got_b0 = hop(send_b, SEQ, CHIP)
    send_a = fold(at_place, many, [(first_terms(chunk, (1, 2), lambda p: (1 - p[1], 0)), one)])[0]
    got_a0 = hop(send_a, FSDP, 1)
    send_b, send_a = fold(
        at_place,
        1,
        [
            (second_terms(rest_count, (1, 1), lambda p: (1 - p[1], p[2]))
             + got_terms(got_b0, True, lambda p: 1 - p[1]), one),
            (first_terms(rest_count, (1, 1), lambda p: (p[1], 1 - p[2]))
             + got_terms(got_a0, True, lambda p: 1 - p[2]), one),
        ],
    )
    got_b1 = hop(send_b, FSDP, 1)
    got_a1 = hop(send_a, SEQ, CHIP)

    backs = []
    for i in range(segs):
        backs.append(
            attend_back(i, rows, done[i][:4], heads_grads, done[i][9], done[0][5], query_code)
        )

    last_terms = (
        first_terms(rest_count, (1, 1), lambda p: (p[1], p[2]))
        + got_terms(got_a0, True, lambda p: p[2]) + got_terms(got_a1, False, None)
        + second_terms(rest_count, (1, 1), lambda p: (p[1], p[2]), below_first)
        + got_terms(got_b0, True, lambda p: p[1], below_first) + got_terms(got_b1, False, None, below_first)
    )
    if len(digits) == 2:
        shift, n = digits[1]
        kinds = (F32,) + (BF,) * (n - 1)
        mine, *sends = fold(at_place, 1, [(last_terms, kinds)], turned=True)
        for k, send in enumerate(sends, 1):
            mine = mine + hop(send, FSDP, k << shift).astype(F32)
    else:
        merged = fold(at_place, 1, [(last_terms, (F32,))])[0]
        lead = tuple(n for _, n in reversed(digits[1:]))
        mine = halve(merged.reshape(lead + merged.shape[1:]), place_digits[1:])
    mine = mine.astype(BF)
    other = hop(mine, SEQ, CHIP)
    far = [hop(part, SEQ, CORE) for part in (mine, other)]
    grad_w_out, grad_w_up, grad_w_down, vector_rows = assemble(
        jnp.stack([chip, core]), mine, other, *far, shard, ratio
    )
    per = half // shard

    def vector_of(i):
        return vector_rows[i // per, i % per * shard : (i % per + 1) * shard]

    grad_input = grad_sum_one
    for i in range(segs):
        _, keep_near, keep_chip, send, _ = backs[i]
        near = hop(send, SEQ, CORE)
        far = (keep_chip + near[rows:].astype(F32)).astype(BF)
        grad_input = finish(i, grad_input, keep_near, near, hop(far, SEQ, CHIP))

    keep, send = qkv_grads(
        at_place, [d[4] for d in done], [b[0] for b in backs], [b[4] for b in backs], shard
    )
    lead = tuple(n for _, n in reversed(digits[1:])) + keep.shape[1:]
    mine = halve(keep.reshape(lead), place_digits[1:], [hop(send, FSDP, 1).reshape(lead)]).astype(BF)
    other = hop(mine, SEQ, CORE)
    far_mine = hop(mine, SEQ, CHIP)
    far_other = hop(other, SEQ, CHIP)
    parts = swapped([mine, other, far_mine, far_other], upper_core, upper_chip)

    def columns_of(i):
        return jnp.concatenate([p[:, i * width : (i + 1) * width] for p in parts], axis=1).astype(F32)

    def own_part(vector):
        count = vector.shape[0] * shard // depth
        return lax.dynamic_slice_in_dim(vector, place * count, count)

    grad_q, grad_k, grad_v = (columns_of(i) for i in range(3))
    return (
        layer_out.reshape(layer_input.shape),
        grad_input.reshape(layer_input.shape),
        grad_q[:shard],
        own_part(grad_q[shard]),
        grad_k[:shard],
        grad_v[:shard],
        own_part(grad_v[shard]),
        grad_w_out,
        vector_of(0),
        vector_of(1),
        vector_of(2),
        grad_w_up,
        jnp.concatenate([vector_of(6 + r) for r in range(ratio)]),
        grad_w_down,
        vector_of(3),
        vector_of(4),
        vector_of(5),
    )


def solution(mesh):
    rows, cols = P(FSDP, SEQ, None), P(FSDP, None)
    vec = P(FSDP)
    return jax.shard_map(
        per_device,
        mesh=mesh,
        in_specs=(
            rows, cols, cols, cols, vec, cols, cols, vec, cols, vec,
            vec, vec, cols, vec, cols, vec, vec, vec, rows,
        ),
        out_specs=(
            rows, rows, cols, vec, cols, cols, vec, cols, vec,
            vec, vec, cols, vec, cols, vec, vec, vec,
        ),
        check_vma=False,
    )
```
